32 devices in a mesh: batch: 8 (over z, x), seq: 4 (over y, core).
Axes of the slice: x: 2, y: 2, z: 4, core: 2. Of those that a mesh axis runs over, the one named last changes fastest.
Arguments:
- target: bfloat16 [8, 512, 1024], P('batch', 'seq'), may hold values from -6 to 6
- memory: bfloat16 [8, 256, 1024], P('batch', 'seq'), may hold values from -6 to 6
- cotangent: bfloat16 [8, 512, 1024], P('batch', 'seq'), may hold values from -6 to 6
- target_segments: int32 [8, 512], P('batch'), may hold values from 0 to 3, never falling along the last dimension, each value on 1 to 256 neighbouring positions
- memory_segments: int32 [8, 256], P('batch'), may hold values from 0 to 3, never falling along the last dimension, each value on 1 to 128 neighbouring positions
- bucket_ids: int32 [512], replicated, may hold values from 0 to 31
- self_norm_gain: bfloat16 [1024], P(('batch', 'seq')), may hold values from 0.099609375 to 1.8984375
- self_query: bfloat16 [1024, 1024], P(('batch', 'seq')), may hold values from -0.09375 to 0.09375
- self_key: bfloat16 [1024, 1024], P(('batch', 'seq')), may hold values from -0.09375 to 0.09375
- self_value: bfloat16 [1024, 1024], P(('batch', 'seq')), may hold values from -0.1875 to 0.1875
- self_output: bfloat16 [1024, 1024], P(('batch', 'seq')), may hold values from -0.75 to 0.75
- bias_table: bfloat16 [32, 16], P('batch', 'seq'), may hold values from -4 to 4
- cross_norm_gain: bfloat16 [1024], P(('batch', 'seq')), may hold values from 0.099609375 to 1.8984375
- cross_query: bfloat16 [1024, 1024], P(('batch', 'seq')), may hold values from -0.09375 to 0.09375
- cross_key: bfloat16 [1024, 1024], P(('batch', 'seq')), may hold values from -0.09375 to 0.09375
- cross_value: bfloat16 [1024, 1024], P(('batch', 'seq')), may hold values from -0.1875 to 0.1875
- cross_output: bfloat16 [1024, 1024], P(('batch', 'seq')), may hold values from -0.75 to 0.75
- ffn_norm_gain: bfloat16 [1024], P(('batch', 'seq')), may hold values from 0.099609375 to 1.8984375
- ffn_gate: bfloat16 [1024, 2816], P(('batch', 'seq')), may hold values from -0.1875 to 0.1875
- ffn_up: bfloat16 [1024, 2816], P(('batch', 'seq')), may hold values from -0.1875 to 0.1875
- ffn_down: bfloat16 [2816, 1024], P(('batch', 'seq')), may hold values from -0.109375 to 0.109375
Outputs:
- activations: bfloat16 [8, 512, 1024], P('batch', 'seq')
- target_grad: float32 [8, 512, 1024], P('batch', 'seq')
- memory_grad: float32 [8, 256, 1024], P('batch', 'seq')
- self_norm_gain_grad: float32 [1024], P(('batch', 'seq'))
- self_query_grad: float32 [1024, 1024], P(('batch', 'seq'))
- self_key_grad: float32 [1024, 1024], P(('batch', 'seq'))
- self_value_grad: float32 [1024, 1024], P(('batch', 'seq'))
- self_output_grad: float32 [1024, 1024], P(('batch', 'seq'))
- bias_table_grad: float32 [32, 16], P('batch', 'seq')
- cross_norm_gain_grad: float32 [1024], P(('batch', 'seq'))
- cross_query_grad: float32 [1024, 1024], P(('batch', 'seq'))
- cross_key_grad: float32 [1024, 1024], P(('batch', 'seq'))
- cross_value_grad: float32 [1024, 1024], P(('batch', 'seq'))
- cross_output_grad: float32 [1024, 1024], P(('batch', 'seq'))
- ffn_norm_gain_grad: float32 [1024], P(('batch', 'seq'))
- ffn_gate_grad: float32 [1024, 2816], P(('batch', 'seq'))
- ffn_up_grad: float32 [1024, 2816], P(('batch', 'seq'))
- ffn_down_grad: float32 [2816, 1024], P(('batch', 'seq'))
The draws below stay inside these ranges and needn't reach their ends.
Inputs may be any that keep to these rules, and one draw needn't show every extreme that they name: `target_segments`: in each target sequence the ids never fall, every id 0 to 3 occurs, and the longest document has 256 tokens. `memory_segments`: in each sequence the ids never fall and every id 0 to 3 occurs, so every target document has encoder rows of its own id; the longest has 128 rows. `bucket_ids`: entry d is the bucket of a key d positions before its query.
All inputs are finite; a program needn't handle non-finite values.
Results may differ from the reference program's by a relative error of at most 0.02.
The reference program's roundings to bfloat16 on the way count: a program that leaves them out, or rounds other values in their place, can miss the bound.
Values may be sent and summed in bfloat16 or wider, within the bound.
No kernel may reach another device: no remote copies, remote signals or barrier semaphores. Data moves between devices by JAX's collectives and lax.ppermute only.
A program may use at most 256 MiB of HBM per device.

```python
import math
from functools import partial
import jax
import jax.numpy as jnp
import numpy as np
from jax import lax

D = 1024
HEADS = 16
HD = 64
FF = 2816
BUCKETS = 32
INNER = 1024
LEN = 512
ENC = 256
DOCS = 4
SEQS = 8


def with_ends(array, key, smallest, high):
    longest = array.shape.index(max(array.shape))
    spots = []
    for shift in (0, 1):
        where = [jax.random.randint(jax.random.fold_in(key, axis), (), 0, length) for axis, length in enumerate(array.shape)]
        where[longest] = (where[longest] + shift) % array.shape[longest]
        spots.append(tuple(where))
    return array.at[spots[0]].set(smallest).at[spots[1]].set(high)


def level_of(key, extent, split, smallest, top_value):
    level, own = 1.0, jax.random.fold_in(key, 6)
    for position, shards_of in split:
        heights = jnp.exp(jax.random.uniform(jax.random.fold_in(own, position), (shards_of,), jnp.float32, smallest / len(split), top_value / len(split)))
        level = level * jnp.repeat(heights, extent[position] // shards_of).reshape([-1 if axis == position else 1 for axis in range(len(extent))])
    return level


def split_up(amount, total, reach, lean):
    weights = [(1 << 20) // math.isqrt(standing ** lean) + 1 for standing in range(2, amount + 1)]
    rest, counts = total - reach - (amount - 1), [1] * (amount - 1)
    while rest > 0:
        movable = [i for i in range(amount - 1) if counts[i] < reach]
        mass, left = sum([weights[i] for i in movable]), rest
        for i in movable:
            extra = min(reach - counts[i], max(1, left * weights[i] // mass), rest)
            counts[i] = counts[i] + extra
            rest = rest - extra
    return np.array([reach] + counts)


def uneven_parts(rng, amount, total, limit, slope):
    if amount == 2:
        one = jax.random.randint(rng, (), max(1, total - limit), min(limit, total - 1) + 1)
        return jnp.stack([one, total - one])
    tallies = jnp.asarray(split_up(amount, total, limit, slope), jnp.int32)
    couples = (amount - 1) // 2
    donor, receiver = tallies[1:1 + 2 * couples:2], tallies[2:2 + 2 * couples:2]
    room = jnp.minimum(donor - 1, limit - receiver)
    shifted = jax.random.randint(jax.random.fold_in(rng, 1), (couples,), 0, 1 << 20) % (room + 1)
    tallies = tallies.at[1:1 + 2 * couples:2].set(donor - shifted).at[2:2 + 2 * couples:2].set(receiver + shifted)
    return tallies[jax.random.permutation(jax.random.fold_in(rng, 2), amount)]


def centred(own_key, dims, scale, limit, cuts=(), kind=jnp.bfloat16):
    entries = scale * jax.random.normal(own_key, dims, jnp.float32)
    if cuts:
        entries = entries * level_of(own_key, dims, cuts, -0.22, 0.18)
    return jnp.clip(entries, -limit, limit).astype(kind)


def setup_inputs(seed: int = 0) -> dict:
    arg_keys = jax.random.split(jax.random.key(seed), 22)
    target = centred(arg_keys[0], (SEQS, LEN, D), 1.0, 6.0, ((0, 8), (1, 4)))
    memory = centred(arg_keys[1], (SEQS, ENC, D), 1.0, 6.0, ((0, 8), (1, 4)))
    cotangent = centred(arg_keys[2], (SEQS, LEN, D), 1.0, 6.0, ((0, 8), (1, 4)))
    target_segments = jax.vmap(lambda own: jnp.searchsorted(jnp.cumsum(uneven_parts(own, DOCS, LEN, LEN // 2, 1)), jnp.arange(LEN), side="right"))(jax.random.split(arg_keys[3], SEQS)).reshape((SEQS, LEN)).astype(jnp.int32)
    memory_segments = jax.vmap(lambda own: jnp.searchsorted(jnp.cumsum(uneven_parts(own, DOCS, ENC, ENC // 2, 1)), jnp.arange(ENC), side="right"))(jax.random.split(arg_keys[4], SEQS)).reshape((SEQS, ENC)).astype(jnp.int32)
    bucket_ids = with_ends(jax.random.randint(arg_keys[5], (LEN,), 0, BUCKETS), jax.random.fold_in(arg_keys[5], 1), 0, BUCKETS - 1).astype(jnp.int32)
    self_norm_gain = jnp.clip(1.0 + 0.18 * jax.random.normal(arg_keys[6], (D,), jnp.float32), 0.099609375, 1.8984375).astype(jnp.bfloat16)
    self_query = centred(arg_keys[7], (D, INNER), (4 * D) ** -0.5, 0.09375, ((0, 32),))
    self_key = centred(arg_keys[8], (D, INNER), (4 * D) ** -0.5, 0.09375, ((0, 32),))
    self_value = centred(arg_keys[9], (D, INNER), D ** -0.5, 0.1875, ((0, 32),))
    self_output = centred(arg_keys[10], (INNER, D), (INNER // 16) ** -0.5, 0.75, ((0, 32),))
    bias_table = centred(arg_keys[11], (BUCKETS, HEADS), 1.0, 4.0, ((0, 8), (1, 4)))
    cross_norm_gain = jnp.clip(1.0 + 0.18 * jax.random.normal(arg_keys[12], (D,), jnp.float32), 0.099609375, 1.8984375).astype(jnp.bfloat16)
    cross_query = centred(arg_keys[13], (D, INNER), (4 * D) ** -0.5, 0.09375, ((0, 32),))
    cross_key = centred(arg_keys[14], (D, INNER), (4 * D) ** -0.5, 0.09375, ((0, 32),))
    cross_value = centred(arg_keys[15], (D, INNER), D ** -0.5, 0.1875, ((0, 32),))
    cross_output = centred(arg_keys[16], (INNER, D), (INNER // 16) ** -0.5, 0.75, ((0, 32),))
    ffn_norm_gain = jnp.clip(1.0 + 0.18 * jax.random.normal(arg_keys[17], (D,), jnp.float32), 0.099609375, 1.8984375).astype(jnp.bfloat16)
    ffn_gate = centred(arg_keys[18], (D, FF), D ** -0.5, 0.1875, ((0, 32),))
    ffn_up = centred(arg_keys[19], (D, FF), D ** -0.5, 0.1875, ((0, 32),))
    ffn_down = centred(arg_keys[20], (FF, D), FF ** -0.5, 0.109375, ((0, 32),))
    return dict(target=target, memory=memory, cotangent=cotangent, target_segments=target_segments, memory_segments=memory_segments, bucket_ids=bucket_ids, self_norm_gain=self_norm_gain, self_query=self_query, self_key=self_key, self_value=self_value, self_output=self_output, bias_table=bias_table, cross_norm_gain=cross_norm_gain, cross_query=cross_query, cross_key=cross_key, cross_value=cross_value, cross_output=cross_output, ffn_norm_gain=ffn_norm_gain, ffn_gate=ffn_gate, ffn_up=ffn_up, ffn_down=ffn_down)


EPSILON = 1e-06
MASKED = -1e+30
HIGHEST = lax.Precision.HIGHEST

@jax.custom_vjp
def low(v):
    return lax.optimization_barrier(v.astype(jnp.bfloat16)).astype(jnp.float32)

@jax.custom_vjp
def low_back(v):
    return v

def low_keep(v):
    return (low(v), None)

def low_pass(kept, grad):
    return (grad,)

def back_keep(v):
    return (v, None)

def back_low(kept, grad):
    return (low(grad),)
low.defvjp(low_keep, low_pass)
low_back.defvjp(back_keep, back_low)

def norm_gain(values, gain):
    return values * lax.rsqrt(lax.optimization_barrier(jnp.mean(values * values, axis=-1, keepdims=True)) + EPSILON) * gain

def project(acts, weight):
    return jnp.einsum('...d,de->...e', acts, weight, precision=HIGHEST)

def attend_one(operands, bias_full):
    queries, key_heads, value_heads, allowed = operands
    scores = low_back(jnp.einsum('qhd,khd->hqk', queries, key_heads, precision=HIGHEST)) + bias_full
    scores = jnp.where(allowed[None], scores, MASKED)
    log_total = jax.nn.logsumexp(scores, axis=-1, keepdims=True)
    weights = low(jnp.exp(scores - log_total))
    attended = jnp.einsum('hqk,khd->qhd', weights, value_heads, precision=HIGHEST)
    return attended.reshape(attended.shape[0], -1)

def split_heads(tensor):
    return tensor.reshape(tensor.shape[0], tensor.shape[1], HEADS, HD)

def layer(params, target, memory, target_segments, memory_segments, bucket_ids):
    self_norm_gain, self_query, self_key, self_value, self_output, bias_table, cross_norm_gain, cross_query, cross_key, cross_value, cross_output, ffn_norm_gain, ffn_gate, ffn_up, ffn_down = params
    length = target.shape[1]
    normed_one = low(norm_gain(target, self_norm_gain))
    queries = split_heads(low(low_back(project(normed_one, self_query))))
    key_heads = split_heads(low(low_back(project(normed_one, self_key))))
    value_heads = split_heads(low(low_back(project(normed_one, self_value))))
    positions = jnp.arange(length, dtype=jnp.int32)
    offsets = positions[:, None] - positions[None, :]
    causal = offsets >= 0
    buckets = bucket_ids[jnp.clip(offsets, 0, length - 1)]
    bias_full = jnp.take(bias_table.T, buckets, axis=1)
    self_allowed = causal[None] & (target_segments[:, :, None] == target_segments[:, None, :])
    attended = lax.map(jax.checkpoint(partial(attend_one, bias_full=bias_full)), (queries, key_heads, value_heads, self_allowed))
    attended = low(low_back(attended))
    hidden_one = target + low_back(project(attended, self_output))
    normed_two = low(norm_gain(hidden_one, cross_norm_gain))
    cross_queries = split_heads(low(low_back(project(normed_two, cross_query))))
    cross_keys = split_heads(low(low_back(project(memory, cross_key))))
    cross_values = split_heads(low(low_back(project(memory, cross_value))))
    cross_allowed = target_segments[:, :, None] == memory_segments[:, None, :]
    cross_attended = lax.map(jax.checkpoint(partial(attend_one, bias_full=0.0)), (cross_queries, cross_keys, cross_values, cross_allowed))
    cross_attended = low(low_back(cross_attended))
    hidden_two = hidden_one + low_back(project(cross_attended, cross_output))
    normed_three = low(norm_gain(hidden_two, ffn_norm_gain))
    gate_act = low_back(project(normed_three, ffn_gate))
    up_act = low_back(project(normed_three, ffn_up))
    inner_act = low(jax.nn.gelu(gate_act, approximate=True) * up_act)
    return hidden_two + low_back(project(inner_act, ffn_down))

def reference(target, memory, cotangent, target_segments, memory_segments, bucket_ids, self_norm_gain, self_query, self_key, self_value, self_output, bias_table, cross_norm_gain, cross_query, cross_key, cross_value, cross_output, ffn_norm_gain, ffn_gate, ffn_up, ffn_down):
    params = tuple((weight.astype(jnp.float32) for weight in (self_norm_gain, self_query, self_key, self_value, self_output, bias_table, cross_norm_gain, cross_query, cross_key, cross_value, cross_output, ffn_norm_gain, ffn_gate, ffn_up, ffn_down)))
    per_group = 4
    group_count = target.shape[0] // per_group

    def grouped(tensor):
        return tensor.reshape((group_count, per_group) + tensor.shape[1:])

    def group_step(totals, pieces):
        target_group, memory_group, cot_group, tseg_group, mseg_group = pieces

        def forward(params_in, target_in, memory_in):
            return layer(params_in, target_in, memory_in, tseg_group, mseg_group, bucket_ids)
        result, pullback = jax.vjp(forward, params, target_group.astype(jnp.float32), memory_group.astype(jnp.float32))
        grad_params, grad_target, grad_memory = pullback(cot_group.astype(jnp.float32))
        totals = jax.tree.map(jnp.add, totals, grad_params)
        return (totals, (result.astype(jnp.bfloat16), grad_target, grad_memory))
    zero_grads = jax.tree.map(jnp.zeros_like, params)
    totals, (results, grad_targets, grad_memories) = lax.scan(group_step, zero_grads, (grouped(target), grouped(memory), grouped(cotangent), grouped(target_segments), grouped(memory_segments)))
    return (results.reshape(target.shape), grad_targets.reshape(target.shape), grad_memories.reshape(memory.shape), totals[0], totals[1], totals[2], totals[3], totals[4], totals[5], totals[6], totals[7], totals[8], totals[9], totals[10], totals[11], totals[12], totals[13], totals[14])
```

```python
import functools

import jax
import jax.numpy as jnp
from jax import lax
from jax.experimental import pallas as pl
from jax.experimental.pallas import tpu as pltpu
from jax.sharding import PartitionSpec as P

HD = 64
LANES = 128
SUBLANES = 8
EPSILON = 1e-06
MASKED = -1e30
BF = jnp.bfloat16
F32 = jnp.float32
AXES = ("batch", "seq")
NT = (((1,), (1,)), ((), ()))
TN = (((0,), (0,)), ((), ()))
NN = (((1,), (0,)), ((), ()))


def mm(left, right, dims=NN):
    return lax.dot_general(left, right, dims, preferred_element_type=F32)


def norm_gain(values, gain):
    return values * lax.rsqrt(jnp.mean(values * values, axis=-1, keepdims=True) + EPSILON) * gain


def norm_back(values, gain, grad_out):
    _, pullback = jax.vjp(norm_gain, values, gain)
    return pullback(grad_out)


def gated_unit(gate_act, up_act):
    return jax.nn.gelu(gate_act, approximate=True) * up_act


def head_only(pair, head):
    lane = lax.broadcasted_iota(jnp.int32, pair.shape, 1)
    return jnp.where((lane // HD) == head, pair, jnp.zeros_like(pair))


def pick_heads(first, second):
    lane = lax.broadcasted_iota(jnp.int32, first.shape, 1)
    return jnp.where(lane < HD, first, second)


def spread(window, rows):
    wide = jnp.broadcast_to(window, (rows, window.shape[1]))
    rolled = pltpu.roll(wide, 0, 1, stride=1, stride_axis=0)
    return rolled[:, rows:]


def unspread(grads, rows):
    wide = jnp.concatenate([jnp.zeros((rows, rows), F32), grads], axis=1)
    width = wide.shape[1]
    total = wide[:SUBLANES]
    for start in range(SUBLANES, rows, SUBLANES):
        total = total + pltpu.roll(wide[start : start + SUBLANES], width - start, 1)
    row = lax.broadcasted_iota(jnp.int32, total.shape, 0)
    for bit in (1, 2, 4):
        total = jnp.where((row & bit) != 0, pltpu.roll(total, width - bit, 1), total)
    return jnp.sum(total, axis=0, keepdims=True)


def allowed_pairs(position, query_segments, key_segments, causal):
    rows, keys = query_segments.shape[0], key_segments.shape[1]
    allowed = query_segments == key_segments
    if causal:
        own = lax.broadcasted_iota(jnp.int32, (rows, keys), 0) + position
        other = lax.broadcasted_iota(jnp.int32, (rows, keys), 1)
        allowed = allowed & (own >= other)
    return allowed


def pair_probs(query, key, bias_ref, allowed, head, causal):
    scores = mm(head_only(query, head), key, NT)
    if causal:
        scores = scores + spread(bias_ref[0, head : head + 1, :], query.shape[0])
    scores = jnp.where(allowed, scores, MASKED)
    top = jnp.max(scores, axis=1, keepdims=True)
    grown = jnp.exp(scores - top)
    return grown / jnp.sum(grown, axis=1, keepdims=True)


def attend_body(causal, pos_ref, q_ref, k_ref, v_ref, bias_ref, qseg_ref, kseg_ref, out_ref):
    query, key, value = q_ref[...], k_ref[...], v_ref[...]
    allowed = allowed_pairs(pos_ref[0], qseg_ref[...], kseg_ref[...], causal)
    parts = []
    for head in range(2):
        probs = pair_probs(query, key, bias_ref, allowed, head, causal)
        parts.append(mm(probs.astype(BF), value))
    out_ref[...] = pick_heads(*parts).astype(BF)


def attend_back_body(
    causal, pos_ref, q_ref, k_ref, v_ref, do_ref, bias_ref, qseg_ref, kseg_ref,
    dq_ref, dk_ref, dv_ref, dbias_ref,
):
    query, key, value, grad = q_ref[...], k_ref[...], v_ref[...], do_ref[...]
    allowed = allowed_pairs(pos_ref[0], qseg_ref[...], kseg_ref[...], causal)
    grad_query, grad_key, grad_value = [], 0.0, 0.0
    for head in range(2):
        probs = pair_probs(query, key, bias_ref, allowed, head, causal)
        grad_head = head_only(grad, head)
        grad_probs = mm(grad_head, value, NT)
        inner = jnp.sum(probs * grad_probs, axis=1, keepdims=True)
        grad_scores = probs * (grad_probs - inner)
        low_scores = grad_scores.astype(BF)
        grad_query.append(mm(low_scores, key))
        grad_key = grad_key + mm(low_scores, head_only(query, head), TN)
        grad_value = grad_value + mm(probs.astype(BF), grad_head, TN)
        if causal:
            dbias_ref[0, head : head + 1, :] = unspread(grad_scores, query.shape[0])
    if not causal:
        dbias_ref[...] = jnp.zeros_like(dbias_ref)
    dq_ref[...] = pick_heads(*grad_query).astype(BF)
    dk_ref[...] = grad_key.astype(BF)
    dv_ref[...] = grad_value.astype(BF)


def attention_specs(rows, keys, width):
    pair = lambda count: pl.BlockSpec((count, LANES), lambda step: (0, step))
    whole = lambda shape: pl.BlockSpec(shape, lambda step: (0, 0))
    smem = pl.BlockSpec(memory_space=pltpu.SMEM)
    bias = pl.BlockSpec((1, 2, width), lambda step: (step, 0, 0))
    return pair, bias, smem, [whole((rows, 1)), whole((1, keys))]


PARAMS = pltpu.CompilerParams(dimension_semantics=("arbitrary",), vmem_limit_bytes=48 << 20)


def attend(position, query, key, value, windows, qseg, kseg, causal):
    rows, inner = query.shape
    keys = key.shape[0]
    pair, bias, smem, segs = attention_specs(rows, keys, windows.shape[2])
    return pl.pallas_call(
        functools.partial(attend_body, causal),
        grid=(inner // LANES,),
        in_specs=[smem, pair(rows), pair(keys), pair(keys), bias] + segs,
        out_specs=pair(rows),
        out_shape=jax.ShapeDtypeStruct((rows, inner), BF),
        compiler_params=PARAMS,
        name="attend_self" if causal else "attend_cross",
    )(position, query, key, value, windows, qseg, kseg)


def attend_back(position, query, key, value, grad, windows, qseg, kseg, causal):
    rows, inner = query.shape
    keys = key.shape[0]
    pair, bias, smem, segs = attention_specs(rows, keys, windows.shape[2])
    return pl.pallas_call(
        functools.partial(attend_back_body, causal),
        grid=(inner // LANES,),
        in_specs=[smem, pair(rows), pair(keys), pair(keys), pair(rows), bias] + segs,
        out_specs=[pair(rows), pair(keys), pair(keys), bias],
        out_shape=[
            jax.ShapeDtypeStruct((rows, inner), BF),
            jax.ShapeDtypeStruct((keys, inner), BF),
            jax.ShapeDtypeStruct((keys, inner), BF),
            jax.ShapeDtypeStruct(windows.shape, F32),
        ],
        compiler_params=PARAMS,
        name="attend_self_back" if causal else "attend_cross_back",
    )(position, query, key, value, grad, windows, qseg, kseg)


def seq_perm(size, step):
    return [(i, (i + step) % size) for i in range(size)]


def seq_gather(rows):
    size, own = lax.axis_size("seq"), lax.axis_index("seq")
    full = jnp.zeros((size,) + rows.shape, rows.dtype)
    full = lax.dynamic_update_slice_in_dim(full, rows[None], own, 0)
    for step in range(1, size):
        piece = lax.ppermute(rows, "seq", seq_perm(size, step))
        full = lax.dynamic_update_slice_in_dim(full, piece[None], (own - step) % size, 0)
    return full


def seq_scatter(parts):
    size, own = lax.axis_size("seq"), lax.axis_index("seq")
    total = lax.dynamic_index_in_dim(parts, own, 0, False)
    low = parts.astype(BF)
    for step in range(1, size):
        piece = lax.dynamic_index_in_dim(low, (own + step) % size, 0, False)
        total = total + lax.ppermute(piece, "seq", seq_perm(size, step)).astype(F32)
    return total


def gather_all(shard):
    return lax.all_gather(shard, AXES, axis=0, tiled=True)


def scatter_all(grads):
    return lax.psum_scatter(grads, AXES, scatter_dimension=0, tiled=True).astype(F32)


def per_device(
    target, memory, cotangent, target_segments, memory_segments, bucket_ids,
    self_norm_gain, self_query, self_key, self_value, self_output, bias_table,
    cross_norm_gain, cross_query, cross_key, cross_value, cross_output,
    ffn_norm_gain, ffn_gate, ffn_up, ffn_down,
):
    batch_size, seq_size = lax.axis_size("batch"), lax.axis_size("seq")
    devices = batch_size * seq_size
    seq_index = lax.axis_index("seq")
    rows, width = target.shape[1], target.shape[2]
    length, enc = target_segments.shape[1], memory_segments.shape[1]
    enc_rows = memory.shape[1]
    inner = self_query.shape[1]
    hidden = ffn_gate.shape[1]
    table_rows, table_cols = bias_table.shape
    weight_rows = self_query.shape[0]
    table_size = table_rows * table_cols

    small = jnp.concatenate(
        [self_norm_gain, cross_norm_gain, ffn_norm_gain, bias_table.reshape(-1)]
    )
    small = jnp.pad(small[None], ((0, weight_rows - 1), (0, LANES - small.shape[0])))
    first = gather_all(jnp.concatenate([self_query, self_key, self_value, small], axis=1))
    second = gather_all(
        jnp.concatenate([self_output, cross_query, cross_key, cross_value, cross_output], axis=1)
    )
    third = gather_all(jnp.concatenate([ffn_gate, ffn_up], axis=1))
    down = gather_all(ffn_down)
    w_query, w_kv = first[:, :inner], first[:, inner : 3 * inner]
    smalls = first[:, 3 * inner :].reshape(devices, weight_rows, LANES)[:, 0, :].astype(F32)
    gains = [smalls[:, i * weight_rows : (i + 1) * weight_rows].reshape(1, width) for i in range(3)]
    gain_self, gain_cross, gain_ffn = gains
    table = smalls[:, 3 * weight_rows : 3 * weight_rows + table_size]
    table = table.reshape(batch_size, seq_size, table_rows, table_cols)
    table = jnp.transpose(table, (0, 2, 1, 3)).reshape(batch_size * table_rows, seq_size * table_cols)
    w_out, w_cq, w_ckv, w_co = (
        second[:, :inner],
        second[:, inner : 2 * inner],
        second[:, 2 * inner : 4 * inner],
        second[:, 4 * inner :],
    )

    both = seq_gather(jnp.concatenate([target[0], memory[0]], axis=0))
    target_all = both[:, :rows].reshape(length, width)
    memory_all = both[:, rows:].reshape(enc, width)

    position = seq_index * rows
    heads = table.shape[1]
    distance = position + rows - jnp.arange(rows + length, dtype=jnp.int32)
    near = (distance >= 0) & (distance < length)
    bucket = jnp.take(bucket_ids, jnp.clip(distance, 0, length - 1))
    bucket_range = jnp.arange(table.shape[0], dtype=jnp.int32)
    onehot = ((bucket[:, None] == bucket_range[None, :]) & near[:, None]).astype(BF)
    windows = mm(table.astype(BF), onehot, (((0,), (1,)), ((), ())))
    windows = windows.reshape(heads // 2, 2, rows + length)
    no_windows = jnp.zeros((heads // 2, 2, LANES), F32)

    position1 = position.reshape(1)
    qseg = lax.dynamic_slice_in_dim(target_segments, position, rows, 1).reshape(rows, 1)
    kseg, mseg = target_segments, memory_segments

    target_float = target[0].astype(F32)
    normed_all = norm_gain(target_all.astype(F32), gain_self).astype(BF)
    normed_one = norm_gain(target_float, gain_self).astype(BF)
    queries = mm(normed_one, w_query).astype(BF)
    kv = mm(normed_all, w_kv).astype(BF)
    keys, values = kv[:, :inner], kv[:, inner:]
    attended = attend(position1, queries, keys, values, windows, qseg, kseg, True)
    hidden_one = target_float + mm(attended, w_out)
    normed_two = norm_gain(hidden_one, gain_cross).astype(BF)
    cross_queries = mm(normed_two, w_cq).astype(BF)
    cross_kv = mm(memory_all, w_ckv).astype(BF)
    cross_keys, cross_values = cross_kv[:, :inner], cross_kv[:, inner:]
    cross_attended = attend(
        position1, cross_queries, cross_keys, cross_values, no_windows, qseg, mseg, False
    )
    hidden_two = hidden_one + mm(cross_attended, w_co)
    normed_three = norm_gain(hidden_two, gain_ffn).astype(BF)
    gate_up = mm(normed_three, third)
    inner_act, gated_pull = jax.vjp(gated_unit, gate_up[:, :hidden], gate_up[:, hidden:])
    inner_low = inner_act.astype(BF)
    activations = (hidden_two + mm(inner_low, down)).astype(BF)

    cot = cotangent[0]
    grad_down = mm(inner_low, cot, TN).astype(BF)
    grad_gate, grad_up = gated_pull(mm(cot, down, NT))
    grad_gate_up = jnp.concatenate([grad_gate.astype(BF), grad_up.astype(BF)], axis=1)
    grad_third = mm(normed_three, grad_gate_up, TN).astype(BF)
    down_out = scatter_all(grad_down)
    third_out = scatter_all(grad_third)
    through, grad_gain_ffn = norm_back(hidden_two, gain_ffn, mm(grad_gate_up, third, NT))
    grad_hidden_two = cot.astype(F32) + through

    low_two = grad_hidden_two.astype(BF)
    grad_cross_attended = mm(low_two, w_co, NT).astype(BF)
    grad_cq, grad_ck, grad_cv, _ = attend_back(
        position1, cross_queries, cross_keys, cross_values, grad_cross_attended,
        no_windows, qseg, mseg, False,
    )
    grad_ckv = jnp.concatenate([grad_ck, grad_cv], axis=1)
    cross_out = scatter_all(
        jnp.concatenate(
            [
                mm(normed_two, grad_cq, TN).astype(BF),
                mm(memory_all, grad_ckv, TN).astype(BF),
                mm(cross_attended, low_two, TN).astype(BF),
            ],
            axis=1,
        )
    )
    memory_grad = seq_scatter(mm(grad_ckv, w_ckv, NT).reshape(seq_size, enc_rows, width))
    through, grad_gain_cross = norm_back(hidden_one, gain_cross, mm(grad_cq, w_cq, NT))
    grad_hidden_one = grad_hidden_two + through

    low_one = grad_hidden_one.astype(BF)
    grad_attended = mm(low_one, w_out, NT).astype(BF)
    grad_q, grad_k, grad_v, grad_windows = attend_back(
        position1, queries, keys, values, grad_attended, windows, qseg, kseg, True
    )
    grad_kv = jnp.concatenate([grad_k, grad_v], axis=1)
    normed_grad = seq_scatter(mm(grad_kv, w_kv, NT).reshape(seq_size, rows, width))
    normed_grad = normed_grad + mm(grad_q, w_query, NT)
    through, grad_gain_self = norm_back(target_float, gain_self, normed_grad)
    target_grad = grad_hidden_one + through

    grad_windows = grad_windows.reshape(heads, rows + length)
    grad_table = lax.dot_general(
        onehot.astype(F32), grad_windows, (((0,), (1,)), ((), ())), precision=lax.Precision.HIGHEST
    )
    grad_table = grad_table.reshape(batch_size, table_rows, seq_size, table_cols)
    grad_table = jnp.transpose(grad_table, (0, 2, 1, 3)).reshape(devices, table_size)
    gain_parts = [g.reshape(devices, weight_rows) for g in (grad_gain_self, grad_gain_cross, grad_gain_ffn)]
    small_grad = jnp.concatenate(gain_parts + [grad_table], axis=1)
    small_grad = jnp.pad(
        small_grad[:, None], ((0, 0), (0, weight_rows - 1), (0, LANES - small_grad.shape[1]))
    ).reshape(devices * weight_rows, LANES)
    self_out = scatter_all(
        jnp.concatenate(
            [
                mm(normed_one, grad_q, TN).astype(BF),
                mm(normed_all, grad_kv, TN).astype(BF),
                mm(attended, low_one, TN).astype(BF),
                small_grad.astype(BF),
            ],
            axis=1,
        )
    )
    cut = lambda packed, i: packed[:, i * inner : (i + 1) * inner]
    small_out = self_out[0, 4 * inner :]
    gain_out = [small_out[i * weight_rows : (i + 1) * weight_rows] for i in range(3)]
    table_out = small_out[3 * weight_rows : 3 * weight_rows + table_size]
    return (
        activations[None],
        target_grad[None],
        memory_grad[None],
        gain_out[0],
        cut(self_out, 0),
        cut(self_out, 1),
        cut(self_out, 2),
        cut(self_out, 3),
        table_out.reshape(table_rows, table_cols),
        gain_out[1],
        cut(cross_out, 0),
        cut(cross_out, 1),
        cut(cross_out, 2),
        cut(cross_out, 3),
        gain_out[2],
        third_out[:, :hidden],
        third_out[:, hidden:],
        down_out,
    )


def solution(mesh):
    rows3 = P("batch", "seq", None)
    seg = P("batch", None)
    gain = P(AXES)
    weight = P(AXES, None)
    table = P("batch", "seq")
    return jax.shard_map(
        per_device,
        mesh=mesh,
        in_specs=(
            rows3, rows3, rows3, seg, seg, P(),
            gain, weight, weight, weight, weight, table,
            gain, weight, weight, weight, weight,
            gain, weight, weight, weight,
        ),
        out_specs=(
            rows3, rows3, rows3,
            gain, weight, weight, weight, weight, table,
            gain, weight, weight, weight, weight,
            gain, weight, weight, weight,
        ),
        check_vma=False,
    )
```

```python
import functools

import jax
import jax.numpy as jnp
from jax import lax
from jax.experimental import pallas as pl
from jax.experimental.pallas import tpu as pltpu
from jax.sharding import PartitionSpec as P

HD = 64
LANES = 128
SUBLANES = 8
EPSILON = 1e-06
MASKED = -1e30
BF = jnp.bfloat16
F32 = jnp.float32
AXES = ("batch", "seq")
NT = (((1,), (1,)), ((), ()))
TN = (((0,), (0,)), ((), ()))
NN = (((1,), (0,)), ((), ()))


def mm(left, right, dims=NN):
    return lax.dot_general(left, right, dims, preferred_element_type=F32)


def norm_gain(values, gain):
    return values * lax.rsqrt(jnp.mean(values * values, axis=-1, keepdims=True) + EPSILON) * gain


def norm_back(values, gain, grad_out):
    _, pullback = jax.vjp(norm_gain, values, gain)
    return pullback(grad_out)


def gated_unit(gate_act, up_act):
    return jax.nn.gelu(gate_act, approximate=True) * up_act


def head_only(pair, head):
    lane = lax.broadcasted_iota(jnp.int32, pair.shape, 1)
    return jnp.where((lane // HD) == head, pair, jnp.zeros_like(pair))


def pick_heads(first, second):
    lane = lax.broadcasted_iota(jnp.int32, first.shape, 1)
    return jnp.where(lane < HD, first, second)


def spread(window, rows):
    wide = jnp.broadcast_to(window, (rows, window.shape[1]))
    rolled = pltpu.roll(wide, 0, 1, stride=1, stride_axis=0)
    return rolled[:, rows:]


def unspread(grads, rows):
    wide = jnp.concatenate([jnp.zeros((rows, rows), F32), grads], axis=1)
    width = wide.shape[1]
    total = wide[:SUBLANES]
    for start in range(SUBLANES, rows, SUBLANES):
        total = total + pltpu.roll(wide[start : start + SUBLANES], width - start, 1)
    row = lax.broadcasted_iota(jnp.int32, total.shape, 0)
    for bit in (1, 2, 4):
        total = jnp.where((row & bit) != 0, pltpu.roll(total, width - bit, 1), total)
    return jnp.sum(total, axis=0, keepdims=True)


def allowed_pairs(position, query_segments, key_segments, causal):
    rows, keys = query_segments.shape[0], key_segments.shape[1]
    allowed = query_segments == key_segments
    if causal:
        own = lax.broadcasted_iota(jnp.int32, (rows, keys), 0) + position
        other = lax.broadcasted_iota(jnp.int32, (rows, keys), 1)
        allowed = allowed & (own >= other)
    return allowed


def pair_probs(query, key, bias_ref, allowed, head, causal):
    scores = mm(head_only(query, head), key, NT)
    if causal:
        scores = scores + spread(bias_ref[0, head : head + 1, :], query.shape[0])
    scores = jnp.where(allowed, scores, MASKED)
    top = jnp.max(scores, axis=1, keepdims=True)
    grown = jnp.exp(scores - top)
    return grown / jnp.sum(grown, axis=1, keepdims=True)


def attend_body(causal, pos_ref, q_ref, k_ref, v_ref, bias_ref, qseg_ref, kseg_ref, out_ref):
    query, key, value = q_ref[...], k_ref[...], v_ref[...]
    allowed = allowed_pairs(pos_ref[0], qseg_ref[...], kseg_ref[...], causal)
    parts = []
    for head in range(2):
        probs = pair_probs(query, key, bias_ref, allowed, head, causal)
        parts.append(mm(probs.astype(BF), value))
    out_ref[...] = pick_heads(*parts).astype(BF)


def attend_back_body(
    causal, pos_ref, q_ref, k_ref, v_ref, do_ref, bias_ref, qseg_ref, kseg_ref,
    dq_ref, dk_ref, dv_ref, dbias_ref,
):
    query, key, value, grad = q_ref[...], k_ref[...], v_ref[...], do_ref[...]
    allowed = allowed_pairs(pos_ref[0], qseg_ref[...], kseg_ref[...], causal)
    grad_query, grad_key, grad_value = [], 0.0, 0.0
    for head in range(2):
        probs = pair_probs(query, key, bias_ref, allowed, head, causal)
        grad_head = head_only(grad, head)
        grad_probs = mm(grad_head, value, NT)
        inner = jnp.sum(probs * grad_probs, axis=1, keepdims=True)
        grad_scores = probs * (grad_probs - inner)
        low_scores = grad_scores.astype(BF)
        grad_query.append(mm(low_scores, key))
        grad_key = grad_key + mm(low_scores, head_only(query, head), TN)
        grad_value = grad_value + mm(probs.astype(BF), grad_head, TN)
        if causal:
            dbias_ref[0, head : head + 1, :] = unspread(grad_scores, query.shape[0])
    if not causal:
        dbias_ref[...] = jnp.zeros_like(dbias_ref)
    dq_ref[...] = pick_heads(*grad_query).astype(BF)
    dk_ref[...] = grad_key.astype(BF)
    dv_ref[...] = grad_value.astype(BF)


def attention_specs(rows, keys, width):
    pair = lambda count: pl.BlockSpec((count, LANES), lambda step: (0, step))
    whole = lambda shape: pl.BlockSpec(shape, lambda step: (0, 0))
    smem = pl.BlockSpec(memory_space=pltpu.SMEM)
    bias = pl.BlockSpec((1, 2, width), lambda step: (step, 0, 0))
    return pair, bias, smem, [whole((rows, 1)), whole((1, keys))]


PARAMS = pltpu.CompilerParams(dimension_semantics=("arbitrary",), vmem_limit_bytes=48 << 20)


def attend(position, query, key, value, windows, qseg, kseg, causal):
    rows, inner = query.shape
    keys = key.shape[0]
    pair, bias, smem, segs = attention_specs(rows, keys, windows.shape[2])
    return pl.pallas_call(
        functools.partial(attend_body, causal),
        grid=(inner // LANES,),
        in_specs=[smem, pair(rows), pair(keys), pair(keys), bias] + segs,
        out_specs=pair(rows),
        out_shape=jax.ShapeDtypeStruct((rows, inner), BF),
        compiler_params=PARAMS,
        name="attend_self" if causal else "attend_cross",
    )(position, query, key, value, windows, qseg, kseg)


def attend_back(position, query, key, value, grad, windows, qseg, kseg, causal):
    rows, inner = query.shape
    keys = key.shape[0]
    pair, bias, smem, segs = attention_specs(rows, keys, windows.shape[2])
    return pl.pallas_call(
        functools.partial(attend_back_body, causal),
        grid=(inner // LANES,),
        in_specs=[smem, pair(rows), pair(keys), pair(keys), pair(rows), bias] + segs,
        out_specs=[pair(rows), pair(keys), pair(keys), bias],
        out_shape=[
            jax.ShapeDtypeStruct((rows, inner), BF),
            jax.ShapeDtypeStruct((keys, inner), BF),
            jax.ShapeDtypeStruct((keys, inner), BF),
            jax.ShapeDtypeStruct(windows.shape, F32),
        ],
        compiler_params=PARAMS,
        name="attend_self_back" if causal else "attend_cross_back",
    )(position, query, key, value, grad, windows, qseg, kseg)


def seq_perm(size, step):
    return [(i, (i + step) % size) for i in range(size)]


def seq_gather(rows):
    size, own = lax.axis_size("seq"), lax.axis_index("seq")
    full = jnp.zeros((size,) + rows.shape, rows.dtype)
    full = lax.dynamic_update_slice_in_dim(full, rows[None], own, 0)
    for step in range(1, size):
        piece = lax.ppermute(rows, "seq", seq_perm(size, step))
        full = lax.dynamic_update_slice_in_dim(full, piece[None], (own - step) % size, 0)
    return full


def seq_scatter(parts):
    size, own = lax.axis_size("seq"), lax.axis_index("seq")
    total = lax.dynamic_index_in_dim(parts, own, 0, False)
    low = parts.astype(BF)
    for step in range(1, size):
        piece = lax.dynamic_index_in_dim(low, (own + step) % size, 0, False)
        total = total + lax.ppermute(piece, "seq", seq_perm(size, step)).astype(F32)
    return total


def gather_all(shard):
    return lax.all_gather(shard, AXES, axis=0, tiled=True)


def scatter_all(grads):
    return lax.psum_scatter(grads, AXES, scatter_dimension=0, tiled=True).astype(F32)


class Links:
    def __init__(self):
        self.batch, self.seq = lax.axis_size("batch"), lax.axis_size("seq")
        self.depth = self.batch // 2
        z_x, y_c = lax.axis_index("batch"), lax.axis_index("seq")
        self.z, self.x = z_x // 2, z_x % 2
        self.y, self.core = y_c // 2, y_c % 2
        self.lead = self.core == 0
        self.place = jnp.stack([self.z, self.x, self.y, self.core]).astype(jnp.int32)

    def move(self, value, target):
        pairs = []
        for source in range(self.batch * self.seq):
            z_x, y_c = source // self.seq, source % self.seq
            z, x, y, core = target(z_x // 2, z_x % 2, y_c // 2, y_c % 2)
            pairs.append((source, (z * 2 + x) * self.seq + y * 2 + core))
        return lax.ppermute(value, AXES, pairs)

    def over_core(self, value):
        return self.move(value, lambda z, x, y, core: (z, x, y, 1 - core))

    def over_near(self, value):
        return self.move(
            value, lambda z, x, y, c: (z, x, 1 - y, c) if c else (z, 1 - x, y, c)
        )

    def over_far(self, value):
        return self.move(
            value, lambda z, x, y, c: (z, 1 - x, y, c) if c else (z, x, 1 - y, c)
        )

    def over_z(self, value, step):
        depth = self.depth
        return self.move(value, lambda z, x, y, core: ((z - step) % depth, x, y, core))


def in_order(first, own, other):
    return jnp.concatenate([jnp.where(first, own, other), jnp.where(first, other, own)], axis=0)


def gather_core(links, left, right):
    own = jnp.where(links.lead, left, right)
    other = links.over_core(jnp.where(links.lead, right, left))
    return in_order(links.lead, own, other)


def z_steps(links, value, steps):
    return [links.over_z(value, step) for step in steps]


def gather_near(links, value):
    return jnp.stack([value, links.over_near(value)])


def assemble(links, near, far, near_other, far_other):
    depth, rows, cols = near.shape[1:]

    def body(place_ref, *refs):
        sources, out_ref, sem = refs[:4], refs[4], refs[5]
        z, x, y, core = [place_ref[i] for i in range(4)]
        for which, source in enumerate(sources):
            half = core if which < 2 else 1 - core
            far_step = which % 2
            for near_step in range(2):
                step_x = jnp.where(half == 0, near_step, far_step)
                step_y = jnp.where(half == 0, far_step, near_step)
                for step in range(depth):
                    chip = (((z + step) % depth) * 2 + (x ^ step_x)) * 2 + (y ^ step_y)
                    target = out_ref.at[
                        pl.ds(pl.multiple_of(chip * rows, 16), rows),
                        pl.ds(pl.multiple_of(half * cols, LANES), cols),
                    ]
                    pltpu.make_async_copy(source.at[near_step, step], target, sem).start()
        pltpu.make_async_copy(out_ref, out_ref, sem).wait()

    anywhere = pl.BlockSpec(memory_space=pl.ANY)
    return pl.pallas_call(
        body,
        in_specs=[pl.BlockSpec(memory_space=pltpu.SMEM)] + [anywhere] * 4,
        out_specs=pl.BlockSpec(memory_space=pltpu.VMEM),
        out_shape=jax.ShapeDtypeStruct((depth * 4 * rows, 2 * cols), near.dtype),
        scratch_shapes=[pltpu.SemaphoreType.DMA(())],
        compiler_params=pltpu.CompilerParams(vmem_limit_bytes=48 << 20),
        name="assemble",
    )(links.place, near, far, near_other, far_other)


def weight_grad(links, core, terms, extra=None):
    depth, total_rows = links.depth, terms[0][0].shape[1]
    rows = total_rows // (depth * 4)
    widths = [term[1].shape[1] for term in terms]
    extra_width = 0 if extra is None else extra.shape[1]
    total = sum(widths) + extra_width
    tile = 1408 if total % 1408 == 0 else 512

    def body(place_ref, *refs):
        inputs, out_ref, stage, sems = refs[:-3], refs[-3], refs[-2], refs[-1]
        z, x, y, left = place_ref[0], place_ref[1], place_ref[2], place_ref[3] == 0
        places = []
        for chip in range(depth * 4):
            step_x, step_y = (chip // 2 % 2) ^ x, (chip % 2) ^ y
            near, far = jnp.where(left, step_x, step_y), jnp.where(left, step_y, step_x)
            spot = (near * 2 + far) * depth + (chip // 4 - z) % depth
            places.append(pl.multiple_of(spot * rows, 8))
        copies, start = [], 0

        def emit(start, value, width):
            for chip, spot in enumerate(places):
                stage[pl.ds(spot, rows), start : start + width] = value[
                    chip * rows : (chip + 1) * rows
                ].astype(BF)
            copies.append(
                pltpu.make_async_copy(
                    stage.at[:, pl.ds(start, width)],
                    out_ref.at[:, pl.ds(start, width)],
                    sems.at[len(copies)],
                )
            )
            copies[-1].start()

        for index, width in enumerate(widths):
            acts_l, grad_l, acts_r, grad_r = inputs[4 * index : 4 * index + 4]
            acts = jnp.where(left, acts_l[...], acts_r[...])
            for offset in range(0, width, tile):
                cols = slice(offset, offset + tile)
                grad = jnp.where(left, grad_l[:, cols], grad_r[:, cols])
                emit(start, mm(acts, grad, TN), tile)
                start += tile
        if extra is not None:
            small = inputs[-1][...]
            emit(start, jnp.where(left, small, jnp.zeros_like(small)), extra_width)
        for copy in copies:
            copy.wait()

    place = links.place.at[3].set(core)
    operands = [array for term in terms for array in term] + ([] if extra is None else [extra])
    count = sum(width // tile for width in widths) + (extra is not None)
    vmem = pl.BlockSpec(memory_space=pltpu.VMEM)
    return pl.pallas_call(
        body,
        in_specs=[pl.BlockSpec(memory_space=pltpu.SMEM)] + [vmem] * len(operands),
        out_specs=pl.BlockSpec(memory_space=pl.ANY),
        out_shape=jax.ShapeDtypeStruct((total_rows, total), BF),
        scratch_shapes=[pltpu.VMEM((total_rows, total), BF), pltpu.SemaphoreType.DMA((count,))],
        compiler_params=pltpu.CompilerParams(vmem_limit_bytes=48 << 20),
        name="weight_grad",
    )(place, *operands)


class Scatter:
    def __init__(self, links):
        self.links, self.parts = links, []

    def core(self, sent):
        self.rows = sent.shape[0]
        self.parts.append(self.links.over_core(sent))

    def keep(self, kept):
        self.parts.append(kept)

    def total(self, start, count):
        return sum(part[start : start + count].astype(F32) for part in self.parts)

    def halve(self):
        self.rows //= 2
        return self.total(self.rows, self.rows).astype(BF)

    def near(self, send):
        self.parts.append(self.links.over_near(send))

    def far(self, send):
        self.parts.append(self.links.over_far(send))

    def z_sends(self):
        self.rows //= self.links.depth
        return [
            self.total(step * self.rows, self.rows).astype(BF)
            for step in range(1, self.links.depth)
        ]

    def z(self, sends):
        depth = self.links.depth
        for step, send in enumerate(sends, 1):
            self.parts.append(self.links.over_z(send, depth - step))

    def own(self):
        return self.total(0, self.rows)

    def last(self, total):
        links, half = self.links, self.rows // 2
        above, below = total[:half], total[half:]
        own = jnp.where(links.lead, above, below)
        other = links.over_core(jnp.where(links.lead, below, above))
        return jnp.where(links.lead, own, other), jnp.where(links.lead, other, own)


class PlainScatter:
    def core(self, sent):
        self.sent = sent

    def keep(self, kept):
        self.kept = kept

    def halve(self):
        return self.sent

    def near(self, send):
        self.sent = send

    far = z = near
    z_sends = own = halve

    def last(self, total):
        whole = scatter_all(self.kept)
        return jnp.split(whole, 2, axis=1)


def phase(*values):
    return lax.optimization_barrier(values)


def per_device(
    target, memory, cotangent, target_segments, memory_segments, bucket_ids,
    self_norm_gain, self_query, self_key, self_value, self_output, bias_table,
    cross_norm_gain, cross_query, cross_key, cross_value, cross_output,
    ffn_norm_gain, ffn_gate, ffn_up, ffn_down,
):
    batch_size, seq_size = lax.axis_size("batch"), lax.axis_size("seq")
    devices = batch_size * seq_size
    seq_index = lax.axis_index("seq")
    rows, width = target.shape[1], target.shape[2]
    length, enc = target_segments.shape[1], memory_segments.shape[1]
    enc_rows = memory.shape[1]
    inner = self_query.shape[1]
    hidden = ffn_gate.shape[1]
    table_rows, table_cols = bias_table.shape
    weight_rows = self_query.shape[0]
    table_size = table_rows * table_cols

    links = Links()
    core, lead, depth = links.core, links.lead, links.depth
    small = jnp.concatenate(
        [self_norm_gain, cross_norm_gain, ffn_norm_gain, bias_table.reshape(-1)]
    )
    small = jnp.pad(small[None], ((0, weight_rows - 1), (0, 2 * LANES - small.shape[0])))
    groups = [
        [self_query, self_key, self_value, small],
        [self_output, cross_query, cross_key, cross_value, cross_output],
        [ffn_gate, ffn_up],
    ]
    groups = [jnp.concatenate(group, axis=1) for group in groups]
    cuts = [group.shape[1] // 2 for group in groups]
    left = jnp.concatenate([group[:, :cut] for group, cut in zip(groups, cuts)], axis=1)
    right = jnp.concatenate([group[:, cut:] for group, cut in zip(groups, cuts)], axis=1)
    down_cut = width // 2
    steps = list(range(1, depth))
    some, rest = steps[:1], steps[1:]

    moved = gather_core(links, left, right)
    direct = 2 * ffn_down.shape[0] % 16 == 0
    if direct:
        down0 = gather_core(links, ffn_down[:, :down_cut], ffn_down[:, down_cut:])
    else:
        down0 = gather_all(ffn_down)
    rows_own = jnp.concatenate([target[0], memory[0]], axis=0)
    rows_other = [
        lax.ppermute(rows_own, "seq", seq_perm(seq_size, step)) for step in range(1, seq_size)
    ]
    moved, down0 = phase(moved, down0)
    first0 = moved[:, : cuts[0]]
    second0 = moved[:, cuts[0] : cuts[0] + cuts[1]]
    third0 = moved[:, cuts[0] + cuts[1] :]

    first_z = z_steps(links, first0, steps)
    first_z = jnp.stack([first0] + first_z)
    first_z, second0, third0, rows_other = phase(first_z, second0, third0, rows_other)

    first_near = gather_near(links, first_z)
    second_z = z_steps(links, second0, some)
    both = jnp.zeros((seq_size,) + rows_own.shape, rows_own.dtype)
    for step, piece in enumerate([rows_own] + rows_other):
        both = lax.dynamic_update_slice_in_dim(both, piece[None], (seq_index - step) % seq_size, 0)
    target_all = both[:, :rows].reshape(length, width)
    memory_all = both[:, rows:].reshape(enc, width)
    first_near, second_z, second0, target_all, memory_all = phase(
        first_near, second_z, second0, target_all, memory_all
    )

    first_far = links.over_far(first_near)
    first_near_other = links.over_core(first_near)
    second_z = jnp.stack([second0] + second_z + z_steps(links, second0, rest))
    first_far, first_near_other, second_z, third0 = phase(
        first_far, first_near_other, second_z, third0
    )

    second_near = gather_near(links, second_z)
    third_z = z_steps(links, third0, some)
    first = assemble(
        links, first_near, first_far, first_near_other, links.over_core(first_far)
    )
    first, second_near, third_z, third0, down0 = phase(first, second_near, third_z, third0, down0)

    w_query, w_kv = first[:, :inner], first[:, inner : 3 * inner]
    smalls = first[:, 3 * inner :].reshape(devices, weight_rows, 2 * LANES)[:, 0, :].astype(F32)
    gains = [smalls[:, i * weight_rows : (i + 1) * weight_rows].reshape(1, width) for i in range(3)]
    gain_self, gain_cross, gain_ffn = gains
    table = smalls[:, 3 * weight_rows : 3 * weight_rows + table_size]
    table = table.reshape(batch_size, seq_size, table_rows, table_cols)
    table = jnp.transpose(table, (0, 2, 1, 3)).reshape(batch_size * table_rows, seq_size * table_cols)

    position = seq_index * rows
    heads = table.shape[1]
    distance = position + rows - jnp.arange(rows + length, dtype=jnp.int32)
    near = (distance >= 0) & (distance < length)
    bucket = jnp.take(bucket_ids, jnp.clip(distance, 0, length - 1))
    bucket_range = jnp.arange(table.shape[0], dtype=jnp.int32)
    onehot = ((bucket[:, None] == bucket_range[None, :]) & near[:, None]).astype(BF)
    windows = mm(table.astype(BF), onehot, (((0,), (1,)), ((), ())))
    windows = windows.reshape(heads // 2, 2, rows + length)
    no_windows = jnp.zeros((heads // 2, 2, LANES), F32)
    position1 = position.reshape(1)
    qseg = lax.dynamic_slice_in_dim(target_segments, position, rows, 1).reshape(rows, 1)
    kseg, mseg = target_segments, memory_segments

    second_far = links.over_far(second_near)
    second_near_other = links.over_core(second_near)
    third_z = jnp.stack([third0] + third_z + z_steps(links, third0, rest))
    target_float = target[0].astype(F32)
    normed_all = norm_gain(target_all.astype(F32), gain_self).astype(BF)
    normed_one = norm_gain(target_float, gain_self).astype(BF)
    queries = mm(normed_one, w_query).astype(BF)
    kv = mm(normed_all, w_kv).astype(BF)
    keys, values = kv[:, :inner], kv[:, inner:]
    attended = attend(position1, queries, keys, values, windows, qseg, kseg, True)
    attended, second_far, second_near_other, third_z, down0 = phase(
        attended, second_far, second_near_other, third_z, down0
    )

    third_near = gather_near(links, third_z)
    down_z = z_steps(links, down0, some) if direct else down0
    second = assemble(
        links, second_near, second_far, second_near_other, links.over_core(second_far)
    )
    second, third_near, down_z, down0 = phase(second, third_near, down_z, down0)

    w_out, w_cq, w_ckv, w_co = (
        second[:, :inner],
        second[:, inner : 2 * inner],
        second[:, 2 * inner : 4 * inner],
        second[:, 4 * inner :],
    )

    third_far = links.over_far(third_near)
    third_near_other = links.over_core(third_near)
    if direct:
        down_z = jnp.stack([down0] + down_z + z_steps(links, down0, rest))
    hidden_one = target_float + mm(attended, w_out)
    normed_two = norm_gain(hidden_one, gain_cross).astype(BF)
    cross_queries = mm(normed_two, w_cq).astype(BF)
    cross_kv = mm(memory_all, w_ckv).astype(BF)
    cross_keys, cross_values = cross_kv[:, :inner], cross_kv[:, inner:]
    cross_attended = attend(
        position1, cross_queries, cross_keys, cross_values, no_windows, qseg, mseg, False
    )
    hidden_two = hidden_one + mm(cross_attended, w_co)
    normed_three = norm_gain(hidden_two, gain_ffn).astype(BF)
    normed_three, third_far, third_near_other, down_z = phase(
        normed_three, third_far, third_near_other, down_z
    )

    down_near = gather_near(links, down_z) if direct else down_z
    third = assemble(links, third_near, third_far, third_near_other, links.over_core(third_far))
    third, down_near = phase(third, down_near)

    down_far = links.over_far(down_near) if direct else down_near
    down_near_other = links.over_core(down_near) if direct else down_near
    gate_up = mm(normed_three, third)
    inner_act, gated_pull = jax.vjp(gated_unit, gate_up[:, :hidden], gate_up[:, hidden:])
    inner_low = inner_act.astype(BF)
    inner_low, down_far, down_near_other = phase(inner_low, down_far, down_near_other)
    if direct:
        down = assemble(links, down_near, down_far, down_near_other, links.over_core(down_far))
    else:
        down = down_near

    cot = cotangent[0]
    grad_gate, grad_up = gated_pull(mm(cot, down, NT))
    grad_gate, grad_up = grad_gate.astype(BF), grad_up.astype(BF)
    ffn_terms = [(normed_three, grad_gate, normed_three, grad_up)]
    down_terms = [(inner_low, cot[:, :down_cut], inner_low, cot[:, down_cut:])]
    ffn_sum, down_sum = Scatter(links), Scatter(links) if direct else PlainScatter()
    ffn_send = weight_grad(links, 1 - core, ffn_terms)
    ffn_send, grad_gate, grad_up = phase(ffn_send, grad_gate, grad_up)

    ffn_sum.core(ffn_send)
    down_send = weight_grad(links, 1 - core, down_terms) if direct else inner_low
    activations = (hidden_two + mm(inner_low, down)).astype(BF)
    grad_gate_up = jnp.concatenate([grad_gate, grad_up], axis=1)
    through, grad_gain_ffn = norm_back(hidden_two, gain_ffn, mm(grad_gate_up, third, NT))
    grad_hidden_two = cot.astype(F32) + through
    ffn_sum.keep(weight_grad(links, core, ffn_terms))
    ffn_send = ffn_sum.halve()
    ffn_send, grad_hidden_two, down_send = phase(ffn_send, grad_hidden_two, down_send)

    ffn_sum.near(ffn_send)
    down_sum.core(down_send)
    if direct:
        down_sum.keep(weight_grad(links, core, down_terms))
    else:
        down_sum.keep(mm(inner_low, cot, TN).astype(BF))
    low_two = grad_hidden_two.astype(BF)
    grad_cross_attended = mm(low_two, w_co, NT).astype(BF)
    grad_cq, grad_ck, grad_cv, _ = attend_back(
        position1, cross_queries, cross_keys, cross_values, grad_cross_attended,
        no_windows, qseg, mseg, False,
    )
    cross_terms = [
        (normed_two, grad_cq, cross_attended, low_two),
        (memory_all, grad_ck, memory_all, grad_cv),
    ]
    cross_sum = Scatter(links)
    cross_send = weight_grad(links, 1 - core, cross_terms)
    ffn_send, down_send = ffn_sum.halve(), down_sum.halve()
    ffn_send, down_send, cross_send, grad_cq = phase(ffn_send, down_send, cross_send, grad_cq)

    cross_sum.core(cross_send)
    ffn_sum.far(ffn_send)
    down_sum.near(down_send)
    through, grad_gain_cross = norm_back(hidden_one, gain_cross, mm(grad_cq, w_cq, NT))
    grad_hidden_one = grad_hidden_two + through
    low_one = grad_hidden_one.astype(BF)
    grad_attended = mm(low_one, w_out, NT).astype(BF)
    cross_sum.keep(weight_grad(links, core, cross_terms))
    grad_ckv = jnp.concatenate([grad_ck, grad_cv], axis=1)
    memory_part = mm(grad_ckv, w_ckv, NT).reshape(seq_size, enc_rows, width)
    cross_send, ffn_sends, down_send = cross_sum.halve(), ffn_sum.z_sends(), down_sum.halve()
    grad_attended, cross_send, ffn_sends, down_send, memory_part = phase(
        grad_attended, cross_send, ffn_sends, down_send, memory_part
    )

    cross_sum.near(cross_send)
    ffn_sum.z(ffn_sends)
    down_sum.far(down_send)
    grad_q, grad_k, grad_v, grad_windows = attend_back(
        position1, queries, keys, values, grad_attended, windows, qseg, kseg, True
    )
    grad_kv = jnp.concatenate([grad_k, grad_v], axis=1)
    grad_normed_kv = mm(grad_kv, w_kv, NT)
    grad_normed_q = mm(grad_q, w_query, NT)
    grad_windows = grad_windows.reshape(heads, rows + length)
    grad_table = lax.dot_general(
        onehot.astype(F32), grad_windows, (((0,), (1,)), ((), ())), precision=lax.Precision.HIGHEST
    )
    grad_table = grad_table.reshape(batch_size, table_rows, seq_size, table_cols)
    grad_table = jnp.transpose(grad_table, (0, 2, 1, 3)).reshape(devices, table_size)
    unit = lambda values: values * lax.rsqrt(
        jnp.mean(values * values, axis=-1, keepdims=True) + EPSILON
    )
    grad_gain_self = jnp.sum(unit(target_all.astype(F32)) * grad_normed_kv, axis=0) + jnp.sum(
        unit(target_float) * grad_normed_q, axis=0
    )
    gain_parts = [g.reshape(devices, weight_rows) for g in (grad_gain_self, grad_gain_cross, grad_gain_ffn)]
    small_grad = jnp.concatenate(gain_parts + [grad_table], axis=1)
    small_grad = jnp.pad(
        small_grad[:, None], ((0, 0), (0, weight_rows - 1), (0, LANES - small_grad.shape[1]))
    ).reshape(devices * weight_rows, LANES)
    self_terms = [
        (normed_one, grad_q, attended, low_one),
        (normed_all, grad_k, normed_all, grad_v),
    ]
    self_sum = Scatter(links)
    self_send = weight_grad(links, 1 - core, self_terms, small_grad)
    ffn_total, cross_send, down_sends = ffn_sum.own(), cross_sum.halve(), down_sum.z_sends()
    self_send, ffn_total, cross_send, down_sends, grad_normed_kv = phase(
        self_send, ffn_total, cross_send, down_sends, grad_normed_kv
    )

    self_sum.core(self_send)
    cross_sum.far(cross_send)
    down_sum.z(down_sends)
    grad_gate, grad_up = ffn_sum.last(ffn_total)
    self_sum.keep(weight_grad(links, core, self_terms, small_grad))
    self_send, cross_sends, down_total = self_sum.halve(), cross_sum.z_sends(), down_sum.own()
    self_send, cross_sends, down_total, grad_gate, grad_up = phase(
        self_send, cross_sends, down_total, grad_gate, grad_up
    )

    self_sum.near(self_send)
    cross_sum.z(cross_sends)
    down_left, down_right = down_sum.last(down_total)
    memory_grad = seq_scatter(memory_part)
    normed_grad = seq_scatter(grad_normed_kv.reshape(seq_size, rows, width)) + grad_normed_q
    through, _ = norm_back(target_float, gain_self, normed_grad)
    target_grad = grad_hidden_one + through
    self_send, cross_total = self_sum.halve(), cross_sum.own()
    self_send, cross_total, down_left, down_right = phase(
        self_send, cross_total, down_left, down_right
    )
    self_sum.far(self_send)
    cross_left, cross_right = cross_sum.last(cross_total)
    self_sum.z(self_sum.z_sends())
    self_left, self_right = self_sum.last(self_sum.own())
    down_out = jnp.concatenate([down_left, down_right], axis=1)

    small_out = self_left[0, 2 * inner :]
    gain_out = [small_out[i * weight_rows : (i + 1) * weight_rows] for i in range(3)]
    table_out = small_out[3 * weight_rows : 3 * weight_rows + table_size]
    return (
        activations[None],
        target_grad[None],
        memory_grad[None],
        gain_out[0],
        self_left[:, :inner],
        self_left[:, inner : 2 * inner],
        self_right[:, inner : 2 * inner],
        self_right[:, :inner],
        table_out.reshape(table_rows, table_cols),
        gain_out[1],
        cross_left[:, :inner],
        cross_left[:, inner:],
        cross_right[:, inner:],
        cross_right[:, :inner],
        gain_out[2],
        grad_gate,
        grad_up,
        down_out,
    )


def solution(mesh):
    rows3 = P("batch", "seq", None)
    seg = P("batch", None)
    gain = P(AXES)
    weight = P(AXES, None)
    table = P("batch", "seq")
    return jax.shard_map(
        per_device,
        mesh=mesh,
        in_specs=(
            rows3, rows3, rows3, seg, seg, P(),
            gain, weight, weight, weight, weight, table,
            gain, weight, weight, weight, weight,
            gain, weight, weight, weight,
        ),
        out_specs=(
            rows3, rows3, rows3,
            gain, weight, weight, weight, weight, table,
            gain, weight, weight, weight, weight,
            gain, weight, weight, weight,
        ),
        check_vma=False,
    )
```

```python
import functools

import jax
import jax.numpy as jnp
import numpy as np
from jax import lax
from jax.experimental import pallas as pl
from jax.experimental.pallas import tpu as pltpu
from jax.sharding import PartitionSpec as P

HD = 64
LANES = 128
SUBLANES = 8
EPSILON = 1e-06
MASKED = -1e30
BF = jnp.bfloat16
F32 = jnp.float32
AXES = ("batch", "seq")
NT = (((1,), (1,)), ((), ()))
TN = (((0,), (0,)), ((), ()))
NN = (((1,), (0,)), ((), ()))


def mm(left, right, dims=NN):
    return lax.dot_general(left, right, dims, preferred_element_type=F32)


def gated_unit(gate_act, up_act):
    return jax.nn.gelu(gate_act, approximate=True) * up_act


def head_only(pair, head):
    lane = lax.broadcasted_iota(jnp.int32, pair.shape, 1)
    return jnp.where((lane // HD) == head, pair, jnp.zeros_like(pair))


def pick_heads(first, second):
    lane = lax.broadcasted_iota(jnp.int32, first.shape, 1)
    return jnp.where(lane < HD, first, second)


def spread(window, rows):
    wide = jnp.broadcast_to(window, (rows, window.shape[1]))
    rolled = pltpu.roll(wide, 0, 1, stride=1, stride_axis=0)
    return rolled[:, rows:]


def unspread(grads, rows):
    wide = jnp.concatenate([jnp.zeros((rows, rows), F32), grads], axis=1)
    width = wide.shape[1]
    total = wide[:SUBLANES]
    for start in range(SUBLANES, rows, SUBLANES):
        total = total + pltpu.roll(wide[start : start + SUBLANES], width - start, 1)
    row = lax.broadcasted_iota(jnp.int32, total.shape, 0)
    for bit in (1, 2, 4):
        total = jnp.where((row & bit) != 0, pltpu.roll(total, width - bit, 1), total)
    return jnp.sum(total, axis=0, keepdims=True)


def allowed_pairs(position, query_segments, key_segments, causal):
    rows, keys = query_segments.shape[0], key_segments.shape[1]
    allowed = query_segments == key_segments
    if causal:
        own = lax.broadcasted_iota(jnp.int32, (rows, keys), 0) + position
        other = lax.broadcasted_iota(jnp.int32, (rows, keys), 1)
        allowed = allowed & (own >= other)
    return allowed


def pair_probs(query, key, bias_ref, allowed, head, causal):
    scores = mm(head_only(query, head), key, NT)
    if causal:
        scores = scores + spread(bias_ref[0, head : head + 1, :], query.shape[0])
    scores = jnp.where(allowed, scores, MASKED)
    top = jnp.max(scores, axis=1, keepdims=True)
    grown = jnp.exp(scores - top)
    return grown / jnp.sum(grown, axis=1, keepdims=True)


def attend_pair(query, key, value, bias_ref, allowed, causal):
    parts = []
    for head in range(2):
        probs = pair_probs(query, key, bias_ref, allowed, head, causal)
        parts.append(mm(probs.astype(BF), value))
    return pick_heads(*parts).astype(BF)


def attend_pair_back(query, key, value, grad, bias_ref, dbias_ref, allowed, causal):
    grad_query, grad_key, grad_value = [], 0.0, 0.0
    for head in range(2):
        probs = pair_probs(query, key, bias_ref, allowed, head, causal)
        grad_head = head_only(grad, head)
        grad_probs = mm(grad_head, value, NT)
        inner = jnp.sum(probs * grad_probs, axis=1, keepdims=True)
        grad_scores = probs * (grad_probs - inner)
        low_scores = grad_scores.astype(BF)
        grad_query.append(mm(low_scores, key))
        grad_key = grad_key + mm(low_scores, head_only(query, head), TN)
        grad_value = grad_value + mm(probs.astype(BF), grad_head, TN)
        if causal:
            dbias_ref[0, head : head + 1, :] = unspread(grad_scores, query.shape[0])
    return pick_heads(*grad_query).astype(BF), grad_key.astype(BF), grad_value.astype(BF)


def scale_of(values):
    return lax.rsqrt(jnp.mean(values * values, axis=-1, keepdims=True) + EPSILON)


def norm_back(values, gain, grad_out):
    scale = scale_of(values)
    unit = values * scale
    lean = jnp.mean(grad_out * gain * unit, axis=-1, keepdims=True)
    grad_gain = jnp.sum(grad_out * unit, axis=0, keepdims=True)
    return scale * (grad_out * gain - unit * lean), grad_gain


def cost(microseconds):
    return pl.CostEstimate(flops=microseconds * 10**9, bytes_accessed=1, transcendentals=0)


PARAMS = pltpu.CompilerParams(dimension_semantics=("arbitrary",), vmem_limit_bytes=48 << 20)
SMEM = pl.BlockSpec(memory_space=pltpu.SMEM)


def whole(array, rows=None):
    shape = array.shape if rows is None else (rows, array.shape[1])
    return pl.BlockSpec(shape, lambda step: (0,) * len(shape))


def pair_cols(rows, offset=0):
    return pl.BlockSpec((rows, LANES), lambda step: (0, offset + step))


def shape_of(*shape, dtype=BF):
    return jax.ShapeDtypeStruct(shape, dtype)


def windows_spec(windows):
    return pl.BlockSpec((1, 2, windows.shape[2]), lambda step: (step, 0, 0))


def self_forward(place, target_all, gain, weights, windows, qseg, kseg):
    (length, width), rows = target_all.shape, qseg.shape[0]
    inner = windows.shape[0] * LANES
    pairs = inner // LANES

    def body(
        pos_ref, rows_ref, gain_ref, wq_ref, wk_ref, wv_ref, win_ref, qseg_ref, kseg_ref,
        out_ref, q_ref, k_ref, v_ref, normed_ref,
    ):
        position = pl.multiple_of(pos_ref[0], LANES)

        @pl.when(pl.program_id(0) == 0)
        def _():
            values = rows_ref[...].astype(F32)
            normed_ref[...] = (values * scale_of(values) * gain_ref[...]).astype(BF)

        normed = normed_ref[...]
        query = mm(normed_ref[pl.ds(position, rows), :], wq_ref[...]).astype(BF)
        key = mm(normed, wk_ref[...]).astype(BF)
        value = mm(normed, wv_ref[...]).astype(BF)
        q_ref[...], k_ref[...], v_ref[...] = query, key, value
        allowed = allowed_pairs(position, qseg_ref[...], kseg_ref[...], True)
        out_ref[...] = attend_pair(query, key, value, win_ref, allowed, True)

    return pl.pallas_call(
        body,
        grid=(pairs,),
        in_specs=[
            SMEM, whole(target_all), whole(gain),
            pair_cols(width), pair_cols(width, pairs), pair_cols(width, 2 * pairs),
            windows_spec(windows), whole(qseg), whole(kseg),
        ],
        out_specs=[
            pair_cols(rows), pair_cols(rows), pair_cols(length), pair_cols(length),
            whole(target_all),
        ],
        out_shape=[
            shape_of(rows, inner), shape_of(rows, inner), shape_of(length, inner),
            shape_of(length, inner), shape_of(length, width),
        ],
        compiler_params=PARAMS,
        cost_estimate=cost(16),
        name="self_forward",
    )(place, target_all, gain, weights, weights, weights, windows, qseg, kseg)


def self_back(place, target_all, grad, query, key, value, weights, windows, qseg, kseg):
    (length, width), (rows, inner) = target_all.shape, query.shape
    pairs = inner // LANES

    def body(
        pos_ref, rows_ref, do_ref, q_ref, k_ref, v_ref, wq_ref, wk_ref, wv_ref, win_ref,
        qseg_ref, kseg_ref, dq_ref, dk_ref, dv_ref, dwin_ref, back_ref, dgain_ref,
    ):
        step = pl.program_id(0)
        position = pl.multiple_of(pos_ref[0], LANES)
        own = pl.ds(position, rows)
        allowed = allowed_pairs(position, qseg_ref[...], kseg_ref[...], True)
        dq, dk, dv = attend_pair_back(
            q_ref[...], k_ref[...], v_ref[...], do_ref[...], win_ref, dwin_ref, allowed, True
        )
        dq_ref[...] = jnp.zeros_like(dq_ref)
        dq_ref[own, :] = dq
        dk_ref[...], dv_ref[...] = dk, dv
        back = mm(dk, wk_ref[...], NT) + mm(dv, wv_ref[...], NT)

        @pl.when(step == 0)
        def _():
            back_ref[...] = back

        @pl.when(step > 0)
        def _():
            back_ref[...] += back

        back_ref[own, :] += mm(dq, wq_ref[...], NT)

        @pl.when(step == pairs - 1)
        def _():
            values = rows_ref[...].astype(F32)
            dgain_ref[...] = jnp.sum(
                values * scale_of(values) * back_ref[...], axis=0, keepdims=True
            )

    return pl.pallas_call(
        body,
        grid=(pairs,),
        in_specs=[
            SMEM, whole(target_all), pair_cols(rows),
            pair_cols(rows), pair_cols(length), pair_cols(length),
            pair_cols(width), pair_cols(width, pairs), pair_cols(width, 2 * pairs),
            windows_spec(windows), whole(qseg), whole(kseg),
        ],
        out_specs=[
            pair_cols(length), pair_cols(length), pair_cols(length), windows_spec(windows),
            whole(target_all), pl.BlockSpec((1, width), lambda step: (0, 0)),
        ],
        out_shape=[
            shape_of(length, inner), shape_of(length, inner), shape_of(length, inner),
            shape_of(*windows.shape, dtype=F32), shape_of(length, width, dtype=F32),
            shape_of(1, width, dtype=F32),
        ],
        compiler_params=PARAMS,
        cost_estimate=cost(23),
        name="self_back",
    )(place, target_all, grad, query, key, value, weights, weights, weights, windows, qseg, kseg)


def cross_forward(target, attended, memory_all, gain_cross, gain_ffn, weights, qseg, mseg):
    (rows, width), inner, enc = target.shape, attended.shape[1], memory_all.shape[0]
    pairs = inner // LANES

    def body(
        rows_ref, att_ref, mem_ref, gain_ref, gain3_ref, wo_ref, wq_ref, wk_ref, wv_ref, wc_ref,
        qseg_ref, mseg_ref, one_ref, normed_ref, q_ref, k_ref, v_ref, out_ref, two_ref, last_ref,
    ):
        step = pl.program_id(0)

        @pl.when(step == 0)
        def _():
            hidden = rows_ref[...].astype(F32) + mm(att_ref[...], wo_ref[...])
            one_ref[...] = hidden
            two_ref[...] = hidden
            normed_ref[...] = (hidden * scale_of(hidden) * gain_ref[...]).astype(BF)

        query = mm(normed_ref[...], wq_ref[...]).astype(BF)
        key = mm(mem_ref[...], wk_ref[...]).astype(BF)
        value = mm(mem_ref[...], wv_ref[...]).astype(BF)
        q_ref[...], k_ref[...], v_ref[...] = query, key, value
        allowed = allowed_pairs(0, qseg_ref[...], mseg_ref[...], False)
        out = attend_pair(query, key, value, None, allowed, False)
        out_ref[...] = out
        two_ref[...] += mm(out, wc_ref[...])

        @pl.when(step == pairs - 1)
        def _():
            hidden = two_ref[...]
            last_ref[...] = (hidden * scale_of(hidden) * gain3_ref[...]).astype(BF)

    return pl.pallas_call(
        body,
        grid=(pairs,),
        in_specs=[
            whole(target), whole(attended), whole(memory_all), whole(gain_cross), whole(gain_ffn),
            pl.BlockSpec((width, width), lambda step: (0, 0)),
            pair_cols(width, pairs), pair_cols(width, 2 * pairs), pair_cols(width, 3 * pairs),
            pl.BlockSpec((LANES, width), lambda step: (step, 4)),
            whole(qseg), whole(mseg),
        ],
        out_specs=[
            whole(target), whole(target), pair_cols(rows), pair_cols(enc), pair_cols(enc),
            pair_cols(rows), whole(target), whole(target),
        ],
        out_shape=[
            shape_of(rows, width, dtype=F32), shape_of(rows, width), shape_of(rows, inner),
            shape_of(enc, inner), shape_of(enc, inner), shape_of(rows, inner),
            shape_of(rows, width, dtype=F32), shape_of(rows, width),
        ],
        compiler_params=PARAMS,
        cost_estimate=cost(12),
        name="cross_forward",
    )(
        target, attended, memory_all, gain_cross, gain_ffn, weights, weights, weights, weights,
        weights, qseg, mseg,
    )


def cross_back(grad_two, hidden_one, gain, query, key, value, weights, qseg, mseg):
    (rows, width), inner, enc = hidden_one.shape, query.shape[1], key.shape[0]
    pairs = inner // LANES

    def body(
        grad_ref, one_ref, gain_ref, q_ref, k_ref, v_ref, wo_ref, wq_ref, wk_ref, wv_ref, wc_ref,
        qseg_ref, mseg_ref, dq_ref, dk_ref, dv_ref, mem_ref, done_ref, low_ref, datt_ref,
        dgain_ref, two_ref, back_ref,
    ):
        step = pl.program_id(0)

        @pl.when(step == 0)
        def _():
            two_ref[...] = grad_ref[...].astype(BF)

        grad = mm(two_ref[...], wc_ref[...], NT).astype(BF)
        allowed = allowed_pairs(0, qseg_ref[...], mseg_ref[...], False)
        dq, dk, dv = attend_pair_back(
            q_ref[...], k_ref[...], v_ref[...], grad, None, None, allowed, False
        )
        dq_ref[...], dk_ref[...], dv_ref[...] = dq, dk, dv
        back = mm(dq, wq_ref[...], NT)
        memory = mm(dk, wk_ref[...], NT) + mm(dv, wv_ref[...], NT)

        @pl.when(step == 0)
        def _():
            back_ref[...] = back
            mem_ref[...] = memory

        @pl.when(step > 0)
        def _():
            back_ref[...] += back
            mem_ref[...] += memory

        @pl.when(step == pairs - 1)
        def _():
            through, grad_gain = norm_back(one_ref[...], gain_ref[...], back_ref[...])
            grad_one = grad_ref[...] + through
            low = grad_one.astype(BF)
            done_ref[...] = grad_one
            low_ref[...] = low
            dgain_ref[...] = grad_gain
            datt_ref[...] = mm(low, wo_ref[...], NT).astype(BF)

    row = pl.BlockSpec((1, width), lambda step: (0, 0))
    return pl.pallas_call(
        body,
        grid=(pairs,),
        in_specs=[
            whole(grad_two), whole(hidden_one), row,
            pair_cols(rows), pair_cols(enc), pair_cols(enc),
            pl.BlockSpec((width, width), lambda step: (0, 0)),
            pair_cols(width, pairs), pair_cols(width, 2 * pairs), pair_cols(width, 3 * pairs),
            pl.BlockSpec((LANES, width), lambda step: (step, 4)),
            whole(qseg), whole(mseg),
        ],
        out_specs=[
            pair_cols(rows), pair_cols(enc), pair_cols(enc),
            pl.BlockSpec((enc, width), lambda step: (0, 0)),
            whole(hidden_one), whole(hidden_one), whole(hidden_one), row,
        ],
        out_shape=[
            shape_of(rows, inner), shape_of(enc, inner), shape_of(enc, inner),
            shape_of(enc, width, dtype=F32), shape_of(rows, width, dtype=F32),
            shape_of(rows, width), shape_of(rows, inner), shape_of(1, width, dtype=F32),
        ],
        scratch_shapes=[pltpu.VMEM((rows, width), BF), pltpu.VMEM((rows, width), F32)],
        compiler_params=PARAMS,
        cost_estimate=cost(18),
        name="cross_back",
    )(
        grad_two, hidden_one, gain, query, key, value, weights, weights, weights, weights, weights,
        qseg, mseg,
    )


def gather_all(shard):
    return lax.all_gather(shard, AXES, axis=0, tiled=True)


def scatter_all(grads):
    return lax.psum_scatter(grads, AXES, scatter_dimension=0, tiled=True).astype(F32)


class Links:
    def __init__(self):
        self.batch, self.seq = lax.axis_size("batch"), lax.axis_size("seq")
        self.depth = self.batch // 2
        z_x, y_c = lax.axis_index("batch"), lax.axis_index("seq")
        self.z, self.x = z_x // 2, z_x % 2
        self.y, self.core = y_c // 2, y_c % 2
        self.lead = self.core == 0
        self.place = jnp.stack([self.z, self.x, self.y, self.core]).astype(jnp.int32)

    def move(self, value, target):
        pairs = []
        for source in range(self.batch * self.seq):
            z_x, y_c = source // self.seq, source % self.seq
            z, x, y, core = target(z_x // 2, z_x % 2, y_c // 2, y_c % 2)
            pairs.append((source, (z * 2 + x) * self.seq + y * 2 + core))
        return lax.ppermute(value, AXES, pairs)

    def over_core(self, value):
        return self.move(value, lambda z, x, y, core: (z, x, y, 1 - core))

    def over_y(self, value):
        return self.move(value, lambda z, x, y, core: (z, x, 1 - y, core))

    def over_near(self, value):
        return self.move(
            value, lambda z, x, y, c: (z, x, 1 - y, c) if c else (z, 1 - x, y, c)
        )

    def over_far(self, value):
        return self.move(
            value, lambda z, x, y, c: (z, 1 - x, y, c) if c else (z, x, 1 - y, c)
        )

    def over_z(self, value, step):
        depth = self.depth
        return self.move(value, lambda z, x, y, core: ((z - step) % depth, x, y, core))


def in_order(first, own, other):
    return jnp.concatenate([jnp.where(first, own, other), jnp.where(first, other, own)], axis=0)


def gather_core(links, left, right):
    own = jnp.where(links.lead, left, right)
    other = links.over_core(jnp.where(links.lead, right, left))
    return in_order(links.lead, own, other)


def z_steps(links, value, steps):
    return [links.over_z(value, step) for step in steps]


def gather_near(links, value):
    return jnp.stack([value, links.over_near(value)])


def gather_far(links, value):
    return jnp.stack([value, links.over_far(value)])


def assemble(links, *sources):
    count, (rows, cols) = len(sources) // 2, sources[0].shape[-2:]
    depth = links.depth

    def body(place_ref, *refs):
        inputs, out_ref, sem = refs[:-2], refs[-2], refs[-1]
        z, x, y, core = [place_ref[i] for i in range(4)]
        for which, source in enumerate(inputs):
            half = core if which < count else 1 - core
            for near, far, step in np.ndindex(2, 2, depth):
                if count == 2 and far != which % 2:
                    continue
                step_x, step_y = jnp.where(half == 0, near, far), jnp.where(half == 0, far, near)
                chip = (((z + step) % depth) * 2 + (x ^ step_x)) * 2 + (y ^ step_y)
                target = out_ref.at[
                    pl.ds(pl.multiple_of(chip * rows, 16), rows),
                    pl.ds(pl.multiple_of(half * cols, LANES), cols),
                ]
                part = source.at[near, step] if count == 2 else source.at[step, far, near]
                pltpu.make_async_copy(part, target, sem).start()
        pltpu.make_async_copy(out_ref, out_ref, sem).wait()

    return pl.pallas_call(
        body,
        in_specs=[pl.BlockSpec(memory_space=pltpu.SMEM)]
        + [pl.BlockSpec(memory_space=pl.ANY)] * len(sources),
        out_specs=pl.BlockSpec(memory_space=pltpu.VMEM),
        out_shape=jax.ShapeDtypeStruct((depth * 4 * rows, 2 * cols), sources[0].dtype),
        scratch_shapes=[pltpu.SemaphoreType.DMA(())],
        compiler_params=pltpu.CompilerParams(vmem_limit_bytes=48 << 20),
        cost_estimate=cost(6),
        name="assemble",
    )(links.place, *sources)


def weight_grad(links, core, terms, extra=None, z_first=False):
    depth, total_rows = links.depth, terms[0][0].shape[1]
    rows = total_rows // (depth * 4)
    widths = [term[1].shape[1] for term in terms]
    extra_width = 0 if extra is None else extra.shape[1]
    total = sum(widths) + extra_width
    tile = 1408 if total % 1408 == 0 else 512

    def body(place_ref, *refs):
        inputs, out_ref, stage, sems = refs[:-3], refs[-3], refs[-2], refs[-1]
        z, x, y, left = place_ref[0], place_ref[1], place_ref[2], place_ref[3] == 0
        places = []
        for chip in range(depth * 4):
            step_x, step_y = (chip // 2 % 2) ^ x, (chip % 2) ^ y
            near, far = jnp.where(left, step_x, step_y), jnp.where(left, step_y, step_x)
            step = (chip // 4 - z) % depth
            spot = (step * 2 + far) * 2 + near if z_first else (near * 2 + far) * depth + step
            places.append(pl.multiple_of(spot * rows, 8))
        copies, start = [], 0

        def emit(start, value, width):
            for chip, spot in enumerate(places):
                stage[pl.ds(spot, rows), start : start + width] = value[
                    chip * rows : (chip + 1) * rows
                ].astype(BF)
            copies.append(
                pltpu.make_async_copy(
                    stage.at[:, pl.ds(start, width)],
                    out_ref.at[:, pl.ds(start, width)],
                    sems.at[len(copies)],
                )
            )
            copies[-1].start()

        for index, width in enumerate(widths):
            acts_l, grad_l, acts_r, grad_r = inputs[4 * index : 4 * index + 4]
            acts = jnp.where(left, acts_l[...], acts_r[...])
            for offset in range(0, width, tile):
                cols = slice(offset, offset + tile)
                grad = jnp.where(left, grad_l[:, cols], grad_r[:, cols])
                emit(start, mm(acts, grad, TN), tile)
                start += tile
        if extra is not None:
            small = inputs[-1][...]
            emit(start, jnp.where(left, small, jnp.zeros_like(small)), extra_width)
        for copy in copies:
            copy.wait()

    place = links.place.at[3].set(core)
    operands = [array for term in terms for array in term] + ([] if extra is None else [extra])
    count = sum(width // tile for width in widths) + (extra is not None)
    vmem = pl.BlockSpec(memory_space=pltpu.VMEM)
    return pl.pallas_call(
        body,
        in_specs=[pl.BlockSpec(memory_space=pltpu.SMEM)] + [vmem] * len(operands),
        out_specs=pl.BlockSpec(memory_space=pl.ANY),
        out_shape=jax.ShapeDtypeStruct((total_rows, total), BF),
        scratch_shapes=[pltpu.VMEM((total_rows, total), BF), pltpu.SemaphoreType.DMA((count,))],
        compiler_params=pltpu.CompilerParams(vmem_limit_bytes=48 << 20),
        cost_estimate=cost(4),
        name="weight_grad",
    )(place, *operands)


def add_low(one, other):
    return (one.astype(F32) + other.astype(F32)).astype(BF)


class Scatter:
    def __init__(self, links):
        self.links, self.parts = links, []

    def core(self, sent):
        self.rows = sent.shape[0]
        self.parts.append(self.links.over_core(sent))

    def keep(self, kept):
        self.parts.append(kept)

    def total(self, start, count):
        return sum(part[start : start + count].astype(F32) for part in self.parts)

    def halve(self):
        self.rows //= 2
        return self.total(self.rows, self.rows).astype(BF)

    def near(self, send):
        self.parts.append(self.links.over_near(send))

    def far(self, send):
        self.parts.append(self.links.over_far(send))

    def z_sends(self):
        self.rows //= self.links.depth
        return [
            self.total(step * self.rows, self.rows).astype(BF)
            for step in range(1, self.links.depth)
        ]

    def z(self, sends):
        depth = self.links.depth
        for step, send in enumerate(sends, 1):
            self.parts.append(self.links.over_z(send, depth - step))

    def z_start(self, sends):
        links, depth = self.links, self.links.depth
        return links.over_z(sends[-1], 1), links.over_z(sends[-2], depth - 1)

    def z_end(self, sends, back, ahead):
        self.parts.append(back)
        for send in sends[-3::-1]:
            ahead = self.links.over_z(add_low(ahead, send), self.links.depth - 1)
        self.parts.append(ahead)

    def own(self):
        return self.total(0, self.rows)

    def last(self, total):
        links, half = self.links, self.rows // 2
        above, below = total[:half], total[half:]
        own = jnp.where(links.lead, above, below)
        other = links.over_core(jnp.where(links.lead, below, above))
        return jnp.where(links.lead, own, other), jnp.where(links.lead, other, own)


class SeqScatter:
    def __init__(self, links, parts):
        self.links = links
        parts = parts.reshape(2, 2, -1, parts.shape[1])
        take = lambda core: lax.dynamic_index_in_dim(parts, core, 1, False)
        self.kept = take(links.core)
        self.sent = links.over_core(take(1 - links.core).astype(BF))

    def second(self):
        total = self.kept + self.sent.astype(F32)
        take = lambda y: lax.dynamic_index_in_dim(total, y, 0, False)
        self.kept = take(self.links.y)
        self.sent = self.links.over_y(take(1 - self.links.y).astype(BF))

    def total(self):
        return self.kept + self.sent.astype(F32)


class PlainScatter:
    parts = ()

    def core(self, sent):
        self.sent = sent

    def keep(self, kept):
        self.kept = kept

    def halve(self):
        return self.sent

    def near(self, send):
        self.sent = send

    def z_start(self, sends):
        return sends, None

    def z_end(self, sends, back, ahead):
        self.sent = back

    far = near
    z_sends = own = halve

    def last(self, total):
        return jnp.split(scatter_all(self.kept), 2, axis=1)


def phase(*values):
    return lax.optimization_barrier(values)


def per_device(
    target, memory, cotangent, target_segments, memory_segments, bucket_ids,
    self_norm_gain, self_query, self_key, self_value, self_output, bias_table,
    cross_norm_gain, cross_query, cross_key, cross_value, cross_output,
    ffn_norm_gain, ffn_gate, ffn_up, ffn_down,
):
    batch_size, seq_size = lax.axis_size("batch"), lax.axis_size("seq")
    devices = batch_size * seq_size
    seq_index = lax.axis_index("seq")
    rows, width = target.shape[1], target.shape[2]
    length, enc = target_segments.shape[1], memory_segments.shape[1]
    enc_rows = memory.shape[1]
    inner = self_query.shape[1]
    hidden = ffn_gate.shape[1]
    table_rows, table_cols = bias_table.shape
    weight_rows = self_query.shape[0]
    table_size = table_rows * table_cols

    links = Links()
    core, lead, depth = links.core, links.lead, links.depth
    small = jnp.concatenate(
        [self_norm_gain, cross_norm_gain, ffn_norm_gain, bias_table.reshape(-1)]
    )
    small = jnp.pad(small[None], ((0, weight_rows - 1), (0, 2 * LANES - small.shape[0])))
    part = hidden // 2
    groups = [
        [self_query, self_key, self_value, small],
        [self_output, cross_query, cross_key, cross_value, cross_output],
        [ffn_gate[:, :part], ffn_up[:, :part]],
        [ffn_gate[:, part:], ffn_up[:, part:]],
    ]
    groups = [jnp.concatenate(group, axis=1) for group in groups]
    cuts = [group.shape[1] // 2 for group in groups]
    left = jnp.concatenate([group[:, :cut] for group, cut in zip(groups, cuts)], axis=1)
    right = jnp.concatenate([group[:, cut:] for group, cut in zip(groups, cuts)], axis=1)
    down_cut = width // 2
    steps = list(range(1, depth))
    some, rest = steps[:1], steps[1:]
    z_one, z_two, z_three = steps[:1], steps[-1:] if depth > 2 else [], steps[1:-1]
    direct = 2 * ffn_down.shape[0] % 16 == 0
    move = lambda function, *args: function(links, *args) if direct else None

    moved = gather_core(links, left, right)
    down = move(gather_core, ffn_down[:, :down_cut], ffn_down[:, down_cut:])
    if not direct:
        down_whole = gather_all(ffn_down)
    moved, down = phase(moved, down)
    ends = list(np.cumsum(cuts))
    first0, second0, third0, fourth0 = jnp.split(moved, ends[:-1], axis=1)

    position = seq_index * rows
    heads = seq_size * table_cols
    distance = position + rows - jnp.arange(rows + length, dtype=jnp.int32)
    near = (distance >= 0) & (distance < length)
    bucket = jnp.take(bucket_ids, jnp.clip(distance, 0, length - 1))
    bucket_range = jnp.arange(batch_size * table_rows, dtype=jnp.int32)
    onehot = ((bucket[:, None] == bucket_range[None, :]) & near[:, None]).astype(BF)

    first_z = jnp.stack([first0] + z_steps(links, first0, steps))
    down = move(gather_near, down)
    first_z, second0, down = phase(first_z, second0, down)

    first_near = gather_near(links, first_z)
    down = move(gather_far, down)
    second_z = z_steps(links, second0, some)
    rows_own = jnp.concatenate([target[0], memory[0]], axis=0)
    rows_other = links.over_y(rows_own)
    first_near, down, second_z, second0, onehot, rows_own, rows_other = phase(
        first_near, down, second_z, second0, onehot, rows_own, rows_other
    )

    first_far = links.over_far(first_near)
    first_near_other = links.over_core(first_near)
    second_z = jnp.stack([second0] + second_z + z_steps(links, second0, rest))
    rows_pair = in_order(links.y == 0, rows_own, rows_other)
    rows_other = links.over_core(rows_pair)
    first_far, first_near_other, second_z, down, third0, rows_pair, rows_other = phase(
        first_far, first_near_other, second_z, down, third0, rows_pair, rows_other
    )
    by_y = lambda both: both.reshape(2, 1, rows + enc_rows, width)
    both = jnp.concatenate(
        [
            jnp.where(lead, by_y(rows_pair), by_y(rows_other)),
            jnp.where(lead, by_y(rows_other), by_y(rows_pair)),
        ],
        axis=1,
    )
    target_all = both[:, :, :rows].reshape(length, width)
    memory_all = both[:, :, rows:].reshape(enc, width)

    second_near = gather_near(links, second_z)
    third_z = jnp.stack([third0] + z_steps(links, third0, steps))
    first_far_other = links.over_core(first_far)
    first_far_other, second_near, third_z, fourth0, down, target_all, memory_all = phase(
        first_far_other, second_near, third_z, fourth0, down, target_all, memory_all
    )

    second_far = links.over_far(second_near)
    second_near_other = links.over_core(second_near)
    third_near = gather_near(links, third_z)
    fourth_z = jnp.stack([fourth0] + z_steps(links, fourth0, steps))
    down_one = move(z_steps, down, z_one)
    down_two = move(z_steps, down, z_two)
    first = assemble(links, first_near, first_far, first_near_other, first_far_other)
    smalls = first[:, 3 * inner :].reshape(devices, weight_rows, 2 * LANES)[:, 0, :].astype(F32)
    gains = [smalls[:, i * weight_rows : (i + 1) * weight_rows].reshape(1, width) for i in range(3)]
    gain_self, gain_cross, gain_ffn = gains
    table = smalls[:, 3 * weight_rows : 3 * weight_rows + table_size]
    table = table.reshape(batch_size, seq_size, table_rows, table_cols)
    table = jnp.transpose(table, (0, 2, 1, 3)).reshape(batch_size * table_rows, seq_size * table_cols)

    windows = mm(table.astype(BF), onehot, (((0,), (1,)), ((), ())))
    windows = windows.reshape(heads // 2, 2, rows + length)
    position1 = position.reshape(1)
    qseg = lax.dynamic_slice_in_dim(target_segments, position, rows, 1).reshape(rows, 1)
    kseg, mseg = target_segments, memory_segments

    attended, queries, keys, values, normed_all = self_forward(
        position1, target_all, gain_self, first, windows, qseg, kseg
    )
    attended, second_far, second_near_other, third_near, fourth_z, down, down_one, down_two = phase(
        attended, second_far, second_near_other, third_near, fourth_z, down, down_one, down_two
    )

    third_far = links.over_far(third_near)
    third_near_other = links.over_core(third_near)
    fourth_near = links.over_near(fourth_z)
    down_three = []
    for step in z_three:
        down_three.append(links.over_z((down_one + down_three)[-1], 1) if direct else None)
    second = assemble(
        links, second_near, second_far, second_near_other, links.over_core(second_far)
    )
    (
        hidden_one, normed_two, cross_queries, cross_keys, cross_values, cross_attended,
        hidden_two, normed_three,
    ) = cross_forward(
        target[0], attended, memory_all, gain_cross, gain_ffn, second, qseg, mseg
    )
    normed_three, third_far, third_near_other, fourth_z, fourth_near = phase(
        normed_three, third_far, third_near_other, fourth_z, fourth_near
    )
    down, down_one, down_two, down_three, normed_three = phase(
        down, down_one, down_two, down_three, normed_three
    )

    fourth_near = jnp.stack([fourth_z, fourth_near])
    fourth_far = links.over_far(fourth_near)
    fourth_near_other = links.over_core(fourth_near)
    if direct:
        down = jnp.stack([down] + down_one + down_three + down_two)
    down_other = links.over_core(down) if direct else None
    third = assemble(links, third_near, third_far, third_near_other, links.over_core(third_far))
    third_gate_up = mm(normed_three, third)
    if direct:
        w_down = assemble(links, down, down_other)
    else:
        w_down = down_whole
    third_gate_up, fourth_far, fourth_near_other, w_down = phase(
        third_gate_up, fourth_far, fourth_near_other, w_down
    )

    fourth_far_other = links.over_core(fourth_far)
    cot = cotangent[0]

    def gated(gate_up, start):
        inner_act, pull = jax.vjp(gated_unit, gate_up[:, :part], gate_up[:, part:])
        grad_gate, grad_up = pull(mm(cot, w_down[start : start + part], NT))
        return inner_act.astype(BF), grad_gate.astype(BF), grad_up.astype(BF)

    inner_a, gate_a, up_a = gated(third_gate_up, 0)
    third_sum, fourth_sum = Scatter(links), Scatter(links)
    third_terms = [(normed_three, gate_a, normed_three, up_a)]
    third_send = weight_grad(links, 1 - core, third_terms)
    third_send, gate_a, up_a, fourth_far_other, w_down = phase(
        third_send, gate_a, up_a, fourth_far_other, w_down
    )

    third_sum.core(third_send)
    fourth = assemble(links, fourth_near, fourth_far, fourth_near_other, fourth_far_other)
    third_sum.keep(weight_grad(links, core, third_terms))
    third_send = third_sum.halve()
    third_send, fourth = phase(third_send, fourth)

    third_sum.near(third_send)
    inner_b, gate_b, up_b = gated(mm(normed_three, fourth), part)
    fourth_terms = [(normed_three, gate_b, normed_three, up_b)]
    fourth_sum.core(weight_grad(links, 1 - core, fourth_terms))
    inner_low = jnp.concatenate([inner_a, inner_b], axis=1)
    down_terms = [(inner_low, cot[:, :down_cut], inner_low, cot[:, down_cut:])]
    down_sum = Scatter(links) if direct else PlainScatter()
    if direct:
        down_sum.core(weight_grad(links, 1 - core, down_terms, z_first=True))
        down_sum.keep(weight_grad(links, core, down_terms, z_first=True))
    else:
        down_sum.core(inner_low)
        down_sum.keep(mm(inner_low, cot, TN).astype(BF))
    grad_normed_three = mm(jnp.concatenate([gate_a, up_a], axis=1), third, NT) + mm(
        jnp.concatenate([gate_b, up_b], axis=1), fourth, NT
    )
    through, grad_gain_ffn = norm_back(hidden_two, gain_ffn, grad_normed_three)
    grad_hidden_two = cot.astype(F32) + through
    fourth_sum.keep(weight_grad(links, core, fourth_terms))
    third_sum.parts, fourth_sum.parts, down_sum.parts, grad_hidden_two = phase(
        third_sum.parts, fourth_sum.parts, down_sum.parts, grad_hidden_two
    )

    third_sum.far(third_sum.halve())
    fourth_sum.near(fourth_sum.halve())
    down_sends = down_sum.z_sends()
    down_back, down_ahead = down_sum.z_start(down_sends)
    low_two = grad_hidden_two.astype(BF)
    (
        grad_cq, grad_ck, grad_cv, memory_part, grad_hidden_one, low_one, grad_attended,
        grad_gain_cross,
    ) = cross_back(
        grad_hidden_two, hidden_one, gain_cross, cross_queries, cross_keys, cross_values, second,
        qseg, mseg,
    )
    half = inner // 2
    (
        third_sum.parts, fourth_sum.parts, down_back, down_ahead, grad_cq, grad_ck, grad_cv,
        low_one, grad_attended,
    ) = phase(
        third_sum.parts, fourth_sum.parts, down_back, down_ahead, grad_cq, grad_ck, grad_cv,
        low_one, grad_attended,
    )

    cross_terms = [
        (normed_two, grad_cq, cross_attended, low_two),
        (memory_all, grad_ck, memory_all, grad_cv),
        (attended, low_one[:, :half], attended, low_one[:, half:]),
    ]
    cross_sum = Scatter(links)
    cross_sum.core(weight_grad(links, 1 - core, cross_terms))
    fourth_sum.far(fourth_sum.halve())
    third_sum.z(third_sum.z_sends())
    cross_sum.keep(weight_grad(links, core, cross_terms))
    cross_sum.parts, fourth_sum.parts, grad_attended = phase(
        cross_sum.parts, fourth_sum.parts, grad_attended
    )

    cross_sum.near(cross_sum.halve())
    down_sum.z_end(down_sends, down_back, down_ahead)
    grad_q, grad_k, grad_v, grad_windows, grad_normed, grad_gain_self = self_back(
        position1, target_all, grad_attended, queries, keys, values, first, windows, qseg, kseg
    )
    (
        cross_sum.parts, third_sum.parts, down_sum.parts, grad_q, grad_k, grad_v, grad_windows,
        grad_normed, grad_gain_self, memory_part,
    ) = phase(
        cross_sum.parts, third_sum.parts, down_sum.parts, grad_q, grad_k, grad_v, grad_windows,
        grad_normed, grad_gain_self, memory_part,
    )

    cross_sum.far(cross_sum.halve())
    grad_windows = grad_windows.reshape(heads, rows + length)
    grad_table = lax.dot_general(
        onehot.astype(F32), grad_windows, (((0,), (1,)), ((), ())), precision=lax.Precision.HIGHEST
    )
    grad_table = grad_table.reshape(batch_size, table_rows, seq_size, table_cols)
    grad_table = jnp.transpose(grad_table, (0, 2, 1, 3)).reshape(devices, table_size)
    gain_parts = [g.reshape(devices, weight_rows) for g in (grad_gain_self, grad_gain_cross, grad_gain_ffn)]
    small_grad = jnp.concatenate(gain_parts + [grad_table], axis=1)
    small_grad = jnp.pad(
        small_grad[:, None], ((0, 0), (0, weight_rows - 1), (0, LANES - small_grad.shape[1]))
    ).reshape(devices * weight_rows, LANES)
    cut = inner + half
    self_terms = [
        (normed_all, grad_q, normed_all, grad_v),
        (normed_all, grad_k[:, :half], normed_all, grad_k[:, half:]),
    ]
    self_sum = Scatter(links)
    self_sum.core(weight_grad(links, 1 - core, self_terms, small_grad))
    self_sum.keep(weight_grad(links, core, self_terms, small_grad))
    fourth_sum.z(fourth_sum.z_sends())
    self_sum.parts, cross_sum.parts = phase(self_sum.parts, cross_sum.parts)

    self_sum.near(self_sum.halve())
    cross_sends = cross_sum.z_sends()
    cross_back_z, cross_ahead_z = cross_sum.z_start(cross_sends)
    down_sum.far(down_sum.halve())
    normed_rows = SeqScatter(links, grad_normed)
    activations = (hidden_two + mm(inner_low, w_down)).astype(BF)
    (
        self_sum.parts, cross_back_z, cross_ahead_z, down_sum.parts, fourth_sum.parts,
        normed_rows.sent,
    ) = phase(
        self_sum.parts, cross_back_z, cross_ahead_z, down_sum.parts, fourth_sum.parts,
        normed_rows.sent,
    )

    self_sum.far(self_sum.halve())
    cross_sum.z_end(cross_sends, cross_back_z, cross_ahead_z)
    down_sum.near(down_sum.halve())
    normed_rows.second()
    gate_one, up_one = third_sum.last(third_sum.own())
    memory_rows = SeqScatter(links, memory_part)
    self_sum.parts, down_sum.parts, cross_sum.parts, normed_rows.sent, memory_rows.sent = phase(
        self_sum.parts, down_sum.parts, cross_sum.parts, normed_rows.sent, memory_rows.sent
    )

    self_sum.z(self_sum.z_sends())
    memory_rows.second()
    memory_grad = memory_rows.total()
    down_out = jnp.concatenate(down_sum.last(down_sum.own()), axis=1)
    cross_left, cross_right = cross_sum.last(cross_sum.own())
    gate_two, up_two = fourth_sum.last(fourth_sum.own())
    through, _ = norm_back(target[0].astype(F32), gain_self, normed_rows.total())
    target_grad = grad_hidden_one + through
    self_left, self_right = self_sum.last(self_sum.own())
    join = lambda left, right: jnp.concatenate([left, right], axis=1)

    small_out = self_left[0, cut:]
    gain_out = [small_out[i * weight_rows : (i + 1) * weight_rows] for i in range(3)]
    table_out = small_out[3 * weight_rows : 3 * weight_rows + table_size]
    return (
        activations[None],
        target_grad[None],
        memory_grad[None],
        gain_out[0],
        self_left[:, :inner],
        join(self_left[:, inner:cut], self_right[:, inner:cut]),
        self_right[:, :inner],
        join(cross_left[:, 2 * inner :], cross_right[:, 2 * inner :]),
        table_out.reshape(table_rows, table_cols),
        gain_out[1],
        cross_left[:, :inner],
        cross_left[:, inner : 2 * inner],
        cross_right[:, inner : 2 * inner],
        cross_right[:, :inner],
        gain_out[2],
        jnp.concatenate([gate_one, gate_two], axis=1),
        jnp.concatenate([up_one, up_two], axis=1),
        down_out,
    )


def solution(mesh):
    rows3 = P("batch", "seq", None)
    seg = P("batch", None)
    gain = P(AXES)
    weight = P(AXES, None)
    table = P("batch", "seq")
    return jax.shard_map(
        per_device,
        mesh=mesh,
        in_specs=(
            rows3, rows3, rows3, seg, seg, P(),
            gain, weight, weight, weight, weight, table,
            gain, weight, weight, weight, weight,
            gain, weight, weight, weight,
        ),
        out_specs=(
            rows3, rows3, rows3,
            gain, weight, weight, weight, weight, table,
            gain, weight, weight, weight, weight,
            gain, weight, weight, weight,
        ),
        check_vma=False,
    )
```

```python
import functools

import jax
import jax.numpy as jnp
import numpy as np
from jax import lax
from jax.experimental import pallas as pl
from jax.experimental.pallas import tpu as pltpu
from jax.sharding import PartitionSpec as P

HD = 64
LANES = 128
SUBLANES = 8
EPSILON = 1e-06
MASKED = -1e30
BF = jnp.bfloat16
F32 = jnp.float32
AXES = ("batch", "seq")
NT = (((1,), (1,)), ((), ()))
TN = (((0,), (0,)), ((), ()))
NN = (((1,), (0,)), ((), ()))


def mm(left, right, dims=NN):
    return lax.dot_general(left, right, dims, preferred_element_type=F32)


def gated_unit(gate_act, up_act):
    return jax.nn.gelu(gate_act, approximate=True) * up_act


def head_only(pair, head):
    lane = lax.broadcasted_iota(jnp.int32, pair.shape, 1)
    return jnp.where((lane // HD) == head, pair, jnp.zeros_like(pair))


def pick_heads(first, second):
    lane = lax.broadcasted_iota(jnp.int32, first.shape, 1)
    return jnp.where(lane < HD, first, second)


def spread(window, rows):
    wide = jnp.broadcast_to(window, (rows, window.shape[1]))
    rolled = pltpu.roll(wide, 0, 1, stride=1, stride_axis=0)
    return rolled[:, rows:]


def unspread(grads, rows):
    wide = jnp.concatenate([jnp.zeros((rows, rows), F32), grads], axis=1)
    width = wide.shape[1]
    total = wide[:SUBLANES]
    for start in range(SUBLANES, rows, SUBLANES):
        total = total + pltpu.roll(wide[start : start + SUBLANES], width - start, 1)
    row = lax.broadcasted_iota(jnp.int32, total.shape, 0)
    for bit in (1, 2, 4):
        total = jnp.where((row & bit) != 0, pltpu.roll(total, width - bit, 1), total)
    return jnp.sum(total, axis=0, keepdims=True)


def allowed_pairs(position, query_segments, key_segments, causal):
    rows, keys = query_segments.shape[0], key_segments.shape[1]
    allowed = query_segments == key_segments
    if causal:
        own = lax.broadcasted_iota(jnp.int32, (rows, keys), 0) + position
        other = lax.broadcasted_iota(jnp.int32, (rows, keys), 1)
        allowed = allowed & (own >= other)
    return allowed


def pair_probs(query, key, bias_ref, allowed, head, causal):
    scores = mm(head_only(query, head), key, NT)
    if causal:
        scores = scores + spread(bias_ref[0, head : head + 1, :], query.shape[0])
    scores = jnp.where(allowed, scores, MASKED)
    top = jnp.max(scores, axis=1, keepdims=True)
    grown = jnp.exp(scores - top)
    return grown / jnp.sum(grown, axis=1, keepdims=True)


def attend_pair(query, key, value, bias_ref, allowed, causal):
    parts = []
    for head in range(2):
        probs = pair_probs(query, key, bias_ref, allowed, head, causal)
        parts.append(mm(probs.astype(BF), value))
    return pick_heads(*parts).astype(BF)


def attend_pair_back(query, key, value, grad, bias_ref, dbias_ref, allowed, causal):
    grad_query, grad_key, grad_value = [], 0.0, 0.0
    for head in range(2):
        probs = pair_probs(query, key, bias_ref, allowed, head, causal)
        grad_head = head_only(grad, head)
        grad_probs = mm(grad_head, value, NT)
        inner = jnp.sum(probs * grad_probs, axis=1, keepdims=True)
        grad_scores = probs * (grad_probs - inner)
        low_scores = grad_scores.astype(BF)
        grad_query.append(mm(low_scores, key))
        grad_key = grad_key + mm(low_scores, head_only(query, head), TN)
        grad_value = grad_value + mm(probs.astype(BF), grad_head, TN)
        if causal:
            dbias_ref[0, head : head + 1, :] = unspread(grad_scores, query.shape[0])
    return pick_heads(*grad_query).astype(BF), grad_key.astype(BF), grad_value.astype(BF)


def scale_of(values):
    return lax.rsqrt(jnp.mean(values * values, axis=-1, keepdims=True) + EPSILON)


def norm_back(values, gain, grad_out):
    scale = scale_of(values)
    unit = values * scale
    lean = jnp.mean(grad_out * gain * unit, axis=-1, keepdims=True)
    grad_gain = jnp.sum(grad_out * unit, axis=0, keepdims=True)
    return scale * (grad_out * gain - unit * lean), grad_gain


def cost(microseconds):
    return pl.CostEstimate(flops=microseconds * 10**9, bytes_accessed=1, transcendentals=0)


PARAMS = pltpu.CompilerParams(dimension_semantics=("arbitrary",), vmem_limit_bytes=48 << 20)
SMEM = pl.BlockSpec(memory_space=pltpu.SMEM)


def whole(array, rows=None):
    shape = array.shape if rows is None else (rows, array.shape[1])
    return pl.BlockSpec(shape, lambda step: (0,) * len(shape))


def pair_cols(rows, offset=0):
    return pl.BlockSpec((rows, LANES), lambda step: (0, offset + step))


def shape_of(*shape, dtype=BF):
    return jax.ShapeDtypeStruct(shape, dtype)


def windows_spec(windows):
    return pl.BlockSpec((1, 2, windows.shape[2]), lambda step: (step, 0, 0))


def self_forward(place, target_all, gain, weights, windows, qseg, kseg):
    (length, width), rows = target_all.shape, qseg.shape[0]
    inner = windows.shape[0] * LANES
    pairs = inner // LANES

    def body(
        pos_ref, rows_ref, gain_ref, wq_ref, wk_ref, wv_ref, win_ref, qseg_ref, kseg_ref,
        out_ref, q_ref, k_ref, v_ref, normed_ref,
    ):
        position = pl.multiple_of(pos_ref[0], LANES)

        @pl.when(pl.program_id(0) == 0)
        def _():
            values = rows_ref[...].astype(F32)
            normed_ref[...] = (values * scale_of(values) * gain_ref[...]).astype(BF)

        normed = normed_ref[...]
        query = mm(normed_ref[pl.ds(position, rows), :], wq_ref[...]).astype(BF)
        key = mm(normed, wk_ref[...]).astype(BF)
        value = mm(normed, wv_ref[...]).astype(BF)
        q_ref[...], k_ref[...], v_ref[...] = query, key, value
        allowed = allowed_pairs(position, qseg_ref[...], kseg_ref[...], True)
        out_ref[...] = attend_pair(query, key, value, win_ref, allowed, True)

    return pl.pallas_call(
        body,
        grid=(pairs,),
        in_specs=[
            SMEM, whole(target_all), whole(gain),
            pair_cols(width), pair_cols(width, pairs), pair_cols(width, 2 * pairs),
            windows_spec(windows), whole(qseg), whole(kseg),
        ],
        out_specs=[
            pair_cols(rows), pair_cols(rows), pair_cols(length), pair_cols(length),
            whole(target_all),
        ],
        out_shape=[
            shape_of(rows, inner), shape_of(rows, inner), shape_of(length, inner),
            shape_of(length, inner), shape_of(length, width),
        ],
        compiler_params=PARAMS,
        cost_estimate=cost(16),
        name="self_forward",
    )(place, target_all, gain, weights, weights, weights, windows, qseg, kseg)


def self_back(place, target_all, grad, query, key, value, weights, windows, qseg, kseg):
    (length, width), (rows, inner) = target_all.shape, query.shape
    pairs = inner // LANES

    def body(
        pos_ref, rows_ref, do_ref, q_ref, k_ref, v_ref, wq_ref, wk_ref, wv_ref, win_ref,
        qseg_ref, kseg_ref, dq_ref, dk_ref, dv_ref, dwin_ref, back_ref, dgain_ref,
    ):
        step = pl.program_id(0)
        position = pl.multiple_of(pos_ref[0], LANES)
        own = pl.ds(position, rows)
        allowed = allowed_pairs(position, qseg_ref[...], kseg_ref[...], True)
        dq, dk, dv = attend_pair_back(
            q_ref[...], k_ref[...], v_ref[...], do_ref[...], win_ref, dwin_ref, allowed, True
        )
        dq_ref[...] = jnp.zeros_like(dq_ref)
        dq_ref[own, :] = dq
        dk_ref[...], dv_ref[...] = dk, dv
        back = mm(dk, wk_ref[...], NT) + mm(dv, wv_ref[...], NT)

        @pl.when(step == 0)
        def _():
            back_ref[...] = back

        @pl.when(step > 0)
        def _():
            back_ref[...] += back

        back_ref[own, :] += mm(dq, wq_ref[...], NT)

        @pl.when(step == pairs - 1)
        def _():
            values = rows_ref[...].astype(F32)
            dgain_ref[...] = jnp.sum(
                values * scale_of(values) * back_ref[...], axis=0, keepdims=True
            )

    return pl.pallas_call(
        body,
        grid=(pairs,),
        in_specs=[
            SMEM, whole(target_all), pair_cols(rows),
            pair_cols(rows), pair_cols(length), pair_cols(length),
            pair_cols(width), pair_cols(width, pairs), pair_cols(width, 2 * pairs),
            windows_spec(windows), whole(qseg), whole(kseg),
        ],
        out_specs=[
            pair_cols(length), pair_cols(length), pair_cols(length), windows_spec(windows),
            whole(target_all), pl.BlockSpec((1, width), lambda step: (0, 0)),
        ],
        out_shape=[
            shape_of(length, inner), shape_of(length, inner), shape_of(length, inner),
            shape_of(*windows.shape, dtype=F32), shape_of(length, width, dtype=F32),
            shape_of(1, width, dtype=F32),
        ],
        compiler_params=PARAMS,
        cost_estimate=cost(1),
        name="self_back",
    )(place, target_all, grad, query, key, value, weights, weights, weights, windows, qseg, kseg)


def cross_forward(target, attended, memory_all, gain_cross, gain_ffn, weights, qseg, mseg):
    (rows, width), inner, enc = target.shape, attended.shape[1], memory_all.shape[0]
    pairs = inner // LANES

    def body(
        rows_ref, att_ref, mem_ref, gain_ref, gain3_ref, wo_ref, wq_ref, wk_ref, wv_ref, wc_ref,
        qseg_ref, mseg_ref, one_ref, normed_ref, q_ref, k_ref, v_ref, out_ref, two_ref, last_ref,
    ):
        step = pl.program_id(0)

        @pl.when(step == 0)
        def _():
            hidden = rows_ref[...].astype(F32) + mm(att_ref[...], wo_ref[...])
            one_ref[...] = hidden
            two_ref[...] = hidden
            normed_ref[...] = (hidden * scale_of(hidden) * gain_ref[...]).astype(BF)

        query = mm(normed_ref[...], wq_ref[...]).astype(BF)
        key = mm(mem_ref[...], wk_ref[...]).astype(BF)
        value = mm(mem_ref[...], wv_ref[...]).astype(BF)
        q_ref[...], k_ref[...], v_ref[...] = query, key, value
        allowed = allowed_pairs(0, qseg_ref[...], mseg_ref[...], False)
        out = attend_pair(query, key, value, None, allowed, False)
        out_ref[...] = out
        two_ref[...] += mm(out, wc_ref[...])

        @pl.when(step == pairs - 1)
        def _():
            hidden = two_ref[...]
            last_ref[...] = (hidden * scale_of(hidden) * gain3_ref[...]).astype(BF)

    return pl.pallas_call(
        body,
        grid=(pairs,),
        in_specs=[
            whole(target), whole(attended), whole(memory_all), whole(gain_cross), whole(gain_ffn),
            pl.BlockSpec((width, width), lambda step: (0, 0)),
            pair_cols(width, pairs), pair_cols(width, 2 * pairs), pair_cols(width, 3 * pairs),
            pl.BlockSpec((LANES, width), lambda step: (step, 4)),
            whole(qseg), whole(mseg),
        ],
        out_specs=[
            whole(target), whole(target), pair_cols(rows), pair_cols(enc), pair_cols(enc),
            pair_cols(rows), whole(target), whole(target),
        ],
        out_shape=[
            shape_of(rows, width, dtype=F32), shape_of(rows, width), shape_of(rows, inner),
            shape_of(enc, inner), shape_of(enc, inner), shape_of(rows, inner),
            shape_of(rows, width, dtype=F32), shape_of(rows, width),
        ],
        compiler_params=PARAMS,
        cost_estimate=cost(12),
        name="cross_forward",
    )(
        target, attended, memory_all, gain_cross, gain_ffn, weights, weights, weights, weights,
        weights, qseg, mseg,
    )


def cross_back(grad_two, hidden_one, gain, query, key, value, weights, qseg, mseg):
    (rows, width), inner, enc = hidden_one.shape, query.shape[1], key.shape[0]
    pairs = inner // LANES

    def body(
        grad_ref, one_ref, gain_ref, q_ref, k_ref, v_ref, wo_ref, wq_ref, wk_ref, wv_ref, wc_ref,
        qseg_ref, mseg_ref, dq_ref, dk_ref, dv_ref, mem_ref, done_ref, low_ref, datt_ref,
        dgain_ref, two_ref, back_ref,
    ):
        step = pl.program_id(0)

        @pl.when(step == 0)
        def _():
            two_ref[...] = grad_ref[...].astype(BF)

        grad = mm(two_ref[...], wc_ref[...], NT).astype(BF)
        allowed = allowed_pairs(0, qseg_ref[...], mseg_ref[...], False)
        dq, dk, dv = attend_pair_back(
            q_ref[...], k_ref[...], v_ref[...], grad, None, None, allowed, False
        )
        dq_ref[...], dk_ref[...], dv_ref[...] = dq, dk, dv
        back = mm(dq, wq_ref[...], NT)
        memory = mm(dk, wk_ref[...], NT) + mm(dv, wv_ref[...], NT)

        @pl.when(step == 0)
        def _():
            back_ref[...] = back
            mem_ref[...] = memory

        @pl.when(step > 0)
        def _():
            back_ref[...] += back
            mem_ref[...] += memory

        @pl.when(step == pairs - 1)
        def _():
            through, grad_gain = norm_back(one_ref[...], gain_ref[...], back_ref[...])
            grad_one = grad_ref[...] + through
            low = grad_one.astype(BF)
            done_ref[...] = grad_one
            low_ref[...] = low
            dgain_ref[...] = grad_gain
            datt_ref[...] = mm(low, wo_ref[...], NT).astype(BF)

    row = pl.BlockSpec((1, width), lambda step: (0, 0))
    return pl.pallas_call(
        body,
        grid=(pairs,),
        in_specs=[
            whole(grad_two), whole(hidden_one), row,
            pair_cols(rows), pair_cols(enc), pair_cols(enc),
            pl.BlockSpec((width, width), lambda step: (0, 0)),
            pair_cols(width, pairs), pair_cols(width, 2 * pairs), pair_cols(width, 3 * pairs),
            pl.BlockSpec((LANES, width), lambda step: (step, 4)),
            whole(qseg), whole(mseg),
        ],
        out_specs=[
            pair_cols(rows), pair_cols(enc), pair_cols(enc),
            pl.BlockSpec((enc, width), lambda step: (0, 0)),
            whole(hidden_one), whole(hidden_one), whole(hidden_one), row,
        ],
        out_shape=[
            shape_of(rows, inner), shape_of(enc, inner), shape_of(enc, inner),
            shape_of(enc, width, dtype=F32), shape_of(rows, width, dtype=F32),
            shape_of(rows, width), shape_of(rows, inner), shape_of(1, width, dtype=F32),
        ],
        scratch_shapes=[pltpu.VMEM((rows, width), BF), pltpu.VMEM((rows, width), F32)],
        compiler_params=PARAMS,
        cost_estimate=cost(1),
        name="cross_back",
    )(
        grad_two, hidden_one, gain, query, key, value, weights, weights, weights, weights, weights,
        qseg, mseg,
    )


def gather_all(shard):
    return lax.all_gather(shard, AXES, axis=0, tiled=True)


def scatter_all(grads):
    return lax.psum_scatter(grads, AXES, scatter_dimension=0, tiled=True).astype(F32)


class Links:
    def __init__(self):
        self.batch, self.seq = lax.axis_size("batch"), lax.axis_size("seq")
        self.depth = self.batch // 2
        z_x, y_c = lax.axis_index("batch"), lax.axis_index("seq")
        self.z, self.x = z_x // 2, z_x % 2
        self.y, self.core = y_c // 2, y_c % 2
        self.lead = self.core == 0
        self.place = jnp.stack([self.z, self.x, self.y, self.core]).astype(jnp.int32)

    def move(self, value, target):
        pairs = []
        for source in range(self.batch * self.seq):
            z_x, y_c = source // self.seq, source % self.seq
            z, x, y, core = target(z_x // 2, z_x % 2, y_c // 2, y_c % 2)
            pairs.append((source, (z * 2 + x) * self.seq + y * 2 + core))
        return lax.ppermute(value, AXES, pairs)

    def over_core(self, value):
        return self.move(value, lambda z, x, y, core: (z, x, y, 1 - core))

    def over_y(self, value):
        return self.move(value, lambda z, x, y, core: (z, x, 1 - y, core))

    def over_near(self, value):
        return self.move(
            value, lambda z, x, y, c: (z, x, 1 - y, c) if c else (z, 1 - x, y, c)
        )

    def over_far(self, value):
        return self.move(
            value, lambda z, x, y, c: (z, 1 - x, y, c) if c else (z, x, 1 - y, c)
        )

    def over_z(self, value, step):
        depth = self.depth
        return self.move(value, lambda z, x, y, core: ((z - step) % depth, x, y, core))


def in_order(first, own, other):
    return jnp.concatenate([jnp.where(first, own, other), jnp.where(first, other, own)], axis=0)


def gather_core(links, left, right):
    own = jnp.where(links.lead, left, right)
    other = links.over_core(jnp.where(links.lead, right, left))
    return in_order(links.lead, own, other)


def z_steps(links, value, steps):
    return [links.over_z(value, step) for step in steps]


def gather_near(links, value):
    return jnp.stack([value, links.over_near(value)])


def gather_far(links, value):
    return jnp.stack([value, links.over_far(value)])


def assemble(links, *sources):
    count, (rows, cols) = len(sources) // 2, sources[0].shape[-2:]
    depth = links.depth

    def body(place_ref, *refs):
        inputs, out_ref, sem = refs[:-2], refs[-2], refs[-1]
        z, x, y, core = [place_ref[i] for i in range(4)]
        for which, source in enumerate(inputs):
            half = core if which < count else 1 - core
            for near, far, step in np.ndindex(2, 2, depth):
                if count == 2 and far != which % 2:
                    continue
                step_x, step_y = jnp.where(half == 0, near, far), jnp.where(half == 0, far, near)
                chip = (((z + step) % depth) * 2 + (x ^ step_x)) * 2 + (y ^ step_y)
                target = out_ref.at[
                    pl.ds(pl.multiple_of(chip * rows, 16), rows),
                    pl.ds(pl.multiple_of(half * cols, LANES), cols),
                ]
                part = source.at[near, step] if count == 2 else source.at[step, far, near]
                pltpu.make_async_copy(part, target, sem).start()
        pltpu.make_async_copy(out_ref, out_ref, sem).wait()

    return pl.pallas_call(
        body,
        in_specs=[pl.BlockSpec(memory_space=pltpu.SMEM)]
        + [pl.BlockSpec(memory_space=pl.ANY)] * len(sources),
        out_specs=pl.BlockSpec(memory_space=pltpu.VMEM),
        out_shape=jax.ShapeDtypeStruct((depth * 4 * rows, 2 * cols), sources[0].dtype),
        scratch_shapes=[pltpu.SemaphoreType.DMA(())],
        compiler_params=pltpu.CompilerParams(vmem_limit_bytes=48 << 20),
        cost_estimate=cost(6),
        name="assemble",
    )(links.place, *sources)


def weight_grad(links, terms, extra=None, z_first=False):
    depth, total_rows = links.depth, terms[0][0].shape[1]
    rows = total_rows // (depth * 4)
    widths = [term[1].shape[1] for term in terms]
    extra_width = 0 if extra is None else extra.shape[1]
    total = sum(widths) + extra_width
    tile = 1408 if total % 1408 == 0 else 512
    operands = [array for term in terms for array in term] + ([] if extra is None else [extra])
    amount = len(operands)

    def body(place_ref, *refs):
        sources, outs = refs[:amount], refs[amount : amount + 2]
        stages, sems = refs[amount + 2 : amount + 4], refs[amount + 4]
        inputs, arrived = refs[amount + 5 : -1], refs[-1]
        fetches = [
            pltpu.make_async_copy(source, target, arrived.at[index])
            for index, (source, target) in enumerate(zip(sources, inputs))
        ]
        for fetch in fetches:
            fetch.start()
        z, x, y = place_ref[0], place_ref[1], place_ref[2]

        def copy(side, index, start, width):
            cols = pl.ds(start, width)
            return pltpu.make_async_copy(
                stages[side].at[:, cols], outs[side].at[:, cols], sems.at[side, index]
            )

        for side in range(2):
            left = place_ref[3] == 1 - side
            places = []
            for chip in range(depth * 4):
                step_x, step_y = (chip // 2 % 2) ^ x, (chip % 2) ^ y
                near, far = jnp.where(left, step_x, step_y), jnp.where(left, step_y, step_x)
                step = (chip // 4 - z) % depth
                spot = (step * 2 + far) * 2 + near if z_first else (near * 2 + far) * depth + step
                places.append(pl.multiple_of(spot * rows, 8))

            def emit(index, start, value, width, side=side, places=places):
                for chip, spot in enumerate(places):
                    stages[side][pl.ds(spot, rows), pl.ds(start, width)] = value[
                        chip * rows : (chip + 1) * rows
                    ].astype(BF)
                copy(side, index, start, width).start()

            begin, first_copy = 0, 0
            for which, width in enumerate(widths):
                acts_l, grad_l, acts_r, grad_r = inputs[4 * which : 4 * which + 4]
                if side == 0:
                    for fetch in fetches[4 * which : 4 * which + 4]:
                        fetch.wait()
                acts = jnp.where(left, acts_l[...], acts_r[...])

                def one_tile(index, carry, begin=begin, first_copy=first_copy, acts=acts,
                             grad_l=grad_l, grad_r=grad_r, left=left, emit=emit):
                    offset = pl.multiple_of(index * tile, LANES)
                    cols = pl.ds(offset, tile)
                    grad = jnp.where(left, grad_l[:, cols], grad_r[:, cols])
                    start = pl.multiple_of(begin + index * tile, LANES)
                    emit(first_copy + index, start, mm(acts, grad, TN), tile)
                    return carry

                lax.fori_loop(0, width // tile, one_tile, 0)
                begin, first_copy = begin + width, first_copy + width // tile
            if extra is not None:
                if side == 0:
                    fetches[-1].wait()
                small = inputs[-1][...]
                emit(first_copy, begin, jnp.where(left, small, jnp.zeros_like(small)), extra_width)
        for side in range(2):
            for index in range(first_copy):
                copy(side, index, index * tile, tile).wait()
            if extra is not None:
                copy(side, first_copy, begin, extra_width).wait()

    count = sum(width // tile for width in widths) + (extra is not None)
    hbm = pl.BlockSpec(memory_space=pltpu.HBM)
    return pl.pallas_call(
        body,
        in_specs=[pl.BlockSpec(memory_space=pltpu.SMEM)] + [hbm] * amount,
        out_specs=[pl.BlockSpec(memory_space=pl.ANY)] * 2,
        out_shape=[jax.ShapeDtypeStruct((total_rows, total), BF)] * 2,
        scratch_shapes=[pltpu.VMEM((total_rows, total), BF)] * 2
        + [pltpu.SemaphoreType.DMA((2, count))]
        + [pltpu.VMEM(array.shape, array.dtype) for array in operands]
        + [pltpu.SemaphoreType.DMA((amount,))],
        compiler_params=pltpu.CompilerParams(vmem_limit_bytes=48 << 20),
        cost_estimate=cost(1),
        name="weight_grad",
    )(links.place, *operands)


def add_low(one, other):
    return (one.astype(F32) + other.astype(F32)).astype(BF)


class Scatter:
    def __init__(self, links):
        self.links, self.parts = links, []

    def core(self, sent):
        self.rows = sent.shape[0]
        self.parts.append(self.links.over_core(sent))

    def keep(self, kept):
        self.parts.append(kept)

    def total(self, start, count):
        return sum(part[start : start + count].astype(F32) for part in self.parts)

    def halve(self):
        self.rows //= 2
        return self.total(self.rows, self.rows).astype(BF)

    def near(self, send):
        self.parts.append(self.links.over_near(send))

    def far(self, send):
        self.parts.append(self.links.over_far(send))

    def z_sends(self):
        self.rows //= self.links.depth
        return [
            self.total(step * self.rows, self.rows).astype(BF)
            for step in range(1, self.links.depth)
        ]

    def z(self, sends):
        depth = self.links.depth
        for step, send in enumerate(sends, 1):
            self.parts.append(self.links.over_z(send, depth - step))

    def z_back(self, sends):
        return self.links.over_z(sends[-1], 1)

    def z_ahead(self, sends):
        return self.links.over_z(sends[-2], self.links.depth - 1)

    def z_end(self, sends, back, ahead):
        self.parts.append(back)
        for send in sends[-3::-1]:
            ahead = self.links.over_z(add_low(ahead, send), self.links.depth - 1)
        self.parts.append(ahead)

    def own(self):
        return self.total(0, self.rows)

    def last(self, total):
        links, half = self.links, self.rows // 2
        above, below = total[:half], total[half:]
        own = jnp.where(links.lead, above, below)
        other = links.over_core(jnp.where(links.lead, below, above))
        return jnp.where(links.lead, own, other), jnp.where(links.lead, other, own)


class SeqScatter:
    def __init__(self, links, parts):
        self.links = links
        parts = parts.reshape(2, 2, -1, parts.shape[1])
        take = lambda core: lax.dynamic_index_in_dim(parts, core, 1, False)
        self.kept = take(links.core)
        self.sent = links.over_core(take(1 - links.core).astype(BF))

    def second(self):
        total = self.kept + self.sent.astype(F32)
        take = lambda y: lax.dynamic_index_in_dim(total, y, 0, False)
        self.kept = take(self.links.y)
        self.sent = self.links.over_y(take(1 - self.links.y).astype(BF))

    def total(self):
        return self.kept + self.sent.astype(F32)


class PlainScatter:
    parts = ()

    def core(self, sent):
        self.sent = sent

    def keep(self, kept):
        self.kept = kept

    def halve(self):
        return self.sent

    def near(self, send):
        self.sent = send

    def z_back(self, sends):
        return sends

    z_ahead = z_back

    def z_end(self, sends, back, ahead):
        self.sent = back

    far = near
    z_sends = own = halve

    def last(self, total):
        return jnp.split(scatter_all(self.kept), 2, axis=1)


def phase(*values):
    return lax.optimization_barrier(values)


def per_device(
    target, memory, cotangent, target_segments, memory_segments, bucket_ids,
    self_norm_gain, self_query, self_key, self_value, self_output, bias_table,
    cross_norm_gain, cross_query, cross_key, cross_value, cross_output,
    ffn_norm_gain, ffn_gate, ffn_up, ffn_down,
):
    batch_size, seq_size = lax.axis_size("batch"), lax.axis_size("seq")
    devices = batch_size * seq_size
    seq_index = lax.axis_index("seq")
    rows, width = target.shape[1], target.shape[2]
    length, enc = target_segments.shape[1], memory_segments.shape[1]
    enc_rows = memory.shape[1]
    inner = self_query.shape[1]
    hidden = ffn_gate.shape[1]
    table_rows, table_cols = bias_table.shape
    weight_rows = self_query.shape[0]
    table_size = table_rows * table_cols

    links = Links()
    core, lead, depth = links.core, links.lead, links.depth
    small = jnp.concatenate(
        [self_norm_gain, cross_norm_gain, ffn_norm_gain, bias_table.reshape(-1)]
    )
    small = jnp.pad(small[None], ((0, weight_rows - 1), (0, 2 * LANES - small.shape[0])))
    part = hidden // 2
    groups = [
        [self_query, self_key, self_value, small],
        [self_output, cross_query, cross_key, cross_value, cross_output],
        [ffn_gate[:, :part], ffn_up[:, :part]],
        [ffn_gate[:, part:], ffn_up[:, part:]],
    ]
    groups = [jnp.concatenate(group, axis=1) for group in groups]
    cuts = [group.shape[1] // 2 for group in groups]
    left = jnp.concatenate([group[:, :cut] for group, cut in zip(groups, cuts)], axis=1)
    right = jnp.concatenate([group[:, cut:] for group, cut in zip(groups, cuts)], axis=1)
    down_cut = width // 2
    steps = list(range(1, depth))
    z_one, z_two, z_three = steps[:1], steps[-1:] if depth > 2 else [], steps[1:-1]
    direct = 2 * ffn_down.shape[0] % 16 == 0
    move = lambda function, *args: function(links, *args) if direct else None

    moved = gather_core(links, left, right)
    down = move(gather_core, ffn_down[:, :down_cut], ffn_down[:, down_cut:])
    if not direct:
        down_whole = gather_all(ffn_down)
    moved, down = phase(moved, down)
    ends = list(np.cumsum(cuts))
    first0, second0, third0, fourth0 = jnp.split(moved, ends[:-1], axis=1)

    position = seq_index * rows
    heads = seq_size * table_cols
    distance = position + rows - jnp.arange(rows + length, dtype=jnp.int32)
    near = (distance >= 0) & (distance < length)
    bucket = jnp.take(bucket_ids, jnp.clip(distance, 0, length - 1))
    bucket_range = jnp.arange(batch_size * table_rows, dtype=jnp.int32)
    onehot = ((bucket[:, None] == bucket_range[None, :]) & near[:, None]).astype(BF)

    first_z = jnp.stack([first0] + z_steps(links, first0, steps))
    first_z, second0, down = phase(first_z, second0, down)

    first_near = gather_near(links, first_z)
    down = move(gather_near, down)
    second_one, second_two = z_steps(links, second0, z_one), z_steps(links, second0, z_two)
    rows_own = jnp.concatenate([target[0], memory[0]], axis=0)
    rows_other = links.over_y(rows_own)
    first_near, down, second_one, second_two, second0, onehot, rows_own, rows_other = phase(
        first_near, down, second_one, second_two, second0, onehot, rows_own, rows_other
    )

    first_far = links.over_far(first_near)
    first_near_other = links.over_core(first_near)
    second_z = jnp.stack(
        [second0] + second_one + z_steps(links, second0, z_three) + second_two
    )
    rows_pair = in_order(links.y == 0, rows_own, rows_other)
    rows_other = links.over_core(rows_pair)
    first_far, first_near_other, second_z, down, third0, rows_pair, rows_other = phase(
        first_far, first_near_other, second_z, down, third0, rows_pair, rows_other
    )
    by_y = lambda both: both.reshape(2, 1, rows + enc_rows, width)
    both = jnp.concatenate(
        [
            jnp.where(lead, by_y(rows_pair), by_y(rows_other)),
            jnp.where(lead, by_y(rows_other), by_y(rows_pair)),
        ],
        axis=1,
    )
    target_all = both[:, :, :rows].reshape(length, width)
    memory_all = both[:, :, rows:].reshape(enc, width)

    second_near = gather_near(links, second_z)
    third_z = jnp.stack([third0] + z_steps(links, third0, steps))
    first_far_other = links.over_core(first_far)
    down = move(gather_far, down)
    first_far_other, second_near, third_z, fourth0, down, target_all, memory_all = phase(
        first_far_other, second_near, third_z, fourth0, down, target_all, memory_all
    )

    second_far = links.over_far(second_near)
    second_near_other = links.over_core(second_near)
    third_near = gather_near(links, third_z)
    fourth_z = jnp.stack([fourth0] + z_steps(links, fourth0, steps))
    down_one = move(z_steps, down, z_one)
    down_two = move(z_steps, down, z_two)
    first = assemble(links, first_near, first_far, first_near_other, first_far_other)
    smalls = first[:, 3 * inner :].reshape(devices, weight_rows, 2 * LANES)[:, 0, :].astype(F32)
    gains = [smalls[:, i * weight_rows : (i + 1) * weight_rows].reshape(1, width) for i in range(3)]
    gain_self, gain_cross, gain_ffn = gains
    table = smalls[:, 3 * weight_rows : 3 * weight_rows + table_size]
    table = table.reshape(batch_size, seq_size, table_rows, table_cols)
    table = jnp.transpose(table, (0, 2, 1, 3)).reshape(batch_size * table_rows, seq_size * table_cols)

    windows = mm(table.astype(BF), onehot, (((0,), (1,)), ((), ())))
    windows = windows.reshape(heads // 2, 2, rows + length)
    position1 = position.reshape(1)
    qseg = lax.dynamic_slice_in_dim(target_segments, position, rows, 1).reshape(rows, 1)
    kseg, mseg = target_segments, memory_segments

    attended, queries, keys, values, normed_all = self_forward(
        position1, target_all, gain_self, first, windows, qseg, kseg
    )
    attended, second_far, second_near_other, third_near, fourth_z, down, down_one, down_two = phase(
        attended, second_far, second_near_other, third_near, fourth_z, down, down_one, down_two
    )

    third_far = links.over_far(third_near)
    third_near_other = links.over_core(third_near)
    fourth_near = links.over_near(fourth_z)
    down_three = []
    for step in z_three:
        down_three.append(links.over_z((down_one + down_three)[-1], 1) if direct else None)
    second = assemble(
        links, second_near, second_far, second_near_other, links.over_core(second_far)
    )
    (
        hidden_one, normed_two, cross_queries, cross_keys, cross_values, cross_attended,
        hidden_two, normed_three,
    ) = cross_forward(
        target[0], attended, memory_all, gain_cross, gain_ffn, second, qseg, mseg
    )
    normed_three, third_far, third_near_other, fourth_z, fourth_near = phase(
        normed_three, third_far, third_near_other, fourth_z, fourth_near
    )
    down, down_one, down_two, down_three, normed_three = phase(
        down, down_one, down_two, down_three, normed_three
    )

    fourth_near = jnp.stack([fourth_z, fourth_near])
    fourth_far = links.over_far(fourth_near)
    fourth_near_other = links.over_core(fourth_near)
    if direct:
        down = jnp.stack([down] + down_one + down_three + down_two)
    down_other = links.over_core(down) if direct else None
    third = assemble(links, third_near, third_far, third_near_other, links.over_core(third_far))
    third_gate_up = mm(normed_three, third)
    if direct:
        w_down = assemble(links, down, down_other)
    else:
        w_down = down_whole
    third_gate_up, fourth_far, fourth_near_other, w_down = phase(
        third_gate_up, fourth_far, fourth_near_other, w_down
    )

    fourth_far_other = links.over_core(fourth_far)
    cot = cotangent[0]


    def gated(gate_up, start):
        inner_act, pull = jax.vjp(gated_unit, gate_up[:, :part], gate_up[:, part:])
        grad_gate, grad_up = pull(mm(cot, w_down[start : start + part], NT))
        return inner_act.astype(BF), grad_gate.astype(BF), grad_up.astype(BF)

    inner_a, gate_a, up_a = gated(third_gate_up, 0)
    third_sum, fourth_sum = Scatter(links), Scatter(links)
    third_terms = [(normed_three, gate_a, normed_three, up_a)]
    third_send, third_keep = weight_grad(links, third_terms)
    third_send, third_keep, gate_a, up_a, fourth_far_other = phase(
        third_send, third_keep, gate_a, up_a, fourth_far_other
    )

    third_sum.core(third_send)
    third_sum.keep(third_keep)
    fourth = assemble(links, fourth_near, fourth_far, fourth_near_other, fourth_far_other)
    third_sum.parts, fourth = phase(third_sum.parts, fourth)

    third_send, fourth = phase(third_sum.halve(), fourth)
    third_sum.near(third_send)
    inner_b, gate_b, up_b = gated(mm(normed_three, fourth), part)
    fourth_terms = [(normed_three, gate_b, normed_three, up_b)]
    fourth_send, fourth_keep = weight_grad(links, fourth_terms)
    inner_low = jnp.concatenate([inner_a, inner_b], axis=1)
    down_terms = [(inner_low, cot[:, :down_cut], inner_low, cot[:, down_cut:])]
    down_sum = Scatter(links) if direct else PlainScatter()
    if direct:
        down_send, down_keep = weight_grad(links, down_terms, z_first=True)
    else:
        down_send, down_keep = inner_low, mm(inner_low, cot, TN).astype(BF)
    third_sum.parts, fourth_send, fourth_keep, down_send, down_keep, gate_b, up_b = phase(
        third_sum.parts, fourth_send, fourth_keep, down_send, down_keep, gate_b, up_b
    )

    third_send, gate_b, up_b = phase(third_sum.halve(), gate_b, up_b)
    third_sum.far(third_send)
    fourth_sum.core(fourth_send)
    fourth_sum.keep(fourth_keep)
    down_sum.core(down_send)
    down_sum.keep(down_keep)
    grad_normed_three = mm(jnp.concatenate([gate_a, up_a], axis=1), third, NT) + mm(
        jnp.concatenate([gate_b, up_b], axis=1), fourth, NT
    )
    through, grad_gain_ffn = norm_back(hidden_two, gain_ffn, grad_normed_three)
    grad_hidden_two = cot.astype(F32) + through
    third_sum.parts, fourth_sum.parts, down_sum.parts, grad_hidden_two = phase(
        third_sum.parts, fourth_sum.parts, down_sum.parts, grad_hidden_two
    )

    down_sends, fourth_send, grad_hidden_two = phase(
        down_sum.z_sends(), fourth_sum.halve(), grad_hidden_two
    )
    fourth_sum.near(fourth_send)
    down_back = down_sum.z_back(down_sends)
    low_two = grad_hidden_two.astype(BF)
    (
        grad_cq, grad_ck, grad_cv, memory_part, grad_hidden_one, low_one, grad_attended,
        grad_gain_cross,
    ) = cross_back(
        grad_hidden_two, hidden_one, gain_cross, cross_queries, cross_keys, cross_values, second,
        qseg, mseg,
    )
    half = inner // 2
    fourth_sum.parts, down_back, grad_cq, grad_ck, grad_cv, low_one, grad_attended, memory_part = (
        phase(
            fourth_sum.parts, down_back, grad_cq, grad_ck, grad_cv, low_one, grad_attended,
            memory_part,
        )
    )

    fourth_send, low_one = phase(fourth_sum.halve(), low_one)
    fourth_sum.far(fourth_send)
    down_ahead = down_sum.z_ahead(down_sends)
    cross_terms = [
        (normed_two, grad_cq, cross_attended, low_two),
        (memory_all, grad_ck, memory_all, grad_cv),
        (attended, low_one[:, :half], attended, low_one[:, half:]),
    ]
    cross_sum = Scatter(links)
    cross_send, cross_keep = weight_grad(links, cross_terms)
    cross_send, cross_keep, fourth_sum.parts, down_ahead = phase(
        cross_send, cross_keep, fourth_sum.parts, down_ahead
    )

    cross_sum.core(cross_send)
    cross_sum.keep(cross_keep)
    memory_rows = SeqScatter(links, memory_part)
    third_sends = third_sum.z_sends()
    (
        cross_sum.parts, third_sends, down_sends, down_back, down_ahead, fourth_sum.parts,
        memory_rows.sent, memory_rows.kept,
    ) = phase(
        cross_sum.parts, third_sends, down_sends, down_back, down_ahead, fourth_sum.parts,
        memory_rows.sent, memory_rows.kept,
    )

    cross_send, grad_attended, third_sends, down_sends, down_back, down_ahead = phase(
        cross_sum.halve(), grad_attended, third_sends, down_sends, down_back, down_ahead
    )
    cross_sum.near(cross_send)
    down_sum.z_end(down_sends, down_back, down_ahead)
    third_sum.z(third_sends)
    grad_q, grad_k, grad_v, grad_windows, grad_normed, grad_gain_self = self_back(
        position1, target_all, grad_attended, queries, keys, values, first, windows, qseg, kseg
    )
    (
        cross_sum.parts, down_sum.parts, fourth_sum.parts, third_sum.parts, grad_q, grad_k,
        grad_v, grad_windows, grad_normed, grad_gain_self, memory_rows.sent, memory_rows.kept,
    ) = phase(
        cross_sum.parts, down_sum.parts, fourth_sum.parts, third_sum.parts, grad_q, grad_k,
        grad_v, grad_windows, grad_normed, grad_gain_self, memory_rows.sent, memory_rows.kept,
    )

    (
        cross_send, fourth_sum.parts, grad_k, grad_windows, grad_gain_self,
    ) = phase(cross_sum.halve(), fourth_sum.parts, grad_k, grad_windows, grad_gain_self)
    cross_sum.far(cross_send)
    memory_rows.second()
    grad_windows = grad_windows.reshape(heads, rows + length)
    grad_table = lax.dot_general(
        onehot.astype(F32), grad_windows, (((0,), (1,)), ((), ())), precision=lax.Precision.HIGHEST
    )
    grad_table = grad_table.reshape(batch_size, table_rows, seq_size, table_cols)
    grad_table = jnp.transpose(grad_table, (0, 2, 1, 3)).reshape(devices, table_size)
    gain_parts = [g.reshape(devices, weight_rows) for g in (grad_gain_self, grad_gain_cross, grad_gain_ffn)]
    small_grad = jnp.concatenate(gain_parts + [grad_table], axis=1)
    small_grad = jnp.pad(
        small_grad[:, None], ((0, 0), (0, weight_rows - 1), (0, LANES - small_grad.shape[1]))
    ).reshape(devices * weight_rows, LANES)
    cut = inner + half
    self_terms = [
        (normed_all, grad_q, normed_all, grad_v),
        (normed_all, grad_k[:, :half], normed_all, grad_k[:, half:]),
    ]
    self_sum = Scatter(links)
    self_send, self_keep = weight_grad(links, self_terms, small_grad)
    (
        self_send, self_keep, cross_sum.parts, down_sum.parts, fourth_sum.parts, third_sum.parts,
        grad_normed, memory_rows.sent, memory_rows.kept, inner_low,
    ) = phase(
        self_send, self_keep, cross_sum.parts, down_sum.parts, fourth_sum.parts, third_sum.parts,
        grad_normed, memory_rows.sent, memory_rows.kept, inner_low,
    )

    self_sum.core(self_send)
    self_sum.keep(self_keep)
    cross_sends, fourth_sends = cross_sum.z_sends(), fourth_sum.z_sends()
    normed_rows = SeqScatter(links, grad_normed)
    self_sum.parts, cross_sends, fourth_sends, normed_rows.sent, normed_rows.kept = phase(
        self_sum.parts, cross_sends, fourth_sends, normed_rows.sent, normed_rows.kept
    )

    self_send, cross_sends, fourth_sends, inner_low = phase(
        self_sum.halve(), cross_sends, fourth_sends, inner_low
    )
    self_sum.near(self_send)
    cross_back_z, cross_ahead_z = cross_sum.z_back(cross_sends), cross_sum.z_ahead(cross_sends)
    fourth_back, fourth_ahead = fourth_sum.z_back(fourth_sends), fourth_sum.z_ahead(fourth_sends)
    activations = (hidden_two + mm(inner_low, w_down)).astype(BF)
    (
        self_sum.parts, cross_back_z, cross_ahead_z, fourth_back, fourth_ahead, down_sum.parts,
        activations, third_sum.parts, normed_rows.sent,
    ) = phase(
        self_sum.parts, cross_back_z, cross_ahead_z, fourth_back, fourth_ahead, down_sum.parts,
        activations, third_sum.parts, normed_rows.sent,
    )

    (
        self_send, down_sum.parts, cross_sends, cross_back_z, cross_ahead_z, fourth_sends,
        fourth_back, fourth_ahead, normed_rows.sent,
    ) = phase(
        self_sum.halve(), down_sum.parts, cross_sends, cross_back_z, cross_ahead_z, fourth_sends,
        fourth_back, fourth_ahead, normed_rows.sent,
    )
    self_sum.far(self_send)
    cross_sum.z_end(cross_sends, cross_back_z, cross_ahead_z)
    fourth_sum.z_end(fourth_sends, fourth_back, fourth_ahead)
    down_sum.far(down_sum.halve())
    normed_rows.second()
    self_sum.parts, cross_sum.parts, fourth_sum.parts, down_sum.parts, normed_rows.sent = phase(
        self_sum.parts, cross_sum.parts, fourth_sum.parts, down_sum.parts, normed_rows.sent
    )

    (
        self_sends, cross_sum.parts, down_sum.parts, third_sum.parts, fourth_sum.parts,
        normed_rows.sent, memory_rows.sent,
    ) = phase(
        self_sum.z_sends(), cross_sum.parts, down_sum.parts, third_sum.parts, fourth_sum.parts,
        normed_rows.sent, memory_rows.sent,
    )
    self_sum.z(self_sends)
    down_sum.near(down_sum.halve())
    gate_one, up_one = third_sum.last(third_sum.own())
    gate_two, up_two = fourth_sum.last(fourth_sum.own())
    cross_left, cross_right = cross_sum.last(cross_sum.own())
    memory_grad = memory_rows.total()
    through, _ = norm_back(target[0].astype(F32), gain_self, normed_rows.total())
    target_grad = grad_hidden_one + through
    down_out = jnp.concatenate(down_sum.last(down_sum.own()), axis=1)
    self_left, self_right = self_sum.last(self_sum.own())
    join = lambda left, right: jnp.concatenate([left, right], axis=1)

    small_out = self_left[0, cut:]
    gain_out = [small_out[i * weight_rows : (i + 1) * weight_rows] for i in range(3)]
    table_out = small_out[3 * weight_rows : 3 * weight_rows + table_size]
    return (
        activations[None],
        target_grad[None],
        memory_grad[None],
        gain_out[0],
        self_left[:, :inner],
        join(self_left[:, inner:cut], self_right[:, inner:cut]),
        self_right[:, :inner],
        join(cross_left[:, 2 * inner :], cross_right[:, 2 * inner :]),
        table_out.reshape(table_rows, table_cols),
        gain_out[1],
        cross_left[:, :inner],
        cross_left[:, inner : 2 * inner],
        cross_right[:, inner : 2 * inner],
        cross_right[:, :inner],
        gain_out[2],
        jnp.concatenate([gate_one, gate_two], axis=1),
        jnp.concatenate([up_one, up_two], axis=1),
        down_out,
    )


def solution(mesh):
    rows3 = P("batch", "seq", None)
    seg = P("batch", None)
    gain = P(AXES)
    weight = P(AXES, None)
    table = P("batch", "seq")
    return jax.shard_map(
        per_device,
        mesh=mesh,
        in_specs=(
            rows3, rows3, rows3, seg, seg, P(),
            gain, weight, weight, weight, weight, table,
            gain, weight, weight, weight, weight,
            gain, weight, weight, weight,
        ),
        out_specs=(
            rows3, rows3, rows3,
            gain, weight, weight, weight, weight, table,
            gain, weight, weight, weight, weight,
            gain, weight, weight, weight,
        ),
        check_vma=False,
    )
```

```python
import functools

import jax
import jax.numpy as jnp
import numpy as np
from jax import lax
from jax.experimental import pallas as pl
from jax.experimental.pallas import tpu as pltpu
from jax.sharding import PartitionSpec as P

HD = 64
LANES = 128
SUBLANES = 8
EPSILON = 1e-06
MASKED = -1e30
BF = jnp.bfloat16
F32 = jnp.float32
AXES = ("batch", "seq")
NT = (((1,), (1,)), ((), ()))
TN = (((0,), (0,)), ((), ()))
NN = (((1,), (0,)), ((), ()))


def mm(left, right, dims=NN):
    return lax.dot_general(left, right, dims, preferred_element_type=F32)


def gated_unit(gate_act, up_act):
    return jax.nn.gelu(gate_act, approximate=True) * up_act


def head_only(pair, head):
    lane = lax.broadcasted_iota(jnp.int32, pair.shape, 1)
    return jnp.where((lane // HD) == head, pair, jnp.zeros_like(pair))


def pick_heads(first, second):
    lane = lax.broadcasted_iota(jnp.int32, first.shape, 1)
    return jnp.where(lane < HD, first, second)


def spread(window, rows):
    wide = jnp.broadcast_to(window, (rows, window.shape[1]))
    rolled = pltpu.roll(wide, 0, 1, stride=1, stride_axis=0)
    return rolled[:, rows:]


def unspread(grads, rows):
    wide = jnp.concatenate([jnp.zeros((rows, rows), F32), grads], axis=1)
    width = wide.shape[1]
    total = wide[:SUBLANES]
    for start in range(SUBLANES, rows, SUBLANES):
        total = total + pltpu.roll(wide[start : start + SUBLANES], width - start, 1)
    row = lax.broadcasted_iota(jnp.int32, total.shape, 0)
    for bit in (1, 2, 4):
        total = jnp.where((row & bit) != 0, pltpu.roll(total, width - bit, 1), total)
    return jnp.sum(total, axis=0, keepdims=True)


def allowed_pairs(position, query_segments, key_segments, causal):
    rows, keys = query_segments.shape[0], key_segments.shape[1]
    allowed = query_segments == key_segments
    if causal:
        own = lax.broadcasted_iota(jnp.int32, (rows, keys), 0) + position
        other = lax.broadcasted_iota(jnp.int32, (rows, keys), 1)
        allowed = allowed & (own >= other)
    return allowed


def pair_probs(query, key, bias_ref, allowed, head, causal):
    scores = mm(head_only(query, head), key, NT)
    if causal:
        scores = scores + spread(bias_ref[0, head : head + 1, :], query.shape[0])
    scores = jnp.where(allowed, scores, MASKED)
    top = jnp.max(scores, axis=1, keepdims=True)
    grown = jnp.exp(scores - top)
    return grown / jnp.sum(grown, axis=1, keepdims=True)


def attend_pair(query, key, value, bias_ref, allowed, causal):
    parts = []
    for head in range(2):
        probs = pair_probs(query, key, bias_ref, allowed, head, causal)
        parts.append(mm(probs.astype(BF), value))
    return pick_heads(*parts).astype(BF)


def attend_pair_back(query, key, value, grad, bias_ref, dbias_ref, allowed, causal):
    grad_query, grad_key, grad_value = [], 0.0, 0.0
    for head in range(2):
        probs = pair_probs(query, key, bias_ref, allowed, head, causal)
        grad_head = head_only(grad, head)
        grad_probs = mm(grad_head, value, NT)
        inner = jnp.sum(probs * grad_probs, axis=1, keepdims=True)
        grad_scores = probs * (grad_probs - inner)
        low_scores = grad_scores.astype(BF)
        grad_query.append(mm(low_scores, key))
        grad_key = grad_key + mm(low_scores, head_only(query, head), TN)
        grad_value = grad_value + mm(probs.astype(BF), grad_head, TN)
        if causal:
            dbias_ref[0, head : head + 1, :] = unspread(grad_scores, query.shape[0])
    return pick_heads(*grad_query).astype(BF), grad_key.astype(BF), grad_value.astype(BF)


def scale_of(values):
    return lax.rsqrt(jnp.mean(values * values, axis=-1, keepdims=True) + EPSILON)


def norm_back(values, gain, grad_out):
    scale = scale_of(values)
    unit = values * scale
    lean = jnp.mean(grad_out * gain * unit, axis=-1, keepdims=True)
    grad_gain = jnp.sum(grad_out * unit, axis=0, keepdims=True)
    return scale * (grad_out * gain - unit * lean), grad_gain


def cost(microseconds):
    return pl.CostEstimate(flops=microseconds * 10**9, bytes_accessed=1, transcendentals=0)


PARAMS = pltpu.CompilerParams(dimension_semantics=("arbitrary",), vmem_limit_bytes=48 << 20)
SMEM = pl.BlockSpec(memory_space=pltpu.SMEM)


def whole(array, rows=None):
    shape = array.shape if rows is None else (rows, array.shape[1])
    return pl.BlockSpec(shape, lambda step: (0,) * len(shape))


def pair_cols(rows, offset=0):
    return pl.BlockSpec((rows, LANES), lambda step: (0, offset + step))


def shape_of(*shape, dtype=BF):
    return jax.ShapeDtypeStruct(shape, dtype)


def windows_spec(windows):
    return pl.BlockSpec((1, 2, windows.shape[2]), lambda step: (step, 0, 0))


def self_forward(place, target_all, gain, weights, windows, qseg, kseg):
    (length, width), rows = target_all.shape, qseg.shape[0]
    inner = windows.shape[0] * LANES
    pairs = inner // LANES

    def body(
        pos_ref, rows_ref, gain_ref, wq_ref, wk_ref, wv_ref, win_ref, qseg_ref, kseg_ref,
        out_ref, q_ref, k_ref, v_ref, normed_ref,
    ):
        position = pl.multiple_of(pos_ref[0], LANES)

        @pl.when(pl.program_id(0) == 0)
        def _():
            values = rows_ref[...].astype(F32)
            normed_ref[...] = (values * scale_of(values) * gain_ref[...]).astype(BF)

        normed = normed_ref[...]
        query = mm(normed_ref[pl.ds(position, rows), :], wq_ref[...]).astype(BF)
        key = mm(normed, wk_ref[...]).astype(BF)
        value = mm(normed, wv_ref[...]).astype(BF)
        q_ref[...], k_ref[...], v_ref[...] = query, key, value
        allowed = allowed_pairs(position, qseg_ref[...], kseg_ref[...], True)
        out_ref[...] = attend_pair(query, key, value, win_ref, allowed, True)

    return pl.pallas_call(
        body,
        grid=(pairs,),
        in_specs=[
            SMEM, whole(target_all), whole(gain),
            pair_cols(width), pair_cols(width, pairs), pair_cols(width, 2 * pairs),
            windows_spec(windows), whole(qseg), whole(kseg),
        ],
        out_specs=[
            pair_cols(rows), pair_cols(rows), pair_cols(length), pair_cols(length),
            whole(target_all),
        ],
        out_shape=[
            shape_of(rows, inner), shape_of(rows, inner), shape_of(length, inner),
            shape_of(length, inner), shape_of(length, width),
        ],
        compiler_params=PARAMS,
        cost_estimate=cost(4),
        name="self_forward",
    )(place, target_all, gain, weights, weights, weights, windows, qseg, kseg)


def self_back(place, target_all, grad, query, key, value, weights, windows, qseg, kseg):
    (length, width), (rows, inner) = target_all.shape, query.shape
    pairs = inner // LANES

    def body(
        pos_ref, rows_ref, do_ref, q_ref, k_ref, v_ref, wq_ref, wk_ref, wv_ref, win_ref,
        qseg_ref, kseg_ref, dq_ref, dk_ref, dv_ref, dwin_ref, back_ref, dgain_ref,
    ):
        step = pl.program_id(0)
        position = pl.multiple_of(pos_ref[0], LANES)
        own = pl.ds(position, rows)
        allowed = allowed_pairs(position, qseg_ref[...], kseg_ref[...], True)
        dq, dk, dv = attend_pair_back(
            q_ref[...], k_ref[...], v_ref[...], do_ref[...], win_ref, dwin_ref, allowed, True
        )
        dq_ref[...] = jnp.zeros_like(dq_ref)
        dq_ref[own, :] = dq
        dk_ref[...], dv_ref[...] = dk, dv
        back = mm(dk, wk_ref[...], NT) + mm(dv, wv_ref[...], NT)

        @pl.when(step == 0)
        def _():
            back_ref[...] = back

        @pl.when(step > 0)
        def _():
            back_ref[...] += back

        back_ref[own, :] += mm(dq, wq_ref[...], NT)

        @pl.when(step == pairs - 1)
        def _():
            values = rows_ref[...].astype(F32)
            dgain_ref[...] = jnp.sum(
                values * scale_of(values) * back_ref[...], axis=0, keepdims=True
            )

    return pl.pallas_call(
        body,
        grid=(pairs,),
        in_specs=[
            SMEM, whole(target_all), pair_cols(rows),
            pair_cols(rows), pair_cols(length), pair_cols(length),
            pair_cols(width), pair_cols(width, pairs), pair_cols(width, 2 * pairs),
            windows_spec(windows), whole(qseg), whole(kseg),
        ],
        out_specs=[
            pair_cols(length), pair_cols(length), pair_cols(length), windows_spec(windows),
            whole(target_all), pl.BlockSpec((1, width), lambda step: (0, 0)),
        ],
        out_shape=[
            shape_of(length, inner), shape_of(length, inner), shape_of(length, inner),
            shape_of(*windows.shape, dtype=F32), shape_of(length, width, dtype=F32),
            shape_of(1, width, dtype=F32),
        ],
        compiler_params=PARAMS,
        cost_estimate=cost(1),
        name="self_back",
    )(place, target_all, grad, query, key, value, weights, weights, weights, windows, qseg, kseg)


def cross_forward(target, attended, memory_all, gain_cross, gain_ffn, weights, qseg, mseg):
    (rows, width), inner, enc = target.shape, attended.shape[1], memory_all.shape[0]
    pairs = inner // LANES

    def body(
        rows_ref, att_ref, mem_ref, gain_ref, gain3_ref, wo_ref, wq_ref, wk_ref, wv_ref, wc_ref,
        qseg_ref, mseg_ref, one_ref, normed_ref, q_ref, k_ref, v_ref, out_ref, two_ref, last_ref,
    ):
        step = pl.program_id(0)

        @pl.when(step == 0)
        def _():
            hidden = rows_ref[...].astype(F32) + mm(att_ref[...], wo_ref[...])
            one_ref[...] = hidden
            two_ref[...] = hidden
            normed_ref[...] = (hidden * scale_of(hidden) * gain_ref[...]).astype(BF)

        query = mm(normed_ref[...], wq_ref[...]).astype(BF)
        key = mm(mem_ref[...], wk_ref[...]).astype(BF)
        value = mm(mem_ref[...], wv_ref[...]).astype(BF)
        q_ref[...], k_ref[...], v_ref[...] = query, key, value
        allowed = allowed_pairs(0, qseg_ref[...], mseg_ref[...], False)
        out = attend_pair(query, key, value, None, allowed, False)
        out_ref[...] = out
        two_ref[...] += mm(out, wc_ref[...])

        @pl.when(step == pairs - 1)
        def _():
            hidden = two_ref[...]
            last_ref[...] = (hidden * scale_of(hidden) * gain3_ref[...]).astype(BF)

    return pl.pallas_call(
        body,
        grid=(pairs,),
        in_specs=[
            whole(target), whole(attended), whole(memory_all), whole(gain_cross), whole(gain_ffn),
            pl.BlockSpec((width, width), lambda step: (0, 0)),
            pair_cols(width, pairs), pair_cols(width, 2 * pairs), pair_cols(width, 3 * pairs),
            pl.BlockSpec((LANES, width), lambda step: (step, 4)),
            whole(qseg), whole(mseg),
        ],
        out_specs=[
            whole(target), whole(target), pair_cols(rows), pair_cols(enc), pair_cols(enc),
            pair_cols(rows), whole(target), whole(target),
        ],
        out_shape=[
            shape_of(rows, width, dtype=F32), shape_of(rows, width), shape_of(rows, inner),
            shape_of(enc, inner), shape_of(enc, inner), shape_of(rows, inner),
            shape_of(rows, width, dtype=F32), shape_of(rows, width),
        ],
        compiler_params=PARAMS,
        cost_estimate=cost(8),
        name="cross_forward",
    )(
        target, attended, memory_all, gain_cross, gain_ffn, weights, weights, weights, weights,
        weights, qseg, mseg,
    )


def cross_back(grad_two, hidden_one, gain, query, key, value, weights, qseg, mseg):
    (rows, width), inner, enc = hidden_one.shape, query.shape[1], key.shape[0]
    pairs = inner // LANES

    def body(
        grad_ref, one_ref, gain_ref, q_ref, k_ref, v_ref, wo_ref, wq_ref, wk_ref, wv_ref, wc_ref,
        qseg_ref, mseg_ref, dq_ref, dk_ref, dv_ref, mem_ref, done_ref, low_ref, datt_ref,
        dgain_ref, two_ref, back_ref,
    ):
        step = pl.program_id(0)

        @pl.when(step == 0)
        def _():
            two_ref[...] = grad_ref[...].astype(BF)

        grad = mm(two_ref[...], wc_ref[...], NT).astype(BF)
        allowed = allowed_pairs(0, qseg_ref[...], mseg_ref[...], False)
        dq, dk, dv = attend_pair_back(
            q_ref[...], k_ref[...], v_ref[...], grad, None, None, allowed, False
        )
        dq_ref[...], dk_ref[...], dv_ref[...] = dq, dk, dv
        back = mm(dq, wq_ref[...], NT)
        memory = mm(dk, wk_ref[...], NT) + mm(dv, wv_ref[...], NT)

        @pl.when(step == 0)
        def _():
            back_ref[...] = back
            mem_ref[...] = memory

        @pl.when(step > 0)
        def _():
            back_ref[...] += back
            mem_ref[...] += memory

        @pl.when(step == pairs - 1)
        def _():
            through, grad_gain = norm_back(one_ref[...], gain_ref[...], back_ref[...])
            grad_one = grad_ref[...] + through
            low = grad_one.astype(BF)
            done_ref[...] = grad_one
            low_ref[...] = low
            dgain_ref[...] = grad_gain
            datt_ref[...] = mm(low, wo_ref[...], NT).astype(BF)

    row = pl.BlockSpec((1, width), lambda step: (0, 0))
    return pl.pallas_call(
        body,
        grid=(pairs,),
        in_specs=[
            whole(grad_two), whole(hidden_one), row,
            pair_cols(rows), pair_cols(enc), pair_cols(enc),
            pl.BlockSpec((width, width), lambda step: (0, 0)),
            pair_cols(width, pairs), pair_cols(width, 2 * pairs), pair_cols(width, 3 * pairs),
            pl.BlockSpec((LANES, width), lambda step: (step, 4)),
            whole(qseg), whole(mseg),
        ],
        out_specs=[
            pair_cols(rows), pair_cols(enc), pair_cols(enc),
            pl.BlockSpec((enc, width), lambda step: (0, 0)),
            whole(hidden_one), whole(hidden_one), whole(hidden_one), row,
        ],
        out_shape=[
            shape_of(rows, inner), shape_of(enc, inner), shape_of(enc, inner),
            shape_of(enc, width, dtype=F32), shape_of(rows, width, dtype=F32),
            shape_of(rows, width), shape_of(rows, inner), shape_of(1, width, dtype=F32),
        ],
        scratch_shapes=[pltpu.VMEM((rows, width), BF), pltpu.VMEM((rows, width), F32)],
        compiler_params=PARAMS,
        cost_estimate=cost(1),
        name="cross_back",
    )(
        grad_two, hidden_one, gain, query, key, value, weights, weights, weights, weights, weights,
        qseg, mseg,
    )


def gather_all(shard):
    return lax.all_gather(shard, AXES, axis=0, tiled=True)


def scatter_all(grads):
    return lax.psum_scatter(grads, AXES, scatter_dimension=0, tiled=True).astype(F32)


class Links:
    def __init__(self):
        self.batch, self.seq = lax.axis_size("batch"), lax.axis_size("seq")
        self.depth = self.batch // 2
        z_x, y_c = lax.axis_index("batch"), lax.axis_index("seq")
        self.z, self.x = z_x // 2, z_x % 2
        self.y, self.core = y_c // 2, y_c % 2
        self.lead = self.core == 0
        self.place = jnp.stack([self.z, self.x, self.y, self.core]).astype(jnp.int32)

    def move(self, value, target):
        pairs = []
        for source in range(self.batch * self.seq):
            z_x, y_c = source // self.seq, source % self.seq
            z, x, y, core = target(z_x // 2, z_x % 2, y_c // 2, y_c % 2)
            pairs.append((source, (z * 2 + x) * self.seq + y * 2 + core))
        return lax.ppermute(value, AXES, pairs)

    def over_core(self, value):
        return self.move(value, lambda z, x, y, core: (z, x, y, 1 - core))

    def over_y(self, value):
        return self.move(value, lambda z, x, y, core: (z, x, 1 - y, core))

    def over_near(self, value):
        return self.move(
            value, lambda z, x, y, c: (z, x, 1 - y, c) if c else (z, 1 - x, y, c)
        )

    def over_far(self, value):
        return self.move(
            value, lambda z, x, y, c: (z, 1 - x, y, c) if c else (z, x, 1 - y, c)
        )

    def over_z(self, value, step):
        depth = self.depth
        return self.move(value, lambda z, x, y, core: ((z - step) % depth, x, y, core))


def in_order(first, own, other):
    return jnp.concatenate([jnp.where(first, own, other), jnp.where(first, other, own)], axis=0)


def gather_core(links, left, right):
    own = jnp.where(links.lead, left, right)
    other = links.over_core(jnp.where(links.lead, right, left))
    return in_order(links.lead, own, other)


def z_steps(links, value, steps):
    return [links.over_z(value, step) for step in steps]


def gather_near(links, value):
    return jnp.stack([value, links.over_near(value)])


def gather_far(links, value):
    return jnp.stack([value, links.over_far(value)])


def assemble(links, *sources):
    count, (rows, cols) = len(sources) // 2, sources[0].shape[-2:]
    depth = links.depth

    def body(place_ref, *refs):
        inputs, out_ref, sem = refs[:-2], refs[-2], refs[-1]
        z, x, y, core = [place_ref[i] for i in range(4)]
        for which, source in enumerate(inputs):
            half = core if which < count else 1 - core
            for near, far, step in np.ndindex(2, 2, depth):
                if count == 2 and far != which % 2:
                    continue
                step_x, step_y = jnp.where(half == 0, near, far), jnp.where(half == 0, far, near)
                chip = (((z + step) % depth) * 2 + (x ^ step_x)) * 2 + (y ^ step_y)
                target = out_ref.at[
                    pl.ds(pl.multiple_of(chip * rows, 16), rows),
                    pl.ds(pl.multiple_of(half * cols, LANES), cols),
                ]
                part = source.at[near, step] if count == 2 else source.at[step, far, near]
                pltpu.make_async_copy(part, target, sem).start()
        pltpu.make_async_copy(out_ref, out_ref, sem).wait()

    return pl.pallas_call(
        body,
        in_specs=[pl.BlockSpec(memory_space=pltpu.SMEM)]
        + [pl.BlockSpec(memory_space=pl.ANY)] * len(sources),
        out_specs=pl.BlockSpec(memory_space=pltpu.VMEM),
        out_shape=jax.ShapeDtypeStruct((depth * 4 * rows, 2 * cols), sources[0].dtype),
        scratch_shapes=[pltpu.SemaphoreType.DMA(())],
        compiler_params=pltpu.CompilerParams(vmem_limit_bytes=48 << 20),
        cost_estimate=cost(1),
        name="assemble",
    )(links.place, *sources)


def weight_grad(links, terms, extra=None, z_first=False):
    depth, total_rows = links.depth, terms[0][0][0].shape[1]
    rows = total_rows // (depth * 4)
    widths = [term[0][1].shape[1] for term in terms]
    extra_width = 0 if extra is None else extra.shape[1]
    total = sum(widths) + extra_width
    tile = 1408 if total % 1408 == 0 else 512
    operands = [array for term in terms for pair in term for array in pair]
    operands += [] if extra is None else [extra]
    amount, pieces = len(operands), depth if z_first else 2
    piece_rows = total_rows // pieces

    def body(place_ref, *refs):
        sources, outs = refs[:amount], refs[amount : amount + pieces]
        stage, sems = refs[amount + pieces], refs[amount + pieces + 1]
        inputs, arrived = refs[amount + pieces + 2 : -1], refs[-1]
        fetches = [
            pltpu.make_async_copy(source, target, arrived.at[index])
            for index, (source, target) in enumerate(zip(sources, inputs))
        ]
        for fetch in fetches:
            fetch.start()
        z, x, y, left = place_ref[0], place_ref[1], place_ref[2], place_ref[3] == 0
        places = []
        for chip in range(depth * 4):
            step_x, step_y = (chip // 2 % 2) ^ x, (chip % 2) ^ y
            near, far = jnp.where(left, step_x, step_y), jnp.where(left, step_y, step_x)
            step = (chip // 4 - z) % depth
            spot = (step * 2 + far) * 2 + near if z_first else (near * 2 + far) * depth + step
            places.append(pl.multiple_of(spot * rows, 8))

        def copy(piece, index, start, width):
            cols = pl.ds(start, width)
            return pltpu.make_async_copy(
                stage.at[pl.ds(piece * piece_rows, piece_rows), cols],
                outs[piece].at[:, cols],
                sems.at[piece, index],
            )

        def emit(index, start, value, width):
            for chip, spot in enumerate(places):
                stage[pl.ds(spot, rows), pl.ds(start, width)] = value[
                    chip * rows : (chip + 1) * rows
                ].astype(BF)
            for piece in range(pieces):
                copy(piece, index, start, width).start()

        begin, first_copy, taken = 0, 0, 0
        for term, width in zip(terms, widths):
            pairs = inputs[taken : taken + 2 * len(term)]
            for fetch in fetches[taken : taken + 2 * len(term)]:
                fetch.wait()
            taken += 2 * len(term)

            def one_tile(index, carry, begin=begin, first_copy=first_copy, pairs=pairs):
                cols = pl.ds(pl.multiple_of(index * tile, LANES), tile)
                value = mm(pairs[0][...], pairs[1][:, cols], TN)
                if len(pairs) == 4:
                    value = value + mm(pairs[2][...], pairs[3][:, cols], TN)
                start = pl.multiple_of(begin + index * tile, LANES)
                emit(first_copy + index, start, value, tile)
                return carry

            lax.fori_loop(0, width // tile, one_tile, 0)
            begin, first_copy = begin + width, first_copy + width // tile
        if extra is not None:
            fetches[-1].wait()
            small = inputs[-1][...]
            emit(first_copy, begin, jnp.where(left, small, jnp.zeros_like(small)), extra_width)
        for piece in range(pieces):
            for index in range(first_copy):
                copy(piece, index, index * tile, tile).wait()
            if extra is not None:
                copy(piece, first_copy, begin, extra_width).wait()

    count = sum(width // tile for width in widths) + (extra is not None)
    hbm = pl.BlockSpec(memory_space=pltpu.HBM)
    return pl.pallas_call(
        body,
        in_specs=[pl.BlockSpec(memory_space=pltpu.SMEM)] + [hbm] * amount,
        out_specs=[pl.BlockSpec(memory_space=pl.ANY)] * pieces,
        out_shape=[jax.ShapeDtypeStruct((piece_rows, total), BF)] * pieces,
        scratch_shapes=[pltpu.VMEM((total_rows, total), BF), pltpu.SemaphoreType.DMA((pieces, count))]
        + [pltpu.VMEM(array.shape, array.dtype) for array in operands]
        + [pltpu.SemaphoreType.DMA((amount,))],
        compiler_params=pltpu.CompilerParams(vmem_limit_bytes=48 << 20),
        cost_estimate=cost(1),
        name="weight_grad",
    )(links.place, *operands)


def add_low(one, other):
    return (one.astype(F32) + other.astype(F32)).astype(BF)


class Scatter:
    def __init__(self, links, kept):
        self.links, self.parts, self.rows = links, [kept], kept.shape[0]

    def total(self, start, count):
        return sum(part[start : start + count].astype(F32) for part in self.parts)

    def halve(self):
        self.rows //= 2
        return self.total(self.rows, self.rows).astype(BF)

    def near(self, send):
        self.parts.append(self.links.over_near(send))

    def far(self, send):
        self.parts.append(self.links.over_far(send))

    def z_sends(self):
        self.rows //= self.links.depth
        return [
            self.total(step * self.rows, self.rows).astype(BF)
            for step in range(1, self.links.depth)
        ]

    def z(self, sends):
        depth = self.links.depth
        for step, send in enumerate(sends, 1):
            self.parts.append(self.links.over_z(send, depth - step))

    def z_back(self, sends):
        return self.links.over_z(sends[-1], 1)

    def z_ahead(self, sends):
        return self.links.over_z(sends[-2], self.links.depth - 1)

    def z_mid(self, sends, ahead):
        for send in sends[-3:0:-1]:
            ahead = self.links.over_z(add_low(ahead, send), self.links.depth - 1)
        return add_low(ahead, sends[0])

    def z_last(self, back, ahead):
        self.parts += [back, self.links.over_z(ahead, self.links.depth - 1)]

    def z_end(self, sends, back, ahead):
        self.z_last(back, self.z_mid(sends, ahead))

    def own(self):
        return self.total(0, self.rows)

    def last(self, total):
        links, half = self.links, self.rows // 2
        above, below = total[:half], total[half:]
        own = jnp.where(links.lead, above, below)
        other = links.over_core(jnp.where(links.lead, below, above))
        return jnp.where(links.lead, own, other), jnp.where(links.lead, other, own)


class SeqScatter:
    def __init__(self, links, parts):
        self.links = links
        parts = parts.reshape(2, 2, -1, parts.shape[1])
        take = lambda core: lax.dynamic_index_in_dim(parts, core, 1, False)
        self.kept = take(links.core)
        self.sent = links.over_core(take(1 - links.core).astype(BF))

    def second(self):
        total = self.kept + self.sent.astype(F32)
        take = lambda y: lax.dynamic_index_in_dim(total, y, 0, False)
        self.kept = take(self.links.y)
        self.sent = self.links.over_y(take(1 - self.links.y).astype(BF))

    def total(self):
        return self.kept + self.sent.astype(F32)


class PlainScatter:
    parts = ()

    def __init__(self, kept):
        self.kept = kept

    def halve(self):
        return ()

    def near(self, send):
        pass

    def z_mid(self, sends, ahead):
        return ()

    def z_last(self, back, ahead):
        pass

    def z_back(self, sends):
        return ()

    far, own, z_ahead = near, halve, z_back

    def last(self, total):
        return jnp.split(scatter_all(self.kept), 2, axis=1)


def phase(*values):
    return lax.optimization_barrier(values)


def per_device(
    target, memory, cotangent, target_segments, memory_segments, bucket_ids,
    self_norm_gain, self_query, self_key, self_value, self_output, bias_table,
    cross_norm_gain, cross_query, cross_key, cross_value, cross_output,
    ffn_norm_gain, ffn_gate, ffn_up, ffn_down,
):
    batch_size, seq_size = lax.axis_size("batch"), lax.axis_size("seq")
    devices = batch_size * seq_size
    seq_index = lax.axis_index("seq")
    rows, width = target.shape[1], target.shape[2]
    length, enc = target_segments.shape[1], memory_segments.shape[1]
    enc_rows = memory.shape[1]
    inner = self_query.shape[1]
    hidden = ffn_gate.shape[1]
    table_rows, table_cols = bias_table.shape
    weight_rows = self_query.shape[0]
    table_size = table_rows * table_cols

    links = Links()
    core, lead, depth = links.core, links.lead, links.depth
    small = jnp.concatenate(
        [self_norm_gain, cross_norm_gain, ffn_norm_gain, bias_table.reshape(-1)]
    )
    small = jnp.pad(small[None], ((0, weight_rows - 1), (0, 2 * LANES - small.shape[0])))
    part = hidden // 2
    groups = [
        [self_query, self_key, self_value, small],
        [self_output, cross_query, cross_key, cross_value, cross_output],
        [ffn_gate[:, :part], ffn_up[:, :part]],
        [ffn_gate[:, part:], ffn_up[:, part:]],
    ]
    groups = [jnp.concatenate(group, axis=1) for group in groups]
    cuts = [group.shape[1] // 2 for group in groups]
    left = jnp.concatenate([group[:, :cut] for group, cut in zip(groups, cuts)], axis=1)
    right = jnp.concatenate([group[:, cut:] for group, cut in zip(groups, cuts)], axis=1)
    down_cut = width // 2
    steps = list(range(1, depth))
    z_one, z_two, z_three = steps[:1], steps[-1:] if depth > 2 else [], steps[1:-1]
    direct = 2 * ffn_down.shape[0] % 16 == 0
    move = lambda function, *args: function(links, *args) if direct else None

    moved = gather_core(links, left, right)
    down = move(gather_core, ffn_down[:, :down_cut], ffn_down[:, down_cut:])
    if not direct:
        down_whole = gather_all(ffn_down)
    moved, down = phase(moved, down)
    ends = list(np.cumsum(cuts))
    first0, second0, gated0 = jnp.split(moved, ends[:2], axis=1)

    first_z = jnp.stack([first0] + z_steps(links, first0, steps))
    first_z, second0, down = phase(first_z, second0, down)

    first_near = gather_near(links, first_z)
    down = move(gather_near, down)
    second_one, second_two = z_steps(links, second0, z_one), z_steps(links, second0, z_two)
    rows_own = jnp.concatenate([target[0], memory[0]], axis=0)
    rows_other = links.over_y(rows_own)
    first_near, down, second_one, second_two, second0, rows_own, rows_other = phase(
        first_near, down, second_one, second_two, second0, rows_own, rows_other
    )

    first_far = links.over_far(first_near)
    first_near_other = links.over_core(first_near)
    second_three = []
    for step in z_three:
        second_three.append(links.over_z((second_one + second_three)[-1], 1))
    second_z = jnp.stack([second0] + second_one + second_three + second_two)
    rows_pair = in_order(links.y == 0, rows_own, rows_other)
    rows_other = links.over_core(rows_pair)
    first_far, first_near_other, second_z, down, gated0, rows_pair, rows_other, bucket_ids = phase(
        first_far, first_near_other, second_z, down, gated0, rows_pair, rows_other, bucket_ids
    )
    by_y = lambda both: both.reshape(2, 1, rows + enc_rows, width)
    both = jnp.concatenate(
        [
            jnp.where(lead, by_y(rows_pair), by_y(rows_other)),
            jnp.where(lead, by_y(rows_other), by_y(rows_pair)),
        ],
        axis=1,
    )
    target_all = both[:, :, :rows].reshape(length, width)
    memory_all = both[:, :, rows:].reshape(enc, width)

    position = seq_index * rows
    heads = seq_size * table_cols
    distance = position + rows - jnp.arange(rows + length, dtype=jnp.int32)
    near = (distance >= 0) & (distance < length)
    bucket = jnp.take(bucket_ids, jnp.clip(distance, 0, length - 1))
    bucket_range = jnp.arange(batch_size * table_rows, dtype=jnp.int32)
    onehot = ((bucket[:, None] == bucket_range[None, :]) & near[:, None]).astype(BF)

    second_near = gather_near(links, second_z)
    gated0, down, target_all, memory_all = phase(gated0, down, target_all, memory_all)
    gated_z = jnp.stack([gated0] + z_steps(links, gated0, steps))
    third_z, fourth_z = gated_z[..., : cuts[2]], gated_z[..., cuts[2] :]
    first_far_other = links.over_core(first_far)
    down = move(gather_far, down)
    (
        first_far_other, second_near, third_z, fourth_z, down, target_all, memory_all, onehot,
    ) = phase(
        first_far_other, second_near, third_z, fourth_z, down, target_all, memory_all, onehot,
    )

    second_far = links.over_far(second_near)
    second_near_other = links.over_core(second_near)
    third_near = gather_near(links, third_z)
    down_one, down_two = move(z_steps, down, z_one), move(z_steps, down, z_two)
    first = assemble(links, first_near, first_far, first_near_other, first_far_other)
    smalls = first[:, 3 * inner :].reshape(devices, weight_rows, 2 * LANES)[:, 0, :].astype(F32)
    gains = [smalls[:, i * weight_rows : (i + 1) * weight_rows].reshape(1, width) for i in range(3)]
    gain_self, gain_cross, gain_ffn = gains
    table = smalls[:, 3 * weight_rows : 3 * weight_rows + table_size]
    table = table.reshape(batch_size, seq_size, table_rows, table_cols)
    table = jnp.transpose(table, (0, 2, 1, 3)).reshape(batch_size * table_rows, seq_size * table_cols)

    windows = mm(table.astype(BF), onehot, (((0,), (1,)), ((), ())))
    windows = windows.reshape(heads // 2, 2, rows + length)
    position1 = position.reshape(1)
    qseg = lax.dynamic_slice_in_dim(target_segments, position, rows, 1).reshape(rows, 1)
    kseg, mseg = target_segments, memory_segments

    attended, queries, keys, values, normed_all = self_forward(
        position1, target_all, gain_self, first, windows, qseg, kseg
    )
    attended, second_far, second_near_other, third_near, fourth_z, down, down_one, down_two = phase(
        attended, second_far, second_near_other, third_near, fourth_z, down, down_one, down_two
    )

    third_far = links.over_far(third_near)
    third_near_other = links.over_core(third_near)
    fourth_near = links.over_near(fourth_z)
    down_three = []
    for step in z_three:
        down_three.append(links.over_z((down_one + down_three)[-1], 1) if direct else None)
    second = assemble(
        links, second_near, second_far, second_near_other, links.over_core(second_far)
    )
    (
        hidden_one, normed_two, cross_queries, cross_keys, cross_values, cross_attended,
        hidden_two, normed_three,
    ) = cross_forward(
        target[0], attended, memory_all, gain_cross, gain_ffn, second, qseg, mseg
    )
    choose = lambda left, right: (jnp.where(lead, left, right), jnp.where(lead, right, left))
    cot = cotangent[0]
    cot_own, cot_sent = choose(cot[:, :down_cut], cot[:, down_cut:])
    cot_other = links.over_core(cot_sent)
    (
        normed_three, third_far, third_near_other, fourth_z, fourth_near, down, down_one, down_two,
        down_three, cot_other,
    ) = phase(
        normed_three, third_far, third_near_other, fourth_z, fourth_near, down, down_one, down_two,
        down_three, cot_other,
    )

    fourth_near = jnp.stack([fourth_z, fourth_near])
    fourth_far = links.over_far(fourth_near)
    if direct:
        down = jnp.stack([down] + down_one + down_three + down_two)
    third_far_other, down, fourth_later = phase(links.over_core(third_far), down, fourth_near)
    down_other = links.over_core(down) if direct else None
    fourth_near_other = links.over_core(fourth_later)
    third = assemble(links, third_near, third_far, third_near_other, third_far_other)
    third_gate_up = mm(normed_three, third)
    if direct:
        w_down = assemble(links, down, down_other)
    else:
        w_down = down_whole
    third_gate_up, fourth_far, fourth_near_other, w_down, normed_three = phase(
        third_gate_up, fourth_far, fourth_near_other, w_down, normed_three
    )

    fourth_far_other = links.over_core(fourth_far)
    normed_other = links.over_core(normed_three)
    def gated(gate_up, start):
        inner_act, pull = jax.vjp(gated_unit, gate_up[:, :part], gate_up[:, part:])
        grad_gate, grad_up = pull(mm(cot, w_down[start : start + part], NT))
        return inner_act.astype(BF), grad_gate.astype(BF), grad_up.astype(BF)

    inner_a, gate_a, up_a = gated(third_gate_up, 0)
    third_own, third_sent = choose(gate_a, up_a)
    third_own, third_sent, inner_a, fourth_far_other, normed_other = phase(
        third_own, third_sent, inner_a, fourth_far_other, normed_other
    )

    third_other = links.over_core(third_sent)
    inner_a_other = links.over_core(inner_a)
    fourth = assemble(links, fourth_near, fourth_far, fourth_near_other, fourth_far_other)
    third_other, inner_a_other, fourth = phase(third_other, inner_a_other, fourth)
    third_keep, third_send = weight_grad(
        links, [[(normed_three, third_own), (normed_other, third_other)]]
    )

    third_keep, third_send, fourth = phase(third_keep, third_send, fourth)
    third_sum = Scatter(links, third_keep)
    third_sum.near(third_send)
    inner_b, gate_b, up_b = gated(mm(normed_three, fourth), part)
    fourth_own, fourth_sent = choose(gate_b, up_b)
    fourth_other = links.over_core(fourth_sent)
    inner_b_other = links.over_core(inner_b)
    inner_low = jnp.concatenate([inner_a, inner_b], axis=1)
    inner_other = jnp.concatenate([inner_a_other, inner_b_other], axis=1)
    if direct:
        down_keep, *down_sends = weight_grad(
            links, [[(inner_low, cot_own), (inner_other, cot_other)]], z_first=True
        )
        down_sum = Scatter(links, down_keep)
    else:
        down_sends, down_sum = (), PlainScatter(mm(inner_low, cot, TN).astype(BF))
    (
        third_sum.parts, fourth_own, fourth_other, gate_b, up_b, down_sends, down_sum.parts,
        inner_low,
    ) = phase(
        third_sum.parts, fourth_own, fourth_other, gate_b, up_b, down_sends, down_sum.parts,
        inner_low,
    )

    fourth_keep, fourth_send = weight_grad(
        links, [[(normed_three, fourth_own), (normed_other, fourth_other)]]
    )
    third_send, fourth_keep, fourth_send, gate_b, up_b, down_sends = phase(
        third_sum.halve(), fourth_keep, fourth_send, gate_b, up_b, down_sends
    )
    third_sum.far(third_send)
    fourth_sum = Scatter(links, fourth_keep)
    fourth_sum.near(fourth_send)
    down_back, down_ahead = down_sum.z_back(down_sends), down_sum.z_ahead(down_sends)
    grad_normed_three = mm(jnp.concatenate([gate_a, up_a], axis=1), third, NT) + mm(
        jnp.concatenate([gate_b, up_b], axis=1), fourth, NT
    )
    through, grad_gain_ffn = norm_back(hidden_two, gain_ffn, grad_normed_three)
    grad_hidden_two = cot.astype(F32) + through
    low_two = grad_hidden_two.astype(BF)
    (
        grad_cq, grad_ck, grad_cv, memory_part, grad_hidden_one, low_one, grad_attended,
        grad_gain_cross,
    ) = cross_back(
        grad_hidden_two, hidden_one, gain_cross, cross_queries, cross_keys, cross_values, second,
        qseg, mseg,
    )
    half = inner // 2
    (
        third_sum.parts, fourth_sum.parts, down_sends, down_back, down_ahead, grad_cq, grad_ck,
        grad_cv, low_two, low_one, grad_attended, memory_part,
    ) = phase(
        third_sum.parts, fourth_sum.parts, down_sends, down_back, down_ahead, grad_cq, grad_ck,
        grad_cv, low_two, low_one, grad_attended, memory_part,
    )

    cross_acts, cross_acts_sent = choose(normed_two, cross_attended)
    cross_grad, cross_grad_sent = choose(grad_cq, low_two)
    cross_kv, cross_kv_sent = choose(grad_ck, grad_cv)
    cross_sent = jnp.concatenate(
        [cross_acts_sent, cross_grad_sent, cross_kv_sent, attended, low_one], axis=0
    )
    fourth_send, cross_sent, third_sum.parts, memory_part = phase(
        fourth_sum.halve(), cross_sent, third_sum.parts, memory_part
    )
    fourth_sum.far(fourth_send)
    cross_other = links.over_core(cross_sent)
    third_sum.z(third_sum.z_sends())
    memory_rows = SeqScatter(links, memory_part)
    bounds = np.cumsum([rows, rows, enc, rows]).tolist()
    other_acts, other_grad, other_kv, other_attended, other_low = jnp.split(
        cross_other, bounds, axis=0
    )
    low_half = choose(low_one[:, :half], low_one[:, half:])[0]
    other_low = choose(other_low[:, :half], other_low[:, half:])[0]
    cross_keep, cross_send = weight_grad(
        links,
        [
            [(cross_acts, cross_grad), (other_acts, other_grad)],
            [(memory_all, add_low(cross_kv, other_kv))],
            [(attended, low_half), (other_attended, other_low)],
        ],
    )
    (
        cross_keep, cross_send, fourth_sum.parts, third_sum.parts, grad_attended, down_sends,
        down_back, down_ahead, memory_rows.sent, memory_rows.kept,
    ) = phase(
        cross_keep, cross_send, fourth_sum.parts, third_sum.parts, grad_attended, down_sends,
        down_back, down_ahead, memory_rows.sent, memory_rows.kept,
    )

    cross_sum = Scatter(links, cross_keep)
    cross_sum.near(cross_send)
    down_mid, fourth_sends, grad_attended = phase(
        down_sum.z_mid(down_sends, down_ahead), fourth_sum.z_sends(), grad_attended
    )
    down_sum.z_last(down_back, down_mid)
    fourth_sum.z(fourth_sends)
    grad_q, grad_k, grad_v, grad_windows, grad_normed, grad_gain_self = self_back(
        position1, target_all, grad_attended, queries, keys, values, first, windows, qseg, kseg
    )
    (
        cross_sum.parts, down_sum.parts, fourth_sum.parts, third_sum.parts, grad_q, grad_k, grad_v,
        grad_windows, grad_normed, grad_gain_self, memory_rows.sent, memory_rows.kept,
    ) = phase(
        cross_sum.parts, down_sum.parts, fourth_sum.parts, third_sum.parts, grad_q, grad_k, grad_v,
        grad_windows, grad_normed, grad_gain_self, memory_rows.sent, memory_rows.kept,
    )

    cut = inner + half
    self_own, self_sent = choose(
        jnp.concatenate([grad_q, grad_k[:, :half]], axis=1),
        jnp.concatenate([grad_v, grad_k[:, half:]], axis=1),
    )
    (
        cross_send, self_own, self_sent, grad_windows, grad_gain_self, grad_normed,
    ) = phase(
        cross_sum.halve(), self_own, self_sent, grad_windows, grad_gain_self, grad_normed,
    )
    cross_sum.far(cross_send)
    self_other = links.over_core(self_sent)
    normed_rows = SeqScatter(links, grad_normed)
    grad_windows = grad_windows.reshape(heads, rows + length)
    grad_table = lax.dot_general(
        onehot.astype(F32), grad_windows, (((0,), (1,)), ((), ())), precision=lax.Precision.HIGHEST
    )
    grad_table = grad_table.reshape(batch_size, table_rows, seq_size, table_cols)
    grad_table = jnp.transpose(grad_table, (0, 2, 1, 3)).reshape(devices, table_size)
    gain_parts = [g.reshape(devices, weight_rows) for g in (grad_gain_self, grad_gain_cross, grad_gain_ffn)]
    small_grad = jnp.concatenate(gain_parts + [grad_table], axis=1)
    small_grad = jnp.pad(
        small_grad[:, None], ((0, 0), (0, weight_rows - 1), (0, LANES - small_grad.shape[1]))
    ).reshape(devices * weight_rows, LANES)
    small_grad = small_grad.astype(BF)
    small_other = links.over_core(small_grad)
    (
        self_own, self_other, small_grad, small_other, cross_sum.parts, down_sum.parts, fourth_sum.parts,
        third_sum.parts, normed_rows.sent, normed_rows.kept, memory_rows.sent, memory_rows.kept,
        inner_low,
    ) = phase(
        self_own, self_other, small_grad, small_other, cross_sum.parts, down_sum.parts, fourth_sum.parts,
        third_sum.parts, normed_rows.sent, normed_rows.kept, memory_rows.sent, memory_rows.kept,
        inner_low,
    )
    self_keep, self_send = weight_grad(
        links,
        [[(normed_all, add_low(self_own, self_other))]],
        add_low(small_grad, small_other),
    )

    (
        self_keep, self_send, cross_sum.parts, inner_low, third_sum.parts, fourth_sum.parts,
        down_sum.parts, memory_rows.sent, normed_rows.sent,
    ) = phase(
        self_keep, self_send, cross_sum.parts, inner_low, third_sum.parts, fourth_sum.parts,
        down_sum.parts, memory_rows.sent, normed_rows.sent,
    )
    self_sum = Scatter(links, self_keep)
    self_sum.near(self_send)
    cross_sends, down_send = cross_sum.z_sends(), down_sum.halve()
    memory_rows.second()
    down_sum.far(down_send)
    cross_back_z, cross_ahead_z = cross_sum.z_back(cross_sends), cross_sum.z_ahead(cross_sends)
    activations = (hidden_two + mm(inner_low, w_down)).astype(BF)
    third_total = third_sum.own()
    (
        self_sum.parts, cross_back_z, cross_ahead_z, down_sum.parts, activations, third_total,
        fourth_sum.parts, memory_rows.sent, memory_rows.kept, normed_rows.sent, normed_rows.kept,
    ) = phase(
        self_sum.parts, cross_back_z, cross_ahead_z, down_sum.parts, activations, third_total,
        fourth_sum.parts, memory_rows.sent, memory_rows.kept, normed_rows.sent, normed_rows.kept,
    )

    (
        self_send, down_sum.parts, cross_sends, cross_back_z, cross_ahead_z, normed_rows.sent,
        third_total, fourth_sum.parts, memory_rows.sent,
    ) = phase(
        self_sum.halve(), down_sum.parts, cross_sends, cross_back_z, cross_ahead_z,
        normed_rows.sent, third_total, fourth_sum.parts, memory_rows.sent,
    )
    self_sum.far(self_send)
    cross_sum.z_end(cross_sends, cross_back_z, cross_ahead_z)
    down_sum.near(down_sum.halve())
    normed_rows.second()
    memory_grad = memory_rows.total()
    fourth_total = fourth_sum.own()
    (
        self_sum.parts, cross_sum.parts, down_sum.parts, normed_rows.sent, fourth_total,
        memory_grad,
    ) = phase(
        self_sum.parts, cross_sum.parts, down_sum.parts, normed_rows.sent, fourth_total,
        memory_grad,
    )

    self_sends, cross_sum.parts, down_sum.parts, fourth_total, normed_rows.sent = phase(
        self_sum.z_sends(), cross_sum.parts, down_sum.parts, fourth_total, normed_rows.sent
    )
    self_sum.z(self_sends)
    gate_one, up_one = third_sum.last(third_total)
    gate_two, up_two = fourth_sum.last(fourth_total)
    cross_left, cross_right = cross_sum.last(cross_sum.own())
    through, _ = norm_back(target[0].astype(F32), gain_self, normed_rows.total())
    target_grad = grad_hidden_one + through
    down_out = jnp.concatenate(down_sum.last(down_sum.own()), axis=1)
    self_left, self_right = self_sum.last(self_sum.own())
    join = lambda left, right: jnp.concatenate([left, right], axis=1)

    small_out = self_left[0, cut:]
    gain_out = [small_out[i * weight_rows : (i + 1) * weight_rows] for i in range(3)]
    table_out = small_out[3 * weight_rows : 3 * weight_rows + table_size]
    return (
        activations[None],
        target_grad[None],
        memory_grad[None],
        gain_out[0],
        self_left[:, :inner],
        join(self_left[:, inner:cut], self_right[:, inner:cut]),
        self_right[:, :inner],
        join(cross_left[:, 2 * inner :], cross_right[:, 2 * inner :]),
        table_out.reshape(table_rows, table_cols),
        gain_out[1],
        cross_left[:, :inner],
        cross_left[:, inner : 2 * inner],
        cross_right[:, inner : 2 * inner],
        cross_right[:, :inner],
        gain_out[2],
        jnp.concatenate([gate_one, gate_two], axis=1),
        jnp.concatenate([up_one, up_two], axis=1),
        down_out,
    )


def solution(mesh):
    rows3 = P("batch", "seq", None)
    seg = P("batch", None)
    gain = P(AXES)
    weight = P(AXES, None)
    table = P("batch", "seq")
    return jax.shard_map(
        per_device,
        mesh=mesh,
        in_specs=(
            rows3, rows3, rows3, seg, seg, P(),
            gain, weight, weight, weight, weight, table,
            gain, weight, weight, weight, weight,
            gain, weight, weight, weight,
        ),
        out_specs=(
            rows3, rows3, rows3,
            gain, weight, weight, weight, weight, table,
            gain, weight, weight, weight, weight,
            gain, weight, weight, weight,
        ),
        check_vma=False,
    )
```

```python
import functools

import jax
import jax.numpy as jnp
import numpy as np
from jax import lax
from jax.experimental import pallas as pl
from jax.experimental.pallas import tpu as pltpu
from jax.sharding import PartitionSpec as P

HD = 64
LANES = 128
SUBLANES = 8
EPSILON = 1e-06
MASKED = -1e30
BF = jnp.bfloat16
F32 = jnp.float32
AXES = ("batch", "seq")
NT = (((1,), (1,)), ((), ()))
TN = (((0,), (0,)), ((), ()))
NN = (((1,), (0,)), ((), ()))


def mm(left, right, dims=NN):
    return lax.dot_general(left, right, dims, preferred_element_type=F32)


def gated_unit(gate_act, up_act):
    return jax.nn.gelu(gate_act, approximate=True) * up_act


def head_only(pair, head):
    lane = lax.broadcasted_iota(jnp.int32, pair.shape, 1)
    return jnp.where((lane // HD) == head, pair, jnp.zeros_like(pair))


def pick_heads(first, second):
    lane = lax.broadcasted_iota(jnp.int32, first.shape, 1)
    return jnp.where(lane < HD, first, second)


def spread(window, rows):
    wide = jnp.broadcast_to(window, (rows, window.shape[1]))
    rolled = pltpu.roll(wide, 0, 1, stride=1, stride_axis=0)
    return rolled[:, rows:]


def unspread(grads, rows):
    wide = jnp.concatenate([jnp.zeros((rows, rows), F32), grads], axis=1)
    width = wide.shape[1]
    total = wide[:SUBLANES]
    for start in range(SUBLANES, rows, SUBLANES):
        total = total + pltpu.roll(wide[start : start + SUBLANES], width - start, 1)
    row = lax.broadcasted_iota(jnp.int32, total.shape, 0)
    for bit in (1, 2, 4):
        total = jnp.where((row & bit) != 0, pltpu.roll(total, width - bit, 1), total)
    return jnp.sum(total, axis=0, keepdims=True)


def allowed_pairs(position, query_segments, key_segments, causal):
    rows, keys = query_segments.shape[0], key_segments.shape[1]
    allowed = query_segments == key_segments
    if causal:
        own = lax.broadcasted_iota(jnp.int32, (rows, keys), 0) + position
        other = lax.broadcasted_iota(jnp.int32, (rows, keys), 1)
        allowed = allowed & (own >= other)
    return allowed


def pair_probs(query, key, bias_ref, allowed, head, causal):
    scores = mm(head_only(query, head), key, NT)
    if causal:
        scores = scores + spread(bias_ref[0, head : head + 1, :], query.shape[0])
    scores = jnp.where(allowed, scores, MASKED)
    top = jnp.max(scores, axis=1, keepdims=True)
    grown = jnp.exp(scores - top)
    return grown / jnp.sum(grown, axis=1, keepdims=True)


def attend_pair(query, key, value, bias_ref, allowed, causal):
    parts = []
    for head in range(2):
        probs = pair_probs(query, key, bias_ref, allowed, head, causal)
        parts.append(mm(probs.astype(BF), value))
    return pick_heads(*parts).astype(BF)


def attend_pair_back(query, key, value, grad, bias_ref, dbias_ref, allowed, causal):
    grad_query, grad_key, grad_value = [], 0.0, 0.0
    for head in range(2):
        probs = pair_probs(query, key, bias_ref, allowed, head, causal)
        grad_head = head_only(grad, head)
        grad_probs = mm(grad_head, value, NT)
        inner = jnp.sum(probs * grad_probs, axis=1, keepdims=True)
        grad_scores = probs * (grad_probs - inner)
        low_scores = grad_scores.astype(BF)
        grad_query.append(mm(low_scores, key))
        grad_key = grad_key + mm(low_scores, head_only(query, head), TN)
        grad_value = grad_value + mm(probs.astype(BF), grad_head, TN)
        if causal:
            dbias_ref[0, head : head + 1, :] = unspread(grad_scores, query.shape[0])
    return pick_heads(*grad_query).astype(BF), grad_key.astype(BF), grad_value.astype(BF)


def scale_of(values):
    return lax.rsqrt(jnp.mean(values * values, axis=-1, keepdims=True) + EPSILON)


def norm_back(values, gain, grad_out):
    scale = scale_of(values)
    unit = values * scale
    lean = jnp.mean(grad_out * gain * unit, axis=-1, keepdims=True)
    grad_gain = jnp.sum(grad_out * unit, axis=0, keepdims=True)
    return scale * (grad_out * gain - unit * lean), grad_gain


def cost(microseconds):
    return pl.CostEstimate(flops=microseconds * 10**9, bytes_accessed=1, transcendentals=0)


PARAMS = pltpu.CompilerParams(dimension_semantics=("arbitrary",), vmem_limit_bytes=48 << 20)
SMEM = pl.BlockSpec(memory_space=pltpu.SMEM)


def whole(array, rows=None):
    shape = array.shape if rows is None else (rows, array.shape[1])
    return pl.BlockSpec(shape, lambda step: (0,) * len(shape))


def pair_cols(rows, offset=0):
    return pl.BlockSpec((rows, LANES), lambda step: (0, offset + step))


def shape_of(*shape, dtype=BF):
    return jax.ShapeDtypeStruct(shape, dtype)


def windows_spec(windows):
    return pl.BlockSpec((1, 2, windows.shape[2]), lambda step: (step, 0, 0))


def self_forward(place, target_all, gain, weights, windows, qseg, kseg):
    (length, width), rows = target_all.shape, qseg.shape[0]
    inner = windows.shape[0] * LANES
    pairs = inner // LANES

    def body(
        pos_ref, rows_ref, gain_ref, wq_ref, wk_ref, wv_ref, win_ref, qseg_ref, kseg_ref,
        out_ref, q_ref, k_ref, v_ref, normed_ref,
    ):
        position = pl.multiple_of(pos_ref[0], LANES)

        @pl.when(pl.program_id(0) == 0)
        def _():
            values = rows_ref[...].astype(F32)
            normed_ref[...] = (values * scale_of(values) * gain_ref[...]).astype(BF)

        normed = normed_ref[...]
        query = mm(normed_ref[pl.ds(position, rows), :], wq_ref[...]).astype(BF)
        key = mm(normed, wk_ref[...]).astype(BF)
        value = mm(normed, wv_ref[...]).astype(BF)
        q_ref[...], k_ref[...], v_ref[...] = query, key, value
        allowed = allowed_pairs(position, qseg_ref[...], kseg_ref[...], True)
        out_ref[...] = attend_pair(query, key, value, win_ref, allowed, True)

    return pl.pallas_call(
        body,
        grid=(pairs,),
        in_specs=[
            SMEM, whole(target_all), whole(gain),
            pair_cols(width), pair_cols(width, pairs), pair_cols(width, 2 * pairs),
            windows_spec(windows), whole(qseg), whole(kseg),
        ],
        out_specs=[
            pair_cols(rows), pair_cols(rows), pair_cols(length), pair_cols(length),
            whole(target_all),
        ],
        out_shape=[
            shape_of(rows, inner), shape_of(rows, inner), shape_of(length, inner),
            shape_of(length, inner), shape_of(length, width),
        ],
        compiler_params=PARAMS,
        cost_estimate=cost(4),
        name="self_forward",
    )(place, target_all, gain, weights, weights, weights, windows, qseg, kseg)


def self_back(place, target_all, grad, query, key, value, weights, windows, qseg, kseg):
    (length, width), (rows, inner) = target_all.shape, query.shape
    pairs = inner // LANES

    def body(
        pos_ref, rows_ref, do_ref, q_ref, k_ref, v_ref, wq_ref, wk_ref, wv_ref, win_ref,
        qseg_ref, kseg_ref, dq_ref, dk_ref, dv_ref, dwin_ref, back_ref, dgain_ref,
    ):
        step = pl.program_id(0)
        position = pl.multiple_of(pos_ref[0], LANES)
        own = pl.ds(position, rows)
        allowed = allowed_pairs(position, qseg_ref[...], kseg_ref[...], True)
        dq, dk, dv = attend_pair_back(
            q_ref[...], k_ref[...], v_ref[...], do_ref[...], win_ref, dwin_ref, allowed, True
        )
        dq_ref[...] = jnp.zeros_like(dq_ref)
        dq_ref[own, :] = dq
        dk_ref[...], dv_ref[...] = dk, dv
        back = mm(dk, wk_ref[...], NT) + mm(dv, wv_ref[...], NT)

        @pl.when(step == 0)
        def _():
            back_ref[...] = back

        @pl.when(step > 0)
        def _():
            back_ref[...] += back

        back_ref[own, :] += mm(dq, wq_ref[...], NT)

        @pl.when(step == pairs - 1)
        def _():
            values = rows_ref[...].astype(F32)
            dgain_ref[...] = jnp.sum(
                values * scale_of(values) * back_ref[...], axis=0, keepdims=True
            )

    return pl.pallas_call(
        body,
        grid=(pairs,),
        in_specs=[
            SMEM, whole(target_all), pair_cols(rows),
            pair_cols(rows), pair_cols(length), pair_cols(length),
            pair_cols(width), pair_cols(width, pairs), pair_cols(width, 2 * pairs),
            windows_spec(windows), whole(qseg), whole(kseg),
        ],
        out_specs=[
            pair_cols(length), pair_cols(length), pair_cols(length), windows_spec(windows),
            whole(target_all), pl.BlockSpec((1, width), lambda step: (0, 0)),
        ],
        out_shape=[
            shape_of(length, inner), shape_of(length, inner), shape_of(length, inner),
            shape_of(*windows.shape, dtype=F32), shape_of(length, width, dtype=F32),
            shape_of(1, width, dtype=F32),
        ],
        compiler_params=PARAMS,
        cost_estimate=cost(1),
        name="self_back",
    )(place, target_all, grad, query, key, value, weights, weights, weights, windows, qseg, kseg)


def cross_forward(target, attended, memory_all, gain_cross, gain_ffn, weights, qseg, mseg):
    (rows, width), inner, enc = target.shape, attended.shape[1], memory_all.shape[0]
    pairs = inner // LANES

    def body(
        rows_ref, att_ref, mem_ref, gain_ref, gain3_ref, wo_ref, wq_ref, wk_ref, wv_ref, wc_ref,
        qseg_ref, mseg_ref, one_ref, normed_ref, q_ref, k_ref, v_ref, out_ref, two_ref, last_ref,
    ):
        step = pl.program_id(0)

        @pl.when(step == 0)
        def _():
            hidden = rows_ref[...].astype(F32) + mm(att_ref[...], wo_ref[...])
            one_ref[...] = hidden
            two_ref[...] = hidden
            normed_ref[...] = (hidden * scale_of(hidden) * gain_ref[...]).astype(BF)

        query = mm(normed_ref[...], wq_ref[...]).astype(BF)
        key = mm(mem_ref[...], wk_ref[...]).astype(BF)
        value = mm(mem_ref[...], wv_ref[...]).astype(BF)
        q_ref[...], k_ref[...], v_ref[...] = query, key, value
        allowed = allowed_pairs(0, qseg_ref[...], mseg_ref[...], False)
        out = attend_pair(query, key, value, None, allowed, False)
        out_ref[...] = out
        two_ref[...] += mm(out, wc_ref[...])

        @pl.when(step == pairs - 1)
        def _():
            hidden = two_ref[...]
            last_ref[...] = (hidden * scale_of(hidden) * gain3_ref[...]).astype(BF)

    return pl.pallas_call(
        body,
        grid=(pairs,),
        in_specs=[
            whole(target), whole(attended), whole(memory_all), whole(gain_cross), whole(gain_ffn),
            pl.BlockSpec((width, width), lambda step: (0, 0)),
            pair_cols(width, pairs), pair_cols(width, 2 * pairs), pair_cols(width, 3 * pairs),
            pl.BlockSpec((LANES, width), lambda step: (step, 4)),
            whole(qseg), whole(mseg),
        ],
        out_specs=[
            whole(target), whole(target), pair_cols(rows), pair_cols(enc), pair_cols(enc),
            pair_cols(rows), whole(target), whole(target),
        ],
        out_shape=[
            shape_of(rows, width, dtype=F32), shape_of(rows, width), shape_of(rows, inner),
            shape_of(enc, inner), shape_of(enc, inner), shape_of(rows, inner),
            shape_of(rows, width, dtype=F32), shape_of(rows, width),
        ],
        compiler_params=PARAMS,
        cost_estimate=cost(8),
        name="cross_forward",
    )(
        target, attended, memory_all, gain_cross, gain_ffn, weights, weights, weights, weights,
        weights, qseg, mseg,
    )


def cross_back(grad_two, hidden_one, gain, query, key, value, weights, qseg, mseg):
    (rows, width), inner, enc = hidden_one.shape, query.shape[1], key.shape[0]
    pairs = inner // LANES

    def body(
        grad_ref, one_ref, gain_ref, q_ref, k_ref, v_ref, wo_ref, wq_ref, wk_ref, wv_ref, wc_ref,
        qseg_ref, mseg_ref, dq_ref, dk_ref, dv_ref, mem_ref, done_ref, low_ref, datt_ref,
        dgain_ref, two_ref, back_ref,
    ):
        step = pl.program_id(0)

        @pl.when(step == 0)
        def _():
            two_ref[...] = grad_ref[...].astype(BF)

        grad = mm(two_ref[...], wc_ref[...], NT).astype(BF)
        allowed = allowed_pairs(0, qseg_ref[...], mseg_ref[...], False)
        dq, dk, dv = attend_pair_back(
            q_ref[...], k_ref[...], v_ref[...], grad, None, None, allowed, False
        )
        dq_ref[...], dk_ref[...], dv_ref[...] = dq, dk, dv
        back = mm(dq, wq_ref[...], NT)
        memory = mm(dk, wk_ref[...], NT) + mm(dv, wv_ref[...], NT)

        @pl.when(step == 0)
        def _():
            back_ref[...] = back
            mem_ref[...] = memory

        @pl.when(step > 0)
        def _():
            back_ref[...] += back
            mem_ref[...] += memory

        @pl.when(step == pairs - 1)
        def _():
            through, grad_gain = norm_back(one_ref[...], gain_ref[...], back_ref[...])
            grad_one = grad_ref[...] + through
            low = grad_one.astype(BF)
            done_ref[...] = grad_one
            low_ref[...] = low
            dgain_ref[...] = grad_gain
            datt_ref[...] = mm(low, wo_ref[...], NT).astype(BF)

    row = pl.BlockSpec((1, width), lambda step: (0, 0))
    return pl.pallas_call(
        body,
        grid=(pairs,),
        in_specs=[
            whole(grad_two), whole(hidden_one), row,
            pair_cols(rows), pair_cols(enc), pair_cols(enc),
            pl.BlockSpec((width, width), lambda step: (0, 0)),
            pair_cols(width, pairs), pair_cols(width, 2 * pairs), pair_cols(width, 3 * pairs),
            pl.BlockSpec((LANES, width), lambda step: (step, 4)),
            whole(qseg), whole(mseg),
        ],
        out_specs=[
            pair_cols(rows), pair_cols(enc), pair_cols(enc),
            pl.BlockSpec((enc, width), lambda step: (0, 0)),
            whole(hidden_one), whole(hidden_one), whole(hidden_one), row,
        ],
        out_shape=[
            shape_of(rows, inner), shape_of(enc, inner), shape_of(enc, inner),
            shape_of(enc, width, dtype=F32), shape_of(rows, width, dtype=F32),
            shape_of(rows, width), shape_of(rows, inner), shape_of(1, width, dtype=F32),
        ],
        scratch_shapes=[pltpu.VMEM((rows, width), BF), pltpu.VMEM((rows, width), F32)],
        compiler_params=PARAMS,
        cost_estimate=cost(1),
        name="cross_back",
    )(
        grad_two, hidden_one, gain, query, key, value, weights, weights, weights, weights, weights,
        qseg, mseg,
    )


def gather_all(shard):
    return lax.all_gather(shard, AXES, axis=0, tiled=True)


def scatter_all(grads):
    return lax.psum_scatter(grads, AXES, scatter_dimension=0, tiled=True).astype(F32)


class Links:
    def __init__(self):
        self.batch, self.seq = lax.axis_size("batch"), lax.axis_size("seq")
        self.depth = self.batch // 2
        z_x, y_c = lax.axis_index("batch"), lax.axis_index("seq")
        self.z, self.x = z_x // 2, z_x % 2
        self.y, self.core = y_c // 2, y_c % 2
        self.lead = self.core == 0
        self.place = jnp.stack([self.z, self.x, self.y, self.core]).astype(jnp.int32)

    def move(self, value, target):
        pairs = []
        for source in range(self.batch * self.seq):
            z_x, y_c = source // self.seq, source % self.seq
            z, x, y, core = target(z_x // 2, z_x % 2, y_c // 2, y_c % 2)
            pairs.append((source, (z * 2 + x) * self.seq + y * 2 + core))
        return lax.ppermute(value, AXES, pairs)

    def over_core(self, value):
        return self.move(value, lambda z, x, y, core: (z, x, y, 1 - core))

    def over_y(self, value):
        return self.move(value, lambda z, x, y, core: (z, x, 1 - y, core))

    def over_near(self, value):
        return self.move(
            value, lambda z, x, y, c: (z, x, 1 - y, c) if c else (z, 1 - x, y, c)
        )

    def over_far(self, value):
        return self.move(
            value, lambda z, x, y, c: (z, 1 - x, y, c) if c else (z, x, 1 - y, c)
        )

    def over_z(self, value, step):
        depth = self.depth
        return self.move(value, lambda z, x, y, core: ((z - step) % depth, x, y, core))


def in_order(first, own, other):
    return jnp.concatenate([jnp.where(first, own, other), jnp.where(first, other, own)], axis=0)


def gather_core(links, left, right):
    own = jnp.where(links.lead, left, right)
    other = links.over_core(jnp.where(links.lead, right, left))
    return in_order(links.lead, own, other)


def z_steps(links, value, steps):
    return [links.over_z(value, step) for step in steps]


def gather_near(links, value):
    return jnp.stack([value, links.over_near(value)])


def gather_far(links, value):
    return jnp.stack([value, links.over_far(value)])


def assemble(links, *sources):
    count, (rows, cols) = len(sources) // 2, sources[0].shape[-2:]
    depth = links.depth

    def body(place_ref, *refs):
        inputs, out_ref, sem = refs[:-2], refs[-2], refs[-1]
        z, x, y, core = [place_ref[i] for i in range(4)]
        for which, source in enumerate(inputs):
            half = core if which < count else 1 - core
            for near, far, step in np.ndindex(2, 2, depth):
                if count == 2 and far != which % 2:
                    continue
                step_x, step_y = jnp.where(half == 0, near, far), jnp.where(half == 0, far, near)
                chip = (((z + step) % depth) * 2 + (x ^ step_x)) * 2 + (y ^ step_y)
                target = out_ref.at[
                    pl.ds(pl.multiple_of(chip * rows, 16), rows),
                    pl.ds(pl.multiple_of(half * cols, LANES), cols),
                ]
                part = source.at[near, step] if count == 2 else source.at[step, far, near]
                pltpu.make_async_copy(part, target, sem).start()
        pltpu.make_async_copy(out_ref, out_ref, sem).wait()

    return pl.pallas_call(
        body,
        in_specs=[pl.BlockSpec(memory_space=pltpu.SMEM)]
        + [pl.BlockSpec(memory_space=pl.ANY)] * len(sources),
        out_specs=pl.BlockSpec(memory_space=pltpu.VMEM),
        out_shape=jax.ShapeDtypeStruct((depth * 4 * rows, 2 * cols), sources[0].dtype),
        scratch_shapes=[pltpu.SemaphoreType.DMA(())],
        compiler_params=pltpu.CompilerParams(vmem_limit_bytes=48 << 20),
        cost_estimate=cost(1),
        name="assemble",
    )(links.place, *sources)


def weight_grad(links, terms, extra=None, z_first=False):
    depth, total_rows = links.depth, terms[0][0][0].shape[1]
    rows = total_rows // (depth * 4)
    widths = [term[0][1].shape[1] for term in terms]
    extra_width = 0 if extra is None else extra.shape[1]
    total = sum(widths) + extra_width
    tile = 1408 if total % 1408 == 0 else 512
    operands = [array for term in terms for pair in term for array in pair]
    operands += [] if extra is None else [extra]
    amount, pieces = len(operands), depth if z_first else 2
    piece_rows = total_rows // pieces

    def body(place_ref, *refs):
        sources, outs = refs[:amount], refs[amount : amount + pieces]
        stage, sems = refs[amount + pieces], refs[amount + pieces + 1]
        inputs, arrived = refs[amount + pieces + 2 : -1], refs[-1]
        fetches = [
            pltpu.make_async_copy(source, target, arrived.at[index])
            for index, (source, target) in enumerate(zip(sources, inputs))
        ]
        for fetch in fetches:
            fetch.start()
        z, x, y, left = place_ref[0], place_ref[1], place_ref[2], place_ref[3] == 0
        places = []
        for chip in range(depth * 4):
            step_x, step_y = (chip // 2 % 2) ^ x, (chip % 2) ^ y
            near, far = jnp.where(left, step_x, step_y), jnp.where(left, step_y, step_x)
            step = (chip // 4 - z) % depth
            spot = (step * 2 + far) * 2 + near if z_first else (near * 2 + far) * depth + step
            places.append(pl.multiple_of(spot * rows, 8))

        def copy(piece, index, start, width):
            cols = pl.ds(start, width)
            return pltpu.make_async_copy(
                stage.at[pl.ds(piece * piece_rows, piece_rows), cols],
                outs[piece].at[:, cols],
                sems.at[piece, index],
            )

        def emit(index, start, value, width):
            for chip, spot in enumerate(places):
                stage[pl.ds(spot, rows), pl.ds(start, width)] = value[
                    chip * rows : (chip + 1) * rows
                ].astype(BF)
            for piece in range(pieces):
                copy(piece, index, start, width).start()

        begin, first_copy, taken = 0, 0, 0
        for term, width in zip(terms, widths):
            pairs = inputs[taken : taken + 2 * len(term)]
            for fetch in fetches[taken : taken + 2 * len(term)]:
                fetch.wait()
            taken += 2 * len(term)

            def one_tile(index, carry, begin=begin, first_copy=first_copy, pairs=pairs):
                cols = pl.ds(pl.multiple_of(index * tile, LANES), tile)
                value = mm(pairs[0][...], pairs[1][:, cols], TN)
                if len(pairs) == 4:
                    value = value + mm(pairs[2][...], pairs[3][:, cols], TN)
                start = pl.multiple_of(begin + index * tile, LANES)
                emit(first_copy + index, start, value, tile)
                return carry

            lax.fori_loop(0, width // tile, one_tile, 0)
            begin, first_copy = begin + width, first_copy + width // tile
        if extra is not None:
            fetches[-1].wait()
            small = inputs[-1][...]
            emit(first_copy, begin, jnp.where(left, small, jnp.zeros_like(small)), extra_width)
        for piece in range(pieces):
            for index in range(first_copy):
                copy(piece, index, index * tile, tile).wait()
            if extra is not None:
                copy(piece, first_copy, begin, extra_width).wait()

    count = sum(width // tile for width in widths) + (extra is not None)
    hbm = pl.BlockSpec(memory_space=pltpu.HBM)
    return pl.pallas_call(
        body,
        in_specs=[pl.BlockSpec(memory_space=pltpu.SMEM)] + [hbm] * amount,
        out_specs=[pl.BlockSpec(memory_space=pl.ANY)] * pieces,
        out_shape=[jax.ShapeDtypeStruct((piece_rows, total), BF)] * pieces,
        scratch_shapes=[pltpu.VMEM((total_rows, total), BF), pltpu.SemaphoreType.DMA((pieces, count))]
        + [pltpu.VMEM(array.shape, array.dtype) for array in operands]
        + [pltpu.SemaphoreType.DMA((amount,))],
        compiler_params=pltpu.CompilerParams(vmem_limit_bytes=48 << 20),
        cost_estimate=cost(1),
        name="weight_grad",
    )(links.place, *operands)


def add_low(one, other):
    return (one.astype(F32) + other.astype(F32)).astype(BF)


class Scatter:
    def __init__(self, links, kept):
        self.links, self.parts, self.rows = links, [kept], kept.shape[0]

    def total(self, start, count):
        return sum(part[start : start + count].astype(F32) for part in self.parts)

    def halve(self):
        self.rows //= 2
        return self.total(self.rows, self.rows).astype(BF)

    def near(self, send):
        self.parts.append(self.links.over_near(send))

    def far(self, send):
        self.parts.append(self.links.over_far(send))

    def z_sends(self):
        self.rows //= self.links.depth
        return [
            self.total(step * self.rows, self.rows).astype(BF)
            for step in range(1, self.links.depth)
        ]

    def z(self, sends):
        depth = self.links.depth
        for step, send in enumerate(sends, 1):
            self.parts.append(self.links.over_z(send, depth - step))

    def z_back(self, sends):
        return self.links.over_z(sends[-1], 1)

    def z_ahead(self, sends):
        return self.links.over_z(sends[-2], self.links.depth - 1)

    def z_mid(self, sends, ahead):
        for send in sends[-3:0:-1]:
            ahead = self.links.over_z(add_low(ahead, send), self.links.depth - 1)
        return add_low(ahead, sends[0])

    def z_last(self, back, ahead):
        self.parts += [back, self.links.over_z(ahead, self.links.depth - 1)]

    def z_end(self, sends, back, ahead):
        self.z_last(back, self.z_mid(sends, ahead))

    def own(self):
        return self.total(0, self.rows)

    def last(self, total):
        links, half = self.links, self.rows // 2
        above, below = total[:half], total[half:]
        own = jnp.where(links.lead, above, below)
        other = links.over_core(jnp.where(links.lead, below, above))
        return jnp.where(links.lead, own, other), jnp.where(links.lead, other, own)


class SeqScatter:
    def __init__(self, links, parts):
        self.links = links
        parts = parts.reshape(2, 2, -1, parts.shape[1])
        take = lambda core: lax.dynamic_index_in_dim(parts, core, 1, False)
        self.kept = take(links.core)
        self.sent = links.over_core(take(1 - links.core).astype(BF))

    def second(self):
        total = self.kept + self.sent.astype(F32)
        take = lambda y: lax.dynamic_index_in_dim(total, y, 0, False)
        self.kept = take(self.links.y)
        self.sent = self.links.over_y(take(1 - self.links.y).astype(BF))

    def total(self):
        return self.kept + self.sent.astype(F32)


class PlainScatter:
    parts = ()

    def __init__(self, kept):
        self.kept = kept

    def halve(self):
        return ()

    def near(self, send):
        pass

    def z_mid(self, sends, ahead):
        return ()

    def z_last(self, back, ahead):
        pass

    def z_back(self, sends):
        return ()

    far, own, z_ahead = near, halve, z_back

    def last(self, total):
        return jnp.split(scatter_all(self.kept), 2, axis=1)


def phase(*values):
    return lax.optimization_barrier(values)


def per_device(
    target, memory, cotangent, target_segments, memory_segments, bucket_ids,
    self_norm_gain, self_query, self_key, self_value, self_output, bias_table,
    cross_norm_gain, cross_query, cross_key, cross_value, cross_output,
    ffn_norm_gain, ffn_gate, ffn_up, ffn_down,
):
    batch_size, seq_size = lax.axis_size("batch"), lax.axis_size("seq")
    devices = batch_size * seq_size
    seq_index = lax.axis_index("seq")
    rows, width = target.shape[1], target.shape[2]
    length, enc = target_segments.shape[1], memory_segments.shape[1]
    enc_rows = memory.shape[1]
    inner = self_query.shape[1]
    hidden = ffn_gate.shape[1]
    table_rows, table_cols = bias_table.shape
    weight_rows = self_query.shape[0]
    table_size = table_rows * table_cols

    links = Links()
    core, lead, depth = links.core, links.lead, links.depth
    small = jnp.concatenate(
        [self_norm_gain, cross_norm_gain, ffn_norm_gain, bias_table.reshape(-1)]
    )
    small = jnp.pad(small[None], ((0, weight_rows - 1), (0, 2 * LANES - small.shape[0])))
    part = hidden // 2
    groups = [
        [self_query, self_key, self_value, small],
        [self_output, cross_query, cross_key, cross_value, cross_output],
        [ffn_gate[:, :part], ffn_up[:, :part]],
        [ffn_gate[:, part:], ffn_up[:, part:]],
    ]
    groups = [jnp.concatenate(group, axis=1) for group in groups]
    cuts = [group.shape[1] // 2 for group in groups]
    left = jnp.concatenate([group[:, :cut] for group, cut in zip(groups, cuts)], axis=1)
    right = jnp.concatenate([group[:, cut:] for group, cut in zip(groups, cuts)], axis=1)
    down_cut = width // 2
    steps = list(range(1, depth))
    z_one, z_two, z_three = steps[:1], steps[-1:] if depth > 2 else [], steps[1:-1]
    direct = 2 * ffn_down.shape[0] % 16 == 0
    move = lambda function, *args: function(links, *args) if direct else None

    moved = gather_core(links, left, right)
    down = move(gather_core, ffn_down[:, :down_cut], ffn_down[:, down_cut:])
    if not direct:
        down_whole = gather_all(ffn_down)
    moved, down = phase(moved, down)
    ends = list(np.cumsum(cuts))
    first0, second0, gated0 = jnp.split(moved, ends[:2], axis=1)

    first_z = jnp.stack([first0] + z_steps(links, first0, steps))
    first_z, second0, down = phase(first_z, second0, down)

    first_near = gather_near(links, first_z)
    down = move(gather_near, down)
    second_one, second_two = z_steps(links, second0, z_one), z_steps(links, second0, z_two)
    rows_own = jnp.concatenate([target[0], memory[0]], axis=0)
    rows_other = links.over_y(rows_own)
    first_near, down, second_one, second_two, second0, rows_own, rows_other = phase(
        first_near, down, second_one, second_two, second0, rows_own, rows_other
    )

    first_far = links.over_far(first_near)
    first_near_other = links.over_core(first_near)
    second_three = []
    for step in z_three:
        second_three.append(links.over_z((second_one + second_three)[-1], 1))
    second_z = jnp.stack([second0] + second_one + second_three + second_two)
    rows_pair = in_order(links.y == 0, rows_own, rows_other)
    rows_other = links.over_core(rows_pair)
    first_far, first_near_other, second_z, down, gated0, rows_pair, rows_other, bucket_ids = phase(
        first_far, first_near_other, second_z, down, gated0, rows_pair, rows_other, bucket_ids
    )
    by_y = lambda both: both.reshape(2, 1, rows + enc_rows, width)
    both = jnp.concatenate(
        [
            jnp.where(lead, by_y(rows_pair), by_y(rows_other)),
            jnp.where(lead, by_y(rows_other), by_y(rows_pair)),
        ],
        axis=1,
    )
    target_all = both[:, :, :rows].reshape(length, width)
    memory_all = both[:, :, rows:].reshape(enc, width)

    position = seq_index * rows
    heads = seq_size * table_cols
    distance = position + rows - jnp.arange(rows + length, dtype=jnp.int32)
    near = (distance >= 0) & (distance < length)
    bucket = jnp.take(bucket_ids, jnp.clip(distance, 0, length - 1))
    bucket_range = jnp.arange(batch_size * table_rows, dtype=jnp.int32)
    onehot = ((bucket[:, None] == bucket_range[None, :]) & near[:, None]).astype(BF)

    second_near = gather_near(links, second_z)
    gated0, down, target_all, memory_all = phase(gated0, down, target_all, memory_all)
    gated_z = jnp.stack([gated0] + z_steps(links, gated0, steps))
    third_z, fourth_z = gated_z[..., : cuts[2]], gated_z[..., cuts[2] :]
    first_far_other = links.over_core(first_far)
    down = move(gather_far, down)
    (
        first_far_other, second_near, third_z, fourth_z, down, target_all, memory_all, onehot,
    ) = phase(
        first_far_other, second_near, third_z, fourth_z, down, target_all, memory_all, onehot,
    )

    second_far = links.over_far(second_near)
    second_near_other = links.over_core(second_near)
    third_near = gather_near(links, third_z)
    down_one, down_two = move(z_steps, down, z_one), move(z_steps, down, z_two)
    first = assemble(links, first_near, first_far, first_near_other, first_far_other)
    smalls = first[:, 3 * inner :].reshape(devices, weight_rows, 2 * LANES)[:, 0, :].astype(F32)
    gains = [smalls[:, i * weight_rows : (i + 1) * weight_rows].reshape(1, width) for i in range(3)]
    gain_self, gain_cross, gain_ffn = gains
    table = smalls[:, 3 * weight_rows : 3 * weight_rows + table_size]
    table = table.reshape(batch_size, seq_size, table_rows, table_cols)
    table = jnp.transpose(table, (0, 2, 1, 3)).reshape(batch_size * table_rows, seq_size * table_cols)

    windows = mm(table.astype(BF), onehot, (((0,), (1,)), ((), ())))
    windows = windows.reshape(heads // 2, 2, rows + length)
    position1 = position.reshape(1)
    qseg = lax.dynamic_slice_in_dim(target_segments, position, rows, 1).reshape(rows, 1)
    kseg, mseg = target_segments, memory_segments

    attended, queries, keys, values, normed_all = self_forward(
        position1, target_all, gain_self, first, windows, qseg, kseg
    )
    attended, second_far, second_near_other, third_near, fourth_z, down, down_one, down_two = phase(
        attended, second_far, second_near_other, third_near, fourth_z, down, down_one, down_two
    )

    third_far = links.over_far(third_near)
    third_near_other = links.over_core(third_near)
    fourth_near = links.over_near(fourth_z)
    down_three = []
    for step in z_three:
        down_three.append(links.over_z((down_one + down_three)[-1], 1) if direct else None)
    second = assemble(
        links, second_near, second_far, second_near_other, links.over_core(second_far)
    )
    (
        hidden_one, normed_two, cross_queries, cross_keys, cross_values, cross_attended,
        hidden_two, normed_three,
    ) = cross_forward(
        target[0], attended, memory_all, gain_cross, gain_ffn, second, qseg, mseg
    )
    choose = lambda left, right: (jnp.where(lead, left, right), jnp.where(lead, right, left))
    cot = cotangent[0]
    cot_own, cot_sent = choose(cot[:, :down_cut], cot[:, down_cut:])
    cot_other = links.over_core(cot_sent)
    (
        normed_three, third_far, third_near_other, fourth_z, fourth_near, down, down_one, down_two,
        down_three, cot_other,
    ) = phase(
        normed_three, third_far, third_near_other, fourth_z, fourth_near, down, down_one, down_two,
        down_three, cot_other,
    )

    fourth_near = jnp.stack([fourth_z, fourth_near])
    fourth_far = links.over_far(fourth_near)
    if direct:
        down = jnp.stack([down] + down_one + down_three + down_two)
    third_far_other, down, fourth_later = phase(links.over_core(third_far), down, fourth_near)
    down_other = links.over_core(down) if direct else None
    fourth_near_other = links.over_core(fourth_later)
    third = assemble(links, third_near, third_far, third_near_other, third_far_other)
    third_gate_up = mm(normed_three, third)
    if direct:
        w_down = assemble(links, down, down_other)
    else:
        w_down = down_whole
    third_gate_up, fourth_far, fourth_near_other, w_down, normed_three = phase(
        third_gate_up, fourth_far, fourth_near_other, w_down, normed_three
    )

    fourth_far_other = links.over_core(fourth_far)
    normed_other = links.over_core(normed_three)
    def gated(gate_up, start):
        inner_act, pull = jax.vjp(gated_unit, gate_up[:, :part], gate_up[:, part:])
        grad_gate, grad_up = pull(mm(cot, w_down[start : start + part], NT))
        return inner_act.astype(BF), grad_gate.astype(BF), grad_up.astype(BF)

    inner_a, gate_a, up_a = gated(third_gate_up, 0)
    third_own, third_sent = choose(gate_a, up_a)
    third_own, third_sent, inner_a, fourth_far_other, normed_other = phase(
        third_own, third_sent, inner_a, fourth_far_other, normed_other
    )

    third_other = links.over_core(third_sent)
    inner_a_other = links.over_core(inner_a)
    fourth = assemble(links, fourth_near, fourth_far, fourth_near_other, fourth_far_other)
    third_other, inner_a_other, fourth = phase(third_other, inner_a_other, fourth)
    third_keep, third_send = weight_grad(
        links, [[(normed_three, third_own), (normed_other, third_other)]]
    )

    third_keep, third_send, fourth = phase(third_keep, third_send, fourth)
    third_sum = Scatter(links, third_keep)
    third_sum.near(third_send)
    inner_b, gate_b, up_b = gated(mm(normed_three, fourth), part)
    fourth_own, fourth_sent = choose(gate_b, up_b)
    fourth_other = links.over_core(fourth_sent)
    inner_b_other = links.over_core(inner_b)
    inner_low = jnp.concatenate([inner_a, inner_b], axis=1)
    inner_other = jnp.concatenate([inner_a_other, inner_b_other], axis=1)
    if direct:
        down_keep, *down_sends = weight_grad(
            links, [[(inner_low, cot_own), (inner_other, cot_other)]], z_first=True
        )
        down_sum = Scatter(links, down_keep)
    else:
        down_sends, down_sum = (), PlainScatter(mm(inner_low, cot, TN).astype(BF))
    (
        third_sum.parts, fourth_own, fourth_other, gate_b, up_b, down_sends, down_sum.parts,
        inner_low,
    ) = phase(
        third_sum.parts, fourth_own, fourth_other, gate_b, up_b, down_sends, down_sum.parts,
        inner_low,
    )

    fourth_keep, fourth_send = weight_grad(
        links, [[(normed_three, fourth_own), (normed_other, fourth_other)]]
    )
    third_send, fourth_keep, fourth_send, gate_b, up_b, down_sends = phase(
        third_sum.halve(), fourth_keep, fourth_send, gate_b, up_b, down_sends
    )
    third_sum.far(third_send)
    fourth_sum = Scatter(links, fourth_keep)
    fourth_sum.near(fourth_send)
    down_back, down_ahead = down_sum.z_back(down_sends), down_sum.z_ahead(down_sends)
    grad_normed_three = mm(jnp.concatenate([gate_a, up_a], axis=1), third, NT) + mm(
        jnp.concatenate([gate_b, up_b], axis=1), fourth, NT
    )
    through, grad_gain_ffn = norm_back(hidden_two, gain_ffn, grad_normed_three)
    grad_hidden_two = cot.astype(F32) + through
    low_two = grad_hidden_two.astype(BF)
    (
        grad_cq, grad_ck, grad_cv, memory_part, grad_hidden_one, low_one, grad_attended,
        grad_gain_cross,
    ) = cross_back(
        grad_hidden_two, hidden_one, gain_cross, cross_queries, cross_keys, cross_values, second,
        qseg, mseg,
    )
    half = inner // 2
    (
        third_sum.parts, fourth_sum.parts, down_sends, down_back, down_ahead, grad_cq, grad_ck,
        grad_cv, low_two, low_one, grad_attended, memory_part,
    ) = phase(
        third_sum.parts, fourth_sum.parts, down_sends, down_back, down_ahead, grad_cq, grad_ck,
        grad_cv, low_two, low_one, grad_attended, memory_part,
    )

    cross_acts, cross_acts_sent = choose(normed_two, cross_attended)
    cross_grad, cross_grad_sent = choose(grad_cq, low_two)
    cross_kv, cross_kv_sent = choose(grad_ck, grad_cv)
    cross_sent = jnp.concatenate(
        [cross_acts_sent, cross_grad_sent, cross_kv_sent, attended, low_one], axis=0
    )
    fourth_send, cross_sent, third_sum.parts, memory_part = phase(
        fourth_sum.halve(), cross_sent, third_sum.parts, memory_part
    )
    fourth_sum.far(fourth_send)
    cross_other = links.over_core(cross_sent)
    third_sum.z(third_sum.z_sends())
    memory_rows = SeqScatter(links, memory_part)
    bounds = np.cumsum([rows, rows, enc, rows]).tolist()
    other_acts, other_grad, other_kv, other_attended, other_low = jnp.split(
        cross_other, bounds, axis=0
    )
    low_half = choose(low_one[:, :half], low_one[:, half:])[0]
    other_low = choose(other_low[:, :half], other_low[:, half:])[0]
    cross_keep, cross_send = weight_grad(
        links,
        [
            [(cross_acts, cross_grad), (other_acts, other_grad)],
            [(memory_all, add_low(cross_kv, other_kv))],
            [(attended, low_half), (other_attended, other_low)],
        ],
    )
    (
        cross_keep, cross_send, fourth_sum.parts, third_sum.parts, grad_attended, down_sends,
        down_back, down_ahead, memory_rows.sent, memory_rows.kept,
    ) = phase(
        cross_keep, cross_send, fourth_sum.parts, third_sum.parts, grad_attended, down_sends,
        down_back, down_ahead, memory_rows.sent, memory_rows.kept,
    )

    cross_sum = Scatter(links, cross_keep)
    cross_sum.near(cross_send)
    down_mid, memory_rows.sent, grad_attended = phase(
        down_sum.z_mid(down_sends, down_ahead), memory_rows.sent, grad_attended
    )
    down_sum.z_last(down_back, down_mid)
    memory_rows.second()
    grad_q, grad_k, grad_v, grad_windows, grad_normed, grad_gain_self = self_back(
        position1, target_all, grad_attended, queries, keys, values, first, windows, qseg, kseg
    )
    (
        cross_sum.parts, down_sum.parts, fourth_sum.parts, third_sum.parts, grad_q, grad_k, grad_v,
        grad_windows, grad_normed, grad_gain_self, memory_rows.sent, memory_rows.kept,
    ) = phase(
        cross_sum.parts, down_sum.parts, fourth_sum.parts, third_sum.parts, grad_q, grad_k, grad_v,
        grad_windows, grad_normed, grad_gain_self, memory_rows.sent, memory_rows.kept,
    )

    cut = inner + half
    self_own, self_sent = choose(
        jnp.concatenate([grad_q, grad_k[:, :half]], axis=1),
        jnp.concatenate([grad_v, grad_k[:, half:]], axis=1),
    )
    (
        cross_send, self_own, self_sent, grad_windows, grad_gain_self, fourth_sum.parts,
    ) = phase(
        cross_sum.halve(), self_own, self_sent, grad_windows, grad_gain_self, fourth_sum.parts,
    )
    cross_sum.far(cross_send)
    fourth_sends = fourth_sum.z_sends()
    fourth_back, fourth_ahead = fourth_sum.z_back(fourth_sends), fourth_sum.z_ahead(fourth_sends)
    self_other = links.over_core(self_sent)
    grad_windows = grad_windows.reshape(heads, rows + length)
    grad_table = lax.dot_general(
        onehot.astype(F32), grad_windows, (((0,), (1,)), ((), ())), precision=lax.Precision.HIGHEST
    )
    grad_table = grad_table.reshape(batch_size, table_rows, seq_size, table_cols)
    grad_table = jnp.transpose(grad_table, (0, 2, 1, 3)).reshape(devices, table_size)
    gain_parts = [g.reshape(devices, weight_rows) for g in (grad_gain_self, grad_gain_cross, grad_gain_ffn)]
    small_grad = jnp.concatenate(gain_parts + [grad_table], axis=1)
    small_grad = jnp.pad(
        small_grad[:, None], ((0, 0), (0, weight_rows - 1), (0, LANES - small_grad.shape[1]))
    ).reshape(devices * weight_rows, LANES)
    small_grad = small_grad.astype(BF)
    small_other = links.over_core(small_grad)
    (
        self_own, self_other, small_grad, small_other, cross_sum.parts, down_sum.parts,
        fourth_sends, fourth_back, fourth_ahead, third_sum.parts, grad_normed, memory_rows.sent,
        memory_rows.kept, inner_low,
    ) = phase(
        self_own, self_other, small_grad, small_other, cross_sum.parts, down_sum.parts,
        fourth_sends, fourth_back, fourth_ahead, third_sum.parts, grad_normed, memory_rows.sent,
        memory_rows.kept, inner_low,
    )
    self_keep, self_send = weight_grad(
        links,
        [[(normed_all, add_low(self_own, self_other))]],
        add_low(small_grad, small_other),
    )

    (
        self_keep, self_send, cross_sum.parts, inner_low, third_sum.parts, fourth_sends,
        fourth_back, fourth_ahead, down_sum.parts, memory_rows.sent, grad_normed,
    ) = phase(
        self_keep, self_send, cross_sum.parts, inner_low, third_sum.parts, fourth_sends,
        fourth_back, fourth_ahead, down_sum.parts, memory_rows.sent, grad_normed,
    )
    self_sum = Scatter(links, self_keep)
    self_sum.near(self_send)
    cross_sends = cross_sum.z_sends()
    fourth_sum.z_end(fourth_sends, fourth_back, fourth_ahead)
    normed_rows = SeqScatter(links, grad_normed)
    memory_grad = memory_rows.total()
    cross_back_z, cross_ahead_z = cross_sum.z_back(cross_sends), cross_sum.z_ahead(cross_sends)
    activations = (hidden_two + mm(inner_low, w_down)).astype(BF)
    third_total = third_sum.own()
    (
        self_sum.parts, cross_back_z, cross_ahead_z, down_sum.parts, activations, third_total,
        fourth_sum.parts, memory_grad, normed_rows.sent, normed_rows.kept,
    ) = phase(
        self_sum.parts, cross_back_z, cross_ahead_z, down_sum.parts, activations, third_total,
        fourth_sum.parts, memory_grad, normed_rows.sent, normed_rows.kept,
    )

    (
        self_send, down_sum.parts, cross_sends, cross_back_z, cross_ahead_z, normed_rows.sent,
        third_total, fourth_sum.parts,
    ) = phase(
        self_sum.halve(), down_sum.parts, cross_sends, cross_back_z, cross_ahead_z,
        normed_rows.sent, third_total, fourth_sum.parts,
    )
    self_sum.far(self_send)
    cross_sum.z_end(cross_sends, cross_back_z, cross_ahead_z)
    down_sum.far(down_sum.halve())
    normed_rows.second()
    fourth_total = fourth_sum.own()
    (
        self_sum.parts, cross_sum.parts, down_sum.parts, normed_rows.sent, fourth_total,
    ) = phase(
        self_sum.parts, cross_sum.parts, down_sum.parts, normed_rows.sent, fourth_total,
    )

    self_sends, cross_sum.parts, down_sum.parts, fourth_total, normed_rows.sent = phase(
        self_sum.z_sends(), cross_sum.parts, down_sum.parts, fourth_total, normed_rows.sent
    )
    self_sum.z(self_sends)
    down_sum.near(down_sum.halve())
    gate_one, up_one = third_sum.last(third_total)
    gate_two, up_two = fourth_sum.last(fourth_total)
    cross_left, cross_right = cross_sum.last(cross_sum.own())
    through, _ = norm_back(target[0].astype(F32), gain_self, normed_rows.total())
    target_grad = grad_hidden_one + through
    down_out = jnp.concatenate(down_sum.last(down_sum.own()), axis=1)
    self_left, self_right = self_sum.last(self_sum.own())
    join = lambda left, right: jnp.concatenate([left, right], axis=1)

    small_out = self_left[0, cut:]
    gain_out = [small_out[i * weight_rows : (i + 1) * weight_rows] for i in range(3)]
    table_out = small_out[3 * weight_rows : 3 * weight_rows + table_size]
    return (
        activations[None],
        target_grad[None],
        memory_grad[None],
        gain_out[0],
        self_left[:, :inner],
        join(self_left[:, inner:cut], self_right[:, inner:cut]),
        self_right[:, :inner],
        join(cross_left[:, 2 * inner :], cross_right[:, 2 * inner :]),
        table_out.reshape(table_rows, table_cols),
        gain_out[1],
        cross_left[:, :inner],
        cross_left[:, inner : 2 * inner],
        cross_right[:, inner : 2 * inner],
        cross_right[:, :inner],
        gain_out[2],
        jnp.concatenate([gate_one, gate_two], axis=1),
        jnp.concatenate([up_one, up_two], axis=1),
        down_out,
    )


def solution(mesh):
    rows3 = P("batch", "seq", None)
    seg = P("batch", None)
    gain = P(AXES)
    weight = P(AXES, None)
    table = P("batch", "seq")
    return jax.shard_map(
        per_device,
        mesh=mesh,
        in_specs=(
            rows3, rows3, rows3, seg, seg, P(),
            gain, weight, weight, weight, weight, table,
            gain, weight, weight, weight, weight,
            gain, weight, weight, weight,
        ),
        out_specs=(
            rows3, rows3, rows3,
            gain, weight, weight, weight, weight, table,
            gain, weight, weight, weight, weight,
            gain, weight, weight, weight,
        ),
        check_vma=False,
    )
```

```python
import functools

import jax
import jax.numpy as jnp
import numpy as np
from jax import lax
from jax.experimental import pallas as pl
from jax.experimental.pallas import tpu as pltpu
from jax.sharding import PartitionSpec as P

HD = 64
LANES = 128
SUBLANES = 8
EPSILON = 1e-06
MASKED = -1e30
BF = jnp.bfloat16
F32 = jnp.float32
AXES = ("batch", "seq")
NT = (((1,), (1,)), ((), ()))
TN = (((0,), (0,)), ((), ()))
NN = (((1,), (0,)), ((), ()))


def mm(left, right, dims=NN):
    return lax.dot_general(left, right, dims, preferred_element_type=F32)


def gated_unit(gate_act, up_act):
    return jax.nn.gelu(gate_act, approximate=True) * up_act


def head_only(pair, head):
    lane = lax.broadcasted_iota(jnp.int32, pair.shape, 1)
    return jnp.where((lane // HD) == head, pair, jnp.zeros_like(pair))


def pick_heads(first, second):
    lane = lax.broadcasted_iota(jnp.int32, first.shape, 1)
    return jnp.where(lane < HD, first, second)


def spread(window, rows):
    wide = jnp.broadcast_to(window, (rows, window.shape[1]))
    rolled = pltpu.roll(wide, 0, 1, stride=1, stride_axis=0)
    return rolled[:, rows:]


def unspread(grads, rows):
    wide = jnp.concatenate([jnp.zeros((rows, rows), F32), grads], axis=1)
    width = wide.shape[1]
    total = wide[:SUBLANES]
    for start in range(SUBLANES, rows, SUBLANES):
        total = total + pltpu.roll(wide[start : start + SUBLANES], width - start, 1)
    row = lax.broadcasted_iota(jnp.int32, total.shape, 0)
    for bit in (1, 2, 4):
        total = jnp.where((row & bit) != 0, pltpu.roll(total, width - bit, 1), total)
    return jnp.sum(total, axis=0, keepdims=True)


def allowed_pairs(position, query_segments, key_segments, causal):
    rows, keys = query_segments.shape[0], key_segments.shape[1]
    allowed = query_segments == key_segments
    if causal:
        own = lax.broadcasted_iota(jnp.int32, (rows, keys), 0) + position
        other = lax.broadcasted_iota(jnp.int32, (rows, keys), 1)
        allowed = allowed & (own >= other)
    return allowed


def pair_probs(query, key, bias_ref, allowed, head, causal):
    scores = mm(head_only(query, head), key, NT)
    if causal:
        scores = scores + spread(bias_ref[0, head : head + 1, :], query.shape[0])
    scores = jnp.where(allowed, scores, MASKED)
    top = jnp.max(scores, axis=1, keepdims=True)
    grown = jnp.exp(scores - top)
    return grown * (1.0 / jnp.sum(grown, axis=1, keepdims=True))


def attend_pair(query, key, value, bias_ref, allowed, causal):
    parts = []
    for head in range(2):
        probs = pair_probs(query, key, bias_ref, allowed, head, causal)
        parts.append(mm(probs.astype(BF), value))
    return pick_heads(*parts).astype(BF)


def attend_pair_back(query, key, value, grad, bias_ref, dbias_ref, allowed, causal):
    grad_query, grad_key, grad_value = [], 0.0, 0.0
    for head in range(2):
        probs = pair_probs(query, key, bias_ref, allowed, head, causal)
        grad_head = head_only(grad, head)
        grad_probs = mm(grad_head, value, NT)
        inner = jnp.sum(probs * grad_probs, axis=1, keepdims=True)
        grad_scores = probs * (grad_probs - inner)
        low_scores = grad_scores.astype(BF)
        grad_query.append(mm(low_scores, key))
        grad_key = grad_key + mm(low_scores, head_only(query, head), TN)
        grad_value = grad_value + mm(probs.astype(BF), grad_head, TN)
        if causal:
            dbias_ref[0, head : head + 1, :] = unspread(grad_scores, query.shape[0])
    return pick_heads(*grad_query).astype(BF), grad_key.astype(BF), grad_value.astype(BF)


def scale_of(values):
    return lax.rsqrt(jnp.mean(values * values, axis=-1, keepdims=True) + EPSILON)


def norm_back(values, gain, grad_out):
    scale = scale_of(values)
    unit = values * scale
    lean = jnp.mean(grad_out * gain * unit, axis=-1, keepdims=True)
    grad_gain = jnp.sum(grad_out * unit, axis=0, keepdims=True)
    return scale * (grad_out * gain - unit * lean), grad_gain


def cost(microseconds):
    return pl.CostEstimate(flops=microseconds * 10**9, bytes_accessed=1, transcendentals=0)


PARAMS = pltpu.CompilerParams(dimension_semantics=("arbitrary",), vmem_limit_bytes=48 << 20)
SMEM = pl.BlockSpec(memory_space=pltpu.SMEM)


def whole(array, rows=None):
    shape = array.shape if rows is None else (rows, array.shape[1])
    return pl.BlockSpec(shape, lambda step: (0,) * len(shape))


def pair_cols(rows, offset=0):
    return pl.BlockSpec((rows, LANES), lambda step: (0, offset + step))


def shape_of(*shape, dtype=BF):
    return jax.ShapeDtypeStruct(shape, dtype)


def windows_spec(windows):
    return pl.BlockSpec((1, 2, windows.shape[2]), lambda step: (step, 0, 0))


def self_forward(place, target_all, gain, weights, windows, qseg, kseg):
    (length, width), rows = target_all.shape, qseg.shape[0]
    inner = windows.shape[0] * LANES
    pairs = inner // LANES

    def body(
        pos_ref, rows_ref, gain_ref, wq_ref, wk_ref, wv_ref, win_ref, qseg_ref, kseg_ref,
        out_ref, q_ref, k_ref, v_ref, normed_ref,
    ):
        position = pl.multiple_of(pos_ref[0], LANES)

        @pl.when(pl.program_id(0) == 0)
        def _():
            values = rows_ref[...].astype(F32)
            normed_ref[...] = (values * scale_of(values) * gain_ref[...]).astype(BF)

        normed = normed_ref[...]
        query = mm(normed_ref[pl.ds(position, rows), :], wq_ref[...]).astype(BF)
        key = mm(normed, wk_ref[...]).astype(BF)
        value = mm(normed, wv_ref[...]).astype(BF)
        q_ref[...], k_ref[...], v_ref[...] = query, key, value
        allowed = allowed_pairs(position, qseg_ref[...], kseg_ref[...], True)
        out_ref[...] = attend_pair(query, key, value, win_ref, allowed, True)

    return pl.pallas_call(
        body,
        grid=(pairs,),
        in_specs=[
            SMEM, whole(target_all), whole(gain),
            pair_cols(width), pair_cols(width, pairs), pair_cols(width, 2 * pairs),
            windows_spec(windows), whole(qseg), whole(kseg),
        ],
        out_specs=[
            pair_cols(rows), pair_cols(rows), pair_cols(length), pair_cols(length),
            whole(target_all),
        ],
        out_shape=[
            shape_of(rows, inner), shape_of(rows, inner), shape_of(length, inner),
            shape_of(length, inner), shape_of(length, width),
        ],
        compiler_params=PARAMS,
        cost_estimate=cost(4),
        name="self_forward",
    )(place, target_all, gain, weights, weights, weights, windows, qseg, kseg)


def self_back(place, target_all, grad, query, key, value, weights, windows, qseg, kseg):
    (length, width), (rows, inner) = target_all.shape, query.shape
    pairs = inner // LANES

    def body(
        pos_ref, rows_ref, do_ref, q_ref, k_ref, v_ref, wq_ref, wk_ref, wv_ref, win_ref,
        qseg_ref, kseg_ref, dq_ref, dk_ref, dv_ref, dwin_ref, back_ref, dgain_ref,
    ):
        step = pl.program_id(0)
        position = pl.multiple_of(pos_ref[0], LANES)
        own = pl.ds(position, rows)
        allowed = allowed_pairs(position, qseg_ref[...], kseg_ref[...], True)
        dq, dk, dv = attend_pair_back(
            q_ref[...], k_ref[...], v_ref[...], do_ref[...], win_ref, dwin_ref, allowed, True
        )
        dq_ref[...] = jnp.zeros_like(dq_ref)
        dq_ref[own, :] = dq
        dk_ref[...], dv_ref[...] = dk, dv
        back = mm(dk, wk_ref[...], NT) + mm(dv, wv_ref[...], NT)

        @pl.when(step == 0)
        def _():
            back_ref[...] = back

        @pl.when(step > 0)
        def _():
            back_ref[...] += back

        back_ref[own, :] += mm(dq, wq_ref[...], NT)

        @pl.when(step == pairs - 1)
        def _():
            values = rows_ref[...].astype(F32)
            dgain_ref[...] = jnp.sum(
                values * scale_of(values) * back_ref[...], axis=0, keepdims=True
            )

    return pl.pallas_call(
        body,
        grid=(pairs,),
        in_specs=[
            SMEM, whole(target_all), pair_cols(rows),
            pair_cols(rows), pair_cols(length), pair_cols(length),
            pair_cols(width), pair_cols(width, pairs), pair_cols(width, 2 * pairs),
            windows_spec(windows), whole(qseg), whole(kseg),
        ],
        out_specs=[
            pair_cols(length), pair_cols(length), pair_cols(length), windows_spec(windows),
            whole(target_all), pl.BlockSpec((1, width), lambda step: (0, 0)),
        ],
        out_shape=[
            shape_of(length, inner), shape_of(length, inner), shape_of(length, inner),
            shape_of(*windows.shape, dtype=F32), shape_of(length, width, dtype=F32),
            shape_of(1, width, dtype=F32),
        ],
        compiler_params=PARAMS,
        cost_estimate=cost(1),
        name="self_back",
    )(place, target_all, grad, query, key, value, weights, weights, weights, windows, qseg, kseg)


def cross_forward(target, attended, memory_all, gain_cross, gain_ffn, weights, qseg, mseg):
    (rows, width), inner, enc = target.shape, attended.shape[1], memory_all.shape[0]
    pairs = inner // LANES

    def body(
        rows_ref, att_ref, mem_ref, gain_ref, gain3_ref, wo_ref, wq_ref, wk_ref, wv_ref, wc_ref,
        qseg_ref, mseg_ref, one_ref, normed_ref, q_ref, k_ref, v_ref, out_ref, two_ref, last_ref,
    ):
        step = pl.program_id(0)

        @pl.when(step == 0)
        def _():
            hidden = rows_ref[...].astype(F32) + mm(att_ref[...], wo_ref[...])
            one_ref[...] = hidden
            two_ref[...] = hidden
            normed_ref[...] = (hidden * scale_of(hidden) * gain_ref[...]).astype(BF)

        query = mm(normed_ref[...], wq_ref[...]).astype(BF)
        key = mm(mem_ref[...], wk_ref[...]).astype(BF)
        value = mm(mem_ref[...], wv_ref[...]).astype(BF)
        q_ref[...], k_ref[...], v_ref[...] = query, key, value
        allowed = allowed_pairs(0, qseg_ref[...], mseg_ref[...], False)
        out = attend_pair(query, key, value, None, allowed, False)
        out_ref[...] = out
        two_ref[...] += mm(out, wc_ref[...])

        @pl.when(step == pairs - 1)
        def _():
            hidden = two_ref[...]
            last_ref[...] = (hidden * scale_of(hidden) * gain3_ref[...]).astype(BF)

    return pl.pallas_call(
        body,
        grid=(pairs,),
        in_specs=[
            whole(target), whole(attended), whole(memory_all), whole(gain_cross), whole(gain_ffn),
            pl.BlockSpec((width, width), lambda step: (0, 0)),
            pair_cols(width, pairs), pair_cols(width, 2 * pairs), pair_cols(width, 3 * pairs),
            pl.BlockSpec((LANES, width), lambda step: (step, 4)),
            whole(qseg), whole(mseg),
        ],
        out_specs=[
            whole(target), whole(target), pair_cols(rows), pair_cols(enc), pair_cols(enc),
            pair_cols(rows), whole(target), whole(target),
        ],
        out_shape=[
            shape_of(rows, width, dtype=F32), shape_of(rows, width), shape_of(rows, inner),
            shape_of(enc, inner), shape_of(enc, inner), shape_of(rows, inner),
            shape_of(rows, width, dtype=F32), shape_of(rows, width),
        ],
        compiler_params=PARAMS,
        cost_estimate=cost(8),
        name="cross_forward",
    )(
        target, attended, memory_all, gain_cross, gain_ffn, weights, weights, weights, weights,
        weights, qseg, mseg,
    )


def cross_back(grad_two, hidden_one, gain, query, key, value, weights, qseg, mseg):
    (rows, width), inner, enc = hidden_one.shape, query.shape[1], key.shape[0]
    pairs = inner // LANES

    def body(
        grad_ref, one_ref, gain_ref, q_ref, k_ref, v_ref, wo_ref, wq_ref, wk_ref, wv_ref, wc_ref,
        qseg_ref, mseg_ref, dq_ref, dk_ref, dv_ref, mem_ref, done_ref, low_ref, datt_ref,
        dgain_ref, two_ref, back_ref,
    ):
        step = pl.program_id(0)

        @pl.when(step == 0)
        def _():
            two_ref[...] = grad_ref[...].astype(BF)

        grad = mm(two_ref[...], wc_ref[...], NT).astype(BF)
        allowed = allowed_pairs(0, qseg_ref[...], mseg_ref[...], False)
        dq, dk, dv = attend_pair_back(
            q_ref[...], k_ref[...], v_ref[...], grad, None, None, allowed, False
        )
        dq_ref[...], dk_ref[...], dv_ref[...] = dq, dk, dv
        back = mm(dq, wq_ref[...], NT)
        memory = mm(dk, wk_ref[...], NT) + mm(dv, wv_ref[...], NT)

        @pl.when(step == 0)
        def _():
            back_ref[...] = back
            mem_ref[...] = memory

        @pl.when(step > 0)
        def _():
            back_ref[...] += back
            mem_ref[...] += memory

        @pl.when(step == pairs - 1)
        def _():
            through, grad_gain = norm_back(one_ref[...], gain_ref[...], back_ref[...])
            grad_one = grad_ref[...] + through
            low = grad_one.astype(BF)
            done_ref[...] = grad_one
            low_ref[...] = low
            dgain_ref[...] = grad_gain
            datt_ref[...] = mm(low, wo_ref[...], NT).astype(BF)

    row = pl.BlockSpec((1, width), lambda step: (0, 0))
    return pl.pallas_call(
        body,
        grid=(pairs,),
        in_specs=[
            whole(grad_two), whole(hidden_one), row,
            pair_cols(rows), pair_cols(enc), pair_cols(enc),
            pl.BlockSpec((width, width), lambda step: (0, 0)),
            pair_cols(width, pairs), pair_cols(width, 2 * pairs), pair_cols(width, 3 * pairs),
            pl.BlockSpec((LANES, width), lambda step: (step, 4)),
            whole(qseg), whole(mseg),
        ],
        out_specs=[
            pair_cols(rows), pair_cols(enc), pair_cols(enc),
            pl.BlockSpec((enc, width), lambda step: (0, 0)),
            whole(hidden_one), whole(hidden_one), whole(hidden_one), row,
        ],
        out_shape=[
            shape_of(rows, inner), shape_of(enc, inner), shape_of(enc, inner),
            shape_of(enc, width, dtype=F32), shape_of(rows, width, dtype=F32),
            shape_of(rows, width), shape_of(rows, inner), shape_of(1, width, dtype=F32),
        ],
        scratch_shapes=[pltpu.VMEM((rows, width), BF), pltpu.VMEM((rows, width), F32)],
        compiler_params=PARAMS,
        cost_estimate=cost(1),
        name="cross_back",
    )(
        grad_two, hidden_one, gain, query, key, value, weights, weights, weights, weights, weights,
        qseg, mseg,
    )


def gather_all(shard):
    return lax.all_gather(shard, AXES, axis=0, tiled=True)


def scatter_all(grads):
    return lax.psum_scatter(grads, AXES, scatter_dimension=0, tiled=True).astype(F32)


class Links:
    def __init__(self):
        self.batch, self.seq = lax.axis_size("batch"), lax.axis_size("seq")
        self.depth = self.batch // 2
        z_x, y_c = lax.axis_index("batch"), lax.axis_index("seq")
        self.z, self.x = z_x // 2, z_x % 2
        self.y, self.core = y_c // 2, y_c % 2
        self.lead = self.core == 0
        self.place = jnp.stack([self.z, self.x, self.y, self.core]).astype(jnp.int32)

    def move(self, value, target):
        pairs = []
        for source in range(self.batch * self.seq):
            z_x, y_c = source // self.seq, source % self.seq
            z, x, y, core = target(z_x // 2, z_x % 2, y_c // 2, y_c % 2)
            pairs.append((source, (z * 2 + x) * self.seq + y * 2 + core))
        return lax.ppermute(value, AXES, pairs)

    def over_core(self, value):
        return self.move(value, lambda z, x, y, core: (z, x, y, 1 - core))

    def over_y(self, value):
        return self.move(value, lambda z, x, y, core: (z, x, 1 - y, core))

    def over_near(self, value):
        return self.move(
            value, lambda z, x, y, c: (z, x, 1 - y, c) if c else (z, 1 - x, y, c)
        )

    def over_far(self, value):
        return self.move(
            value, lambda z, x, y, c: (z, 1 - x, y, c) if c else (z, x, 1 - y, c)
        )

    def over_z(self, value, step):
        depth = self.depth
        return self.move(value, lambda z, x, y, core: ((z - step) % depth, x, y, core))


def in_order(first, own, other):
    return jnp.concatenate([jnp.where(first, own, other), jnp.where(first, other, own)], axis=0)


def gather_core(links, left, right):
    own = jnp.where(links.lead, left, right)
    other = links.over_core(jnp.where(links.lead, right, left))
    return in_order(links.lead, own, other)


def z_steps(links, value, steps):
    return [links.over_z(value, step) for step in steps]


def gather_near(links, value):
    return jnp.stack([value, links.over_near(value)])


def gather_far(links, value):
    return jnp.stack([value, links.over_far(value)])


def assemble(links, *sources):
    count, (rows, cols) = len(sources) // 2, sources[0].shape[-2:]
    depth = links.depth

    def body(place_ref, *refs):
        inputs, out_ref, sem = refs[:-2], refs[-2], refs[-1]
        z, x, y, core = [place_ref[i] for i in range(4)]
        for which, source in enumerate(inputs):
            half = core if which < count else 1 - core
            for near, far, step in np.ndindex(2, 2, depth):
                if count == 2 and far != which % 2:
                    continue
                step_x, step_y = jnp.where(half == 0, near, far), jnp.where(half == 0, far, near)
                chip = (((z + step) % depth) * 2 + (x ^ step_x)) * 2 + (y ^ step_y)
                target = out_ref.at[
                    pl.ds(pl.multiple_of(chip * rows, 16), rows),
                    pl.ds(pl.multiple_of(half * cols, LANES), cols),
                ]
                part = source.at[near, step] if count == 2 else source.at[step, far, near]
                pltpu.make_async_copy(part, target, sem).start()
        pltpu.make_async_copy(out_ref, out_ref, sem).wait()

    return pl.pallas_call(
        body,
        in_specs=[pl.BlockSpec(memory_space=pltpu.SMEM)]
        + [pl.BlockSpec(memory_space=pl.ANY)] * len(sources),
        out_specs=pl.BlockSpec(memory_space=pltpu.VMEM),
        out_shape=jax.ShapeDtypeStruct((depth * 4 * rows, 2 * cols), sources[0].dtype),
        scratch_shapes=[pltpu.SemaphoreType.DMA(())],
        compiler_params=pltpu.CompilerParams(vmem_limit_bytes=48 << 20),
        cost_estimate=cost(1),
        name="assemble",
    )(links.place, *sources)


def weight_grad(links, terms, extra=None, z_first=False):
    depth, total_rows = links.depth, terms[0][0][0].shape[1]
    rows = total_rows // (depth * 4)
    widths = [term[0][1].shape[1] for term in terms]
    extra_width = 0 if extra is None else extra.shape[1]
    total = sum(widths) + extra_width
    tile = 1408 if total % 1408 == 0 else 512
    operands = [array for term in terms for pair in term for array in pair]
    operands += [] if extra is None else [extra]
    amount, pieces = len(operands), depth if z_first else 2
    piece_rows = total_rows // pieces

    def body(place_ref, *refs):
        sources, outs = refs[:amount], refs[amount : amount + pieces]
        stage, sems = refs[amount + pieces], refs[amount + pieces + 1]
        inputs, arrived = refs[amount + pieces + 2 : -1], refs[-1]
        fetches = [
            pltpu.make_async_copy(source, target, arrived.at[index])
            for index, (source, target) in enumerate(zip(sources, inputs))
        ]
        for fetch in fetches:
            fetch.start()
        z, x, y, left = place_ref[0], place_ref[1], place_ref[2], place_ref[3] == 0
        places = []
        for chip in range(depth * 4):
            step_x, step_y = (chip // 2 % 2) ^ x, (chip % 2) ^ y
            near, far = jnp.where(left, step_x, step_y), jnp.where(left, step_y, step_x)
            step = (chip // 4 - z) % depth
            spot = (step * 2 + far) * 2 + near if z_first else (near * 2 + far) * depth + step
            places.append(pl.multiple_of(spot * rows, 8))

        def copy(piece, index, start, width):
            cols = pl.ds(start, width)
            return pltpu.make_async_copy(
                stage.at[pl.ds(piece * piece_rows, piece_rows), cols],
                outs[piece].at[:, cols],
                sems.at[piece, index],
            )

        def emit(index, start, value, width):
            for chip, spot in enumerate(places):
                stage[pl.ds(spot, rows), pl.ds(start, width)] = value[
                    chip * rows : (chip + 1) * rows
                ].astype(BF)
            for piece in range(pieces):
                copy(piece, index, start, width).start()

        begin, first_copy, taken = 0, 0, 0
        for term, width in zip(terms, widths):
            pairs = inputs[taken : taken + 2 * len(term)]
            for fetch in fetches[taken : taken + 2 * len(term)]:
                fetch.wait()
            taken += 2 * len(term)

            def one_tile(index, carry, begin=begin, first_copy=first_copy, pairs=pairs):
                cols = pl.ds(pl.multiple_of(index * tile, LANES), tile)
                value = mm(pairs[0][...], pairs[1][:, cols], TN)
                if len(pairs) == 4:
                    value = value + mm(pairs[2][...], pairs[3][:, cols], TN)
                start = pl.multiple_of(begin + index * tile, LANES)
                emit(first_copy + index, start, value, tile)
                return carry

            lax.fori_loop(0, width // tile, one_tile, 0)
            begin, first_copy = begin + width, first_copy + width // tile
        if extra is not None:
            fetches[-1].wait()
            small = inputs[-1][...]
            emit(first_copy, begin, jnp.where(left, small, jnp.zeros_like(small)), extra_width)
        for piece in range(pieces):
            for index in range(first_copy):
                copy(piece, index, index * tile, tile).wait()
            if extra is not None:
                copy(piece, first_copy, begin, extra_width).wait()

    count = sum(width // tile for width in widths) + (extra is not None)
    hbm = pl.BlockSpec(memory_space=pltpu.HBM)
    return pl.pallas_call(
        body,
        in_specs=[pl.BlockSpec(memory_space=pltpu.SMEM)] + [hbm] * amount,
        out_specs=[pl.BlockSpec(memory_space=pl.ANY)] * pieces,
        out_shape=[jax.ShapeDtypeStruct((piece_rows, total), BF)] * pieces,
        scratch_shapes=[pltpu.VMEM((total_rows, total), BF), pltpu.SemaphoreType.DMA((pieces, count))]
        + [pltpu.VMEM(array.shape, array.dtype) for array in operands]
        + [pltpu.SemaphoreType.DMA((amount,))],
        compiler_params=pltpu.CompilerParams(vmem_limit_bytes=48 << 20),
        cost_estimate=cost(1),
        name="weight_grad",
    )(links.place, *operands)


def add_low(one, other):
    return (one.astype(F32) + other.astype(F32)).astype(BF)


class Scatter:
    def __init__(self, links, kept):
        self.links, self.parts, self.rows = links, [kept], kept.shape[0]

    def total(self, start, count):
        return sum(part[start : start + count].astype(F32) for part in self.parts)

    def halve(self):
        self.rows //= 2
        return self.total(self.rows, self.rows).astype(BF)

    def near(self, send):
        self.parts.append(self.links.over_near(send))

    def far(self, send):
        self.parts.append(self.links.over_far(send))

    def z_sends(self):
        self.rows //= self.links.depth
        return [
            self.total(step * self.rows, self.rows).astype(BF)
            for step in range(1, self.links.depth)
        ]

    def z(self, sends):
        depth = self.links.depth
        for step, send in enumerate(sends, 1):
            self.parts.append(self.links.over_z(send, depth - step))

    def z_back(self, sends):
        return self.links.over_z(sends[-1], 1)

    def z_ahead(self, sends):
        return self.links.over_z(sends[-2], self.links.depth - 1)

    def z_mid(self, sends, ahead):
        for send in sends[-3:0:-1]:
            ahead = self.links.over_z(add_low(ahead, send), self.links.depth - 1)
        return add_low(ahead, sends[0])

    def z_last(self, back, ahead):
        self.parts += [back, self.links.over_z(ahead, self.links.depth - 1)]

    def z_end(self, sends, back, ahead):
        self.z_last(back, self.z_mid(sends, ahead))

    def own(self):
        return self.total(0, self.rows)

    def last(self, total):
        links, half = self.links, self.rows // 2
        above, below = total[:half], total[half:]
        own = jnp.where(links.lead, above, below)
        other = links.over_core(jnp.where(links.lead, below, above))
        return jnp.where(links.lead, own, other), jnp.where(links.lead, other, own)


class SeqScatter:
    def __init__(self, links, parts):
        self.links = links
        parts = parts.reshape(2, 2, -1, parts.shape[1])
        take = lambda core: lax.dynamic_index_in_dim(parts, core, 1, False)
        self.kept = take(links.core)
        self.sent = links.over_core(take(1 - links.core).astype(BF))

    def second(self):
        total = self.kept + self.sent.astype(F32)
        take = lambda y: lax.dynamic_index_in_dim(total, y, 0, False)
        self.kept = take(self.links.y)
        self.sent = self.links.over_y(take(1 - self.links.y).astype(BF))

    def total(self):
        return self.kept + self.sent.astype(F32)


class PlainScatter:
    parts = ()

    def __init__(self, kept):
        self.kept = kept

    def halve(self):
        return ()

    def near(self, send):
        pass

    def z_mid(self, sends, ahead):
        return ()

    def z_last(self, back, ahead):
        pass

    def z_back(self, sends):
        return ()

    far, own, z_ahead = near, halve, z_back

    def last(self, total):
        return jnp.split(scatter_all(self.kept), 2, axis=1)


def phase(*values):
    return lax.optimization_barrier(values)


def per_device(
    target, memory, cotangent, target_segments, memory_segments, bucket_ids,
    self_norm_gain, self_query, self_key, self_value, self_output, bias_table,
    cross_norm_gain, cross_query, cross_key, cross_value, cross_output,
    ffn_norm_gain, ffn_gate, ffn_up, ffn_down,
):
    batch_size, seq_size = lax.axis_size("batch"), lax.axis_size("seq")
    devices = batch_size * seq_size
    seq_index = lax.axis_index("seq")
    rows, width = target.shape[1], target.shape[2]
    length, enc = target_segments.shape[1], memory_segments.shape[1]
    enc_rows = memory.shape[1]
    inner = self_query.shape[1]
    hidden = ffn_gate.shape[1]
    table_rows, table_cols = bias_table.shape
    weight_rows = self_query.shape[0]
    table_size = table_rows * table_cols

    links = Links()
    core, lead, depth = links.core, links.lead, links.depth
    small = jnp.concatenate(
        [self_norm_gain, cross_norm_gain, ffn_norm_gain, bias_table.reshape(-1)]
    )
    small = jnp.pad(small[None], ((0, weight_rows - 1), (0, 2 * LANES - small.shape[0])))
    part = hidden // 2
    groups = [
        [self_query, self_key, self_value, small],
        [self_output, cross_query, cross_key, cross_value, cross_output],
        [ffn_gate[:, :part], ffn_up[:, :part]],
        [ffn_gate[:, part:], ffn_up[:, part:]],
    ]
    groups = [jnp.concatenate(group, axis=1) for group in groups]
    cuts = [group.shape[1] // 2 for group in groups]
    left = jnp.concatenate([group[:, :cut] for group, cut in zip(groups, cuts)], axis=1)
    right = jnp.concatenate([group[:, cut:] for group, cut in zip(groups, cuts)], axis=1)
    down_cut = width // 2
    steps = list(range(1, depth))
    z_one, z_two, z_three = steps[:1], steps[-1:] if depth > 2 else [], steps[1:-1]
    direct = 2 * ffn_down.shape[0] % 16 == 0
    move = lambda function, *args: function(links, *args) if direct else None

    moved = gather_core(links, left, right)
    down = move(gather_core, ffn_down[:, :down_cut], ffn_down[:, down_cut:])
    if not direct:
        down_whole = gather_all(ffn_down)
    moved, down = phase(moved, down)
    ends = list(np.cumsum(cuts))
    first0, second0, gated0 = jnp.split(moved, ends[:2], axis=1)

    first_z = jnp.stack([first0] + z_steps(links, first0, steps))
    first_z, second0, down = phase(first_z, second0, down)

    first_near = gather_near(links, first_z)
    down = move(gather_near, down)
    second_one, second_two = z_steps(links, second0, z_one), z_steps(links, second0, z_two)
    rows_own = jnp.concatenate([target[0], memory[0]], axis=0)
    rows_other = links.over_y(rows_own)
    first_near, down, second_one, second_two, second0, rows_own, rows_other = phase(
        first_near, down, second_one, second_two, second0, rows_own, rows_other
    )

    first_far = links.over_far(first_near)
    first_near_other = links.over_core(first_near)
    second_three = []
    for step in z_three:
        second_three.append(links.over_z((second_one + second_three)[-1], 1))
    second_z = jnp.stack([second0] + second_one + second_three + second_two)
    rows_pair = in_order(links.y == 0, rows_own, rows_other)
    rows_other = links.over_core(rows_pair)
    first_far, first_near_other, second_z, down, gated0, rows_pair, rows_other, bucket_ids = phase(
        first_far, first_near_other, second_z, down, gated0, rows_pair, rows_other, bucket_ids
    )
    by_y = lambda both: both.reshape(2, 1, rows + enc_rows, width)
    both = jnp.concatenate(
        [
            jnp.where(lead, by_y(rows_pair), by_y(rows_other)),
            jnp.where(lead, by_y(rows_other), by_y(rows_pair)),
        ],
        axis=1,
    )
    target_all = both[:, :, :rows].reshape(length, width)
    memory_all = both[:, :, rows:].reshape(enc, width)

    position = seq_index * rows
    heads = seq_size * table_cols
    distance = position + rows - jnp.arange(rows + length, dtype=jnp.int32)
    near = (distance >= 0) & (distance < length)
    bucket = jnp.take(bucket_ids, jnp.clip(distance, 0, length - 1))
    bucket_range = jnp.arange(batch_size * table_rows, dtype=jnp.int32)
    onehot = ((bucket[:, None] == bucket_range[None, :]) & near[:, None]).astype(BF)

    second_near = gather_near(links, second_z)
    gated0, down, target_all, memory_all = phase(gated0, down, target_all, memory_all)
    gated_z = jnp.stack([gated0] + z_steps(links, gated0, steps))
    third_z, fourth_z = gated_z[..., : cuts[2]], gated_z[..., cuts[2] :]
    first_far_other = links.over_core(first_far)
    down = move(gather_far, down)
    (
        first_far_other, second_near, third_z, fourth_z, down, target_all, memory_all, onehot,
    ) = phase(
        first_far_other, second_near, third_z, fourth_z, down, target_all, memory_all, onehot,
    )

    second_far = links.over_far(second_near)
    second_near_other = links.over_core(second_near)
    third_near = gather_near(links, third_z)
    down_one, down_two = move(z_steps, down, z_one), move(z_steps, down, z_two)
    first = assemble(links, first_near, first_far, first_near_other, first_far_other)
    smalls = first[:, 3 * inner :].reshape(devices, weight_rows, 2 * LANES)[:, 0, :].astype(F32)
    gains = [smalls[:, i * weight_rows : (i + 1) * weight_rows].reshape(1, width) for i in range(3)]
    gain_self, gain_cross, gain_ffn = gains
    table = smalls[:, 3 * weight_rows : 3 * weight_rows + table_size]
    table = table.reshape(batch_size, seq_size, table_rows, table_cols)
    table = jnp.transpose(table, (0, 2, 1, 3)).reshape(batch_size * table_rows, seq_size * table_cols)

    windows = mm(table.astype(BF), onehot, (((0,), (1,)), ((), ())))
    windows = windows.reshape(heads // 2, 2, rows + length)
    position1 = position.reshape(1)
    qseg = lax.dynamic_slice_in_dim(target_segments, position, rows, 1).reshape(rows, 1)
    kseg, mseg = target_segments, memory_segments

    attended, queries, keys, values, normed_all = self_forward(
        position1, target_all, gain_self, first, windows, qseg, kseg
    )
    attended, second_far, second_near_other, third_near, fourth_z, down, down_one, down_two = phase(
        attended, second_far, second_near_other, third_near, fourth_z, down, down_one, down_two
    )

    third_far = links.over_far(third_near)
    third_near_other = links.over_core(third_near)
    fourth_near = links.over_near(fourth_z)
    down_three = []
    for step in z_three:
        down_three.append(links.over_z((down_one + down_three)[-1], 1) if direct else None)
    second = assemble(
        links, second_near, second_far, second_near_other, links.over_core(second_far)
    )
    (
        hidden_one, normed_two, cross_queries, cross_keys, cross_values, cross_attended,
        hidden_two, normed_three,
    ) = cross_forward(
        target[0], attended, memory_all, gain_cross, gain_ffn, second, qseg, mseg
    )
    choose = lambda left, right: (jnp.where(lead, left, right), jnp.where(lead, right, left))
    cot = cotangent[0]
    cot_own, cot_sent = choose(cot[:, :down_cut], cot[:, down_cut:])
    cot_other = links.over_core(cot_sent)
    (
        normed_three, third_far, third_near_other, fourth_z, fourth_near, down, down_one, down_two,
        down_three, cot_other,
    ) = phase(
        normed_three, third_far, third_near_other, fourth_z, fourth_near, down, down_one, down_two,
        down_three, cot_other,
    )

    fourth_near = jnp.stack([fourth_z, fourth_near])
    fourth_far = links.over_far(fourth_near)
    if direct:
        down = jnp.stack([down] + down_one + down_three + down_two)
    third_far_other, down, fourth_later = phase(links.over_core(third_far), down, fourth_near)
    down_other = links.over_core(down) if direct else None
    fourth_near_other = links.over_core(fourth_later)
    third = assemble(links, third_near, third_far, third_near_other, third_far_other)
    third_gate_up = mm(normed_three, third)
    if direct:
        w_down = assemble(links, down, down_other)
    else:
        w_down = down_whole
    third_gate_up, fourth_far, fourth_near_other, w_down, normed_three = phase(
        third_gate_up, fourth_far, fourth_near_other, w_down, normed_three
    )

    fourth_far_other = links.over_core(fourth_far)
    normed_other = links.over_core(normed_three)
    def gated(gate_up, start):
        inner_act, pull = jax.vjp(gated_unit, gate_up[:, :part], gate_up[:, part:])
        grad_gate, grad_up = pull(mm(cot, w_down[start : start + part], NT))
        return inner_act.astype(BF), grad_gate.astype(BF), grad_up.astype(BF)

    inner_a, gate_a, up_a = gated(third_gate_up, 0)
    third_own, third_sent = choose(gate_a, up_a)
    third_own, third_sent, inner_a, fourth_far_other, normed_other = phase(
        third_own, third_sent, inner_a, fourth_far_other, normed_other
    )

    third_other = links.over_core(third_sent)
    inner_a_other = links.over_core(inner_a)
    fourth = assemble(links, fourth_near, fourth_far, fourth_near_other, fourth_far_other)
    third_other, inner_a_other, fourth = phase(third_other, inner_a_other, fourth)
    third_keep, third_send = weight_grad(
        links, [[(normed_three, third_own), (normed_other, third_other)]]
    )

    third_keep, third_send, fourth = phase(third_keep, third_send, fourth)
    third_sum = Scatter(links, third_keep)
    third_sum.near(third_send)
    inner_b, gate_b, up_b = gated(mm(normed_three, fourth), part)
    fourth_own, fourth_sent = choose(gate_b, up_b)
    fourth_other = links.over_core(fourth_sent)
    inner_b_other = links.over_core(inner_b)
    inner_low = jnp.concatenate([inner_a, inner_b], axis=1)
    inner_other = jnp.concatenate([inner_a_other, inner_b_other], axis=1)
    if direct:
        down_keep, *down_sends = weight_grad(
            links, [[(inner_low, cot_own), (inner_other, cot_other)]], z_first=True
        )
        down_sum = Scatter(links, down_keep)
    else:
        down_sends, down_sum = (), PlainScatter(mm(inner_low, cot, TN).astype(BF))
    (
        third_sum.parts, fourth_own, fourth_other, gate_b, up_b, down_sends, down_sum.parts,
        inner_low,
    ) = phase(
        third_sum.parts, fourth_own, fourth_other, gate_b, up_b, down_sends, down_sum.parts,
        inner_low,
    )

    fourth_keep, fourth_send = weight_grad(
        links, [[(normed_three, fourth_own), (normed_other, fourth_other)]]
    )
    third_send, fourth_keep, fourth_send, gate_b, up_b, down_sends = phase(
        third_sum.halve(), fourth_keep, fourth_send, gate_b, up_b, down_sends
    )
    third_sum.far(third_send)
    fourth_sum = Scatter(links, fourth_keep)
    fourth_sum.near(fourth_send)
    down_back, down_ahead = down_sum.z_back(down_sends), down_sum.z_ahead(down_sends)
    grad_normed_three = mm(jnp.concatenate([gate_a, up_a], axis=1), third, NT) + mm(
        jnp.concatenate([gate_b, up_b], axis=1), fourth, NT
    )
    through, grad_gain_ffn = norm_back(hidden_two, gain_ffn, grad_normed_three)
    grad_hidden_two = cot.astype(F32) + through
    low_two = grad_hidden_two.astype(BF)
    (
        grad_cq, grad_ck, grad_cv, memory_part, grad_hidden_one, low_one, grad_attended,
        grad_gain_cross,
    ) = cross_back(
        grad_hidden_two, hidden_one, gain_cross, cross_queries, cross_keys, cross_values, second,
        qseg, mseg,
    )
    half = inner // 2
    (
        third_sum.parts, fourth_sum.parts, down_sends, down_back, down_ahead, grad_cq, grad_ck,
        grad_cv, low_two, low_one, grad_attended, memory_part,
    ) = phase(
        third_sum.parts, fourth_sum.parts, down_sends, down_back, down_ahead, grad_cq, grad_ck,
        grad_cv, low_two, low_one, grad_attended, memory_part,
    )

    cross_acts, cross_acts_sent = choose(normed_two, cross_attended)
    cross_grad, cross_grad_sent = choose(grad_cq, low_two)
    cross_kv, cross_kv_sent = choose(grad_ck, grad_cv)
    cross_sent = jnp.concatenate(
        [cross_acts_sent, cross_grad_sent, cross_kv_sent, attended, low_one], axis=0
    )
    fourth_send, cross_sent, third_sum.parts, memory_part = phase(
        fourth_sum.halve(), cross_sent, third_sum.parts, memory_part
    )
    fourth_sum.far(fourth_send)
    cross_other = links.over_core(cross_sent)
    third_sum.z(third_sum.z_sends())
    memory_rows = SeqScatter(links, memory_part)
    bounds = np.cumsum([rows, rows, enc, rows]).tolist()
    other_acts, other_grad, other_kv, other_attended, other_low = jnp.split(
        cross_other, bounds, axis=0
    )
    low_half = choose(low_one[:, :half], low_one[:, half:])[0]
    other_low = choose(other_low[:, :half], other_low[:, half:])[0]
    cross_keep, cross_send = weight_grad(
        links,
        [
            [(cross_acts, cross_grad), (other_acts, other_grad)],
            [(memory_all, add_low(cross_kv, other_kv))],
            [(attended, low_half), (other_attended, other_low)],
        ],
    )
    (
        cross_keep, cross_send, fourth_sum.parts, third_sum.parts, grad_attended, down_sends,
        down_back, down_ahead, memory_rows.sent, memory_rows.kept,
    ) = phase(
        cross_keep, cross_send, fourth_sum.parts, third_sum.parts, grad_attended, down_sends,
        down_back, down_ahead, memory_rows.sent, memory_rows.kept,
    )

    cross_sum = Scatter(links, cross_keep)
    cross_sum.near(cross_send)
    down_mid, memory_rows.sent, grad_attended = phase(
        down_sum.z_mid(down_sends, down_ahead), memory_rows.sent, grad_attended
    )
    down_sum.z_last(down_back, down_mid)
    memory_rows.second()
    grad_q, grad_k, grad_v, grad_windows, grad_normed, grad_gain_self = self_back(
        position1, target_all, grad_attended, queries, keys, values, first, windows, qseg, kseg
    )
    (
        cross_sum.parts, down_sum.parts, fourth_sum.parts, third_sum.parts, grad_q, grad_k, grad_v,
        grad_windows, grad_normed, grad_gain_self, memory_rows.sent, memory_rows.kept,
    ) = phase(
        cross_sum.parts, down_sum.parts, fourth_sum.parts, third_sum.parts, grad_q, grad_k, grad_v,
        grad_windows, grad_normed, grad_gain_self, memory_rows.sent, memory_rows.kept,
    )

    cut = inner + half
    self_own, self_sent = choose(
        jnp.concatenate([grad_q, grad_k[:, :half]], axis=1),
        jnp.concatenate([grad_v, grad_k[:, half:]], axis=1),
    )
    (
        cross_send, self_own, self_sent, grad_windows, grad_gain_self, fourth_sum.parts,
    ) = phase(
        cross_sum.halve(), self_own, self_sent, grad_windows, grad_gain_self, fourth_sum.parts,
    )
    cross_sum.far(cross_send)
    fourth_sends = fourth_sum.z_sends()
    fourth_back, fourth_ahead = fourth_sum.z_back(fourth_sends), fourth_sum.z_ahead(fourth_sends)
    self_other = links.over_core(self_sent)
    grad_windows = grad_windows.reshape(heads, rows + length)
    grad_table = lax.dot_general(
        onehot.astype(F32), grad_windows, (((0,), (1,)), ((), ())), precision=lax.Precision.HIGHEST
    )
    grad_table = grad_table.reshape(batch_size, table_rows, seq_size, table_cols)
    grad_table = jnp.transpose(grad_table, (0, 2, 1, 3)).reshape(devices, table_size)
    gain_parts = [g.reshape(devices, weight_rows) for g in (grad_gain_self, grad_gain_cross, grad_gain_ffn)]
    small_grad = jnp.concatenate(gain_parts + [grad_table], axis=1)
    small_grad = jnp.pad(
        small_grad[:, None], ((0, 0), (0, weight_rows - 1), (0, LANES - small_grad.shape[1]))
    ).reshape(devices * weight_rows, LANES)
    small_grad = small_grad.astype(BF)
    small_other = links.over_core(small_grad)
    (
        self_own, self_other, small_grad, small_other, cross_sum.parts, down_sum.parts,
        fourth_sends, fourth_back, fourth_ahead, third_sum.parts, grad_normed, memory_rows.sent,
        memory_rows.kept, inner_low,
    ) = phase(
        self_own, self_other, small_grad, small_other, cross_sum.parts, down_sum.parts,
        fourth_sends, fourth_back, fourth_ahead, third_sum.parts, grad_normed, memory_rows.sent,
        memory_rows.kept, inner_low,
    )
    self_keep, self_send = weight_grad(
        links,
        [[(normed_all, add_low(self_own, self_other))]],
        add_low(small_grad, small_other),
    )

    (
        self_keep, self_send, cross_sum.parts, inner_low, third_sum.parts, fourth_sends,
        fourth_back, fourth_ahead, down_sum.parts, memory_rows.sent, grad_normed,
    ) = phase(
        self_keep, self_send, cross_sum.parts, inner_low, third_sum.parts, fourth_sends,
        fourth_back, fourth_ahead, down_sum.parts, memory_rows.sent, grad_normed,
    )
    self_sum = Scatter(links, self_keep)
    self_sum.near(self_send)
    cross_sends = cross_sum.z_sends()
    fourth_sum.z_end(fourth_sends, fourth_back, fourth_ahead)
    normed_rows = SeqScatter(links, grad_normed)
    memory_grad = memory_rows.total()
    cross_back_z, cross_ahead_z = cross_sum.z_back(cross_sends), cross_sum.z_ahead(cross_sends)
    activations = (hidden_two + mm(inner_low, w_down)).astype(BF)
    third_total = third_sum.own()
    (
        self_sum.parts, cross_back_z, cross_ahead_z, down_sum.parts, activations, third_total,
        fourth_sum.parts, memory_grad, normed_rows.sent, normed_rows.kept,
    ) = phase(
        self_sum.parts, cross_back_z, cross_ahead_z, down_sum.parts, activations, third_total,
        fourth_sum.parts, memory_grad, normed_rows.sent, normed_rows.kept,
    )

    (
        self_send, down_sum.parts, cross_sends, cross_back_z, cross_ahead_z, normed_rows.sent,
        third_total, fourth_sum.parts,
    ) = phase(
        self_sum.halve(), down_sum.parts, cross_sends, cross_back_z, cross_ahead_z,
        normed_rows.sent, third_total, fourth_sum.parts,
    )
    self_sum.far(self_send)
    cross_sum.z_end(cross_sends, cross_back_z, cross_ahead_z)
    down_sum.far(down_sum.halve())
    normed_rows.second()
    fourth_total = fourth_sum.own()
    (
        self_sum.parts, cross_sum.parts, down_sum.parts, normed_rows.sent, fourth_total,
    ) = phase(
        self_sum.parts, cross_sum.parts, down_sum.parts, normed_rows.sent, fourth_total,
    )

    self_sends, cross_sum.parts, down_sum.parts, fourth_total, normed_rows.sent = phase(
        self_sum.z_sends(), cross_sum.parts, down_sum.parts, fourth_total, normed_rows.sent
    )
    self_sum.z(self_sends)
    down_sum.near(down_sum.halve())
    gate_one, up_one = third_sum.last(third_total)
    gate_two, up_two = fourth_sum.last(fourth_total)
    cross_left, cross_right = cross_sum.last(cross_sum.own())
    through, _ = norm_back(target[0].astype(F32), gain_self, normed_rows.total())
    target_grad = grad_hidden_one + through
    down_out = jnp.concatenate(down_sum.last(down_sum.own()), axis=1)
    self_left, self_right = self_sum.last(self_sum.own())
    join = lambda left, right: jnp.concatenate([left, right], axis=1)

    small_out = self_left[0, cut:]
    gain_out = [small_out[i * weight_rows : (i + 1) * weight_rows] for i in range(3)]
    table_out = small_out[3 * weight_rows : 3 * weight_rows + table_size]
    return (
        activations[None],
        target_grad[None],
        memory_grad[None],
        gain_out[0],
        self_left[:, :inner],
        join(self_left[:, inner:cut], self_right[:, inner:cut]),
        self_right[:, :inner],
        join(cross_left[:, 2 * inner :], cross_right[:, 2 * inner :]),
        table_out.reshape(table_rows, table_cols),
        gain_out[1],
        cross_left[:, :inner],
        cross_left[:, inner : 2 * inner],
        cross_right[:, inner : 2 * inner],
        cross_right[:, :inner],
        gain_out[2],
        jnp.concatenate([gate_one, gate_two], axis=1),
        jnp.concatenate([up_one, up_two], axis=1),
        down_out,
    )


def solution(mesh):
    rows3 = P("batch", "seq", None)
    seg = P("batch", None)
    gain = P(AXES)
    weight = P(AXES, None)
    table = P("batch", "seq")
    return jax.shard_map(
        per_device,
        mesh=mesh,
        in_specs=(
            rows3, rows3, rows3, seg, seg, P(),
            gain, weight, weight, weight, weight, table,
            gain, weight, weight, weight, weight,
            gain, weight, weight, weight,
        ),
        out_specs=(
            rows3, rows3, rows3,
            gain, weight, weight, weight, weight, table,
            gain, weight, weight, weight, weight,
            gain, weight, weight, weight,
        ),
        check_vma=False,
    )
```
